32 devices in a mesh: groups: 2 (over y), gy: 16 (over z, x, core).
Axes of the slice: x: 2, y: 2, z: 4, core: 2. Of those that a mesh axis runs over, the one named last changes fastest.
Arguments:
- levels: bfloat16 [32, 75, 512], P(('groups', 'gy')), parts along dimension 0, may hold values from -6 to 6
- ocean: int32 [32, 512], P(('groups', 'gy')), parts along dimension 0, may hold values 0 or 1
- stem: bfloat16 [75, 128], replicated, may hold values from -0.75 to 0.75
- dw_kernel: float32 [2, 49, 128], replicated, may hold values from -0.875 to 0.875
- ln_gain: float32 [2, 128], replicated, may hold values from 0.25 to 1.75
- w_in: bfloat16 [2, 128, 512], replicated, may hold values from -0.5 to 0.5
- w_out: bfloat16 [2, 512, 128], replicated, may hold values from -0.25 to 0.25
- layer_scale: float32 [2, 128], replicated, may hold values from 0.3 to 1
- upstream: bfloat16 [32, 512, 128], P(('groups', 'gy')), parts along dimension 0, may hold values from -6 to 6
Outputs:
- result: bfloat16 [32, 512, 128], P(('groups', 'gy')), parts along dimension 0
- stem_gradient: float32 [150, 128], P('groups'), parts along dimension 0
- grad_kernel: float32 [4, 49, 128], P('groups'), parts along dimension 0
- grad_gain: float32 [4, 128], P('groups'), parts along dimension 0
- grad_w_in: float32 [4, 128, 512], P('groups'), parts along dimension 0
- grad_w_out: float32 [4, 512, 128], P('groups'), parts along dimension 0
- grad_scale: float32 [4, 128], P('groups'), parts along dimension 0
The draws below stay inside these ranges and needn't reach their ends.
There are 2 independent parts, one for each index of `groups`. The reference program is written for one: setup_inputs(seed, part) draws one part's arguments, and reference() takes and returns one part's arrays. A program takes and returns all parts, laid end to end along the dimension named above; an argument that names none is the same for every part. Nothing has to cross between parts.
Inputs may be any that keep to these rules, and one draw needn't show every extreme that they name: 1 marks an ocean cell, 0 a land cell.
All inputs are finite; a program needn't handle non-finite values. No bound on the sum of `ocean` on one device may be relied on, other than what follows from the above.
Results may differ from the reference program's by a relative error of at most 0.0088.
Values may be sent and summed in bfloat16 or wider, within the bound.
No kernel may reach another device: no remote copies, remote signals or barrier semaphores. Data moves between devices by JAX's collectives and lax.ppermute only.
A program may use at most 64 MiB of HBM per device.

```python
import math
from functools import partial
import jax
import jax.numpy as jnp
from jax import lax

C = 128
HID = 512
LEV = 75
LAYERS = 2
TH = 16
TW = 32
TX = 8
TILES = 16
CELLS = 512


def with_ends(drawn, key, smallest, top_value):
    shape = drawn.shape
    spot = [jax.random.randint(jax.random.fold_in(key, axis), (), 0, shape[axis]) for axis in range(len(shape))]
    drawn = drawn.at[tuple(spot)].set(smallest)
    longest = shape.index(max(shape))
    spot[longest] = (spot[longest] + 1) % shape[longest]
    return drawn.at[tuple(spot)].set(top_value)


def block_levels(rng, shape, shards, least, high):
    level = 1.0
    for position, parts in shards:
        steps = jax.random.uniform(jax.random.fold_in(jax.random.fold_in(rng, 6), position), (parts,), jnp.float32, least / len(shards), high / len(shards))
        level = level * jnp.repeat(jnp.exp(steps), shape[position] // parts).reshape((-1,) + (1,) * (len(shape) - 1 - position))
    return level


def normal_values(key, dims, width, bound, pieces=(), held_as=jnp.bfloat16):
    factor_of = block_levels(key, dims, pieces, -0.22, 0.18) if pieces else 1.0
    values = jax.random.normal(key, dims, jnp.float32) * width * factor_of
    return jnp.minimum(jnp.maximum(values, -bound), bound).astype(held_as)


def setup_inputs(seed: int = 0, part: int = 0) -> dict:
    key_of = jax.random.split(jax.random.key(seed), 10)
    own_keys = jax.random.split(jax.random.fold_in(key_of[9], part), 10)
    return {
        "levels": normal_values(own_keys[0], (TILES, LEV, CELLS), 1.0, 6.0, ((0, 16),)),
        "ocean": with_ends((jax.random.randint(own_keys[1], (TILES, CELLS), 0, 5) < 4).astype(jnp.int32), jax.random.fold_in(own_keys[1], 1), 0, 1),
        "stem": normal_values(key_of[2], (LEV, C), LEV ** -0.5, 0.75),
        "dw_kernel": normal_values(key_of[3], (LAYERS, 49, C), 49 ** -0.5, 0.875, (), jnp.float32),
        "ln_gain": jnp.clip(1.0 + 0.15 * jax.random.normal(key_of[4], (LAYERS, C), jnp.float32), 0.25, 1.75),
        "w_in": normal_values(key_of[5], (LAYERS, C, HID), C ** -0.5, 0.5),
        "w_out": normal_values(key_of[6], (LAYERS, HID, C), HID ** -0.5, 0.25),
        "layer_scale": jnp.clip(jnp.exp(jax.random.uniform(key_of[7], (LAYERS, C), jnp.float32, math.log(0.3), math.log(1.0))), 0.3, 1.0),
        "upstream": normal_values(own_keys[8], (TILES, CELLS, C), 1.0, 6.0, ((0, 16),)),
    }


SQRT_TWO_PI = 0.7978845608028654
CUBIC_COEF = 0.044715
NORM_STABILIZER = 1e-06

def gelu_tanh(values):
    inner_arg = SQRT_TWO_PI * (values + CUBIC_COEF * values * values * values)
    return 0.5 * values * (1.0 + jnp.tanh(inner_arg))

def gelu_slope(values):
    tangent = jnp.tanh(SQRT_TWO_PI * (values + CUBIC_COEF * values * values * values))
    return 0.5 * (1.0 + tangent) + 0.5 * values * (1.0 - tangent * tangent) * SQRT_TWO_PI * (1.0 + 3.0 * CUBIC_COEF * values * values)

def normalize(conv_out, gain_row):
    average = lax.optimization_barrier(jnp.mean(conv_out, axis=-1, keepdims=True))
    centered = conv_out - average
    inverse_result = lax.rsqrt(lax.optimization_barrier(jnp.mean(centered * centered, axis=-1, keepdims=True)) + NORM_STABILIZER)
    scaled = centered * inverse_result
    return (scaled, inverse_result, (scaled * gain_row).astype(jnp.bfloat16))

def to_grid(tiles):
    channels = tiles.shape[-1]
    tile_rows = tiles.shape[0] // TX
    blocks = tiles.reshape(tile_rows, TX, TH, TW, channels)
    return blocks.transpose(0, 2, 1, 3, 4).reshape(tile_rows * TH, TX * TW, channels)

def to_tiles(grid):
    channels = grid.shape[-1]
    tile_rows = grid.shape[0] // TH
    blocks = grid.reshape(tile_rows, TH, TX, TW, channels)
    return blocks.transpose(0, 2, 1, 3, 4).reshape(tile_rows * TX, TH * TW, channels)

def extend(grid):
    widened = jnp.concatenate([grid[:, -3:], grid, grid[:, :3]], axis=1)
    south_rows = jnp.zeros((3,) + widened.shape[1:], widened.dtype)
    north_rows = widened[-3:][::-1, ::-1]
    return jnp.concatenate([south_rows, widened, north_rows], axis=0)

def depthwise(tiles, kernel):
    extended = extend(to_grid(tiles))
    grid_rows = extended.shape[0] - 6
    grid_cols = extended.shape[1] - 6
    total = jnp.zeros((grid_rows, grid_cols, extended.shape[2]), extended.dtype)
    for row_tap in range(7):
        for col_tap in range(7):
            total = total + kernel[row_tap * 7 + col_tap] * extended[row_tap:row_tap + grid_rows, col_tap:col_tap + grid_cols]
    return to_tiles(total)

def embed_tile(stem, tile_levels):
    return lax.dot_general(tile_levels, stem, (((0,), (0,)), ((), ())), preferred_element_type=jnp.float32)

def forward_tile(gain_row, weight_in, weight_out, conv_tile):
    scaled, inverse_result, normed = normalize(conv_tile, gain_row)
    hidden_pre = jnp.dot(normed, weight_in, preferred_element_type=jnp.float32)
    activated = gelu_tanh(hidden_pre).astype(jnp.bfloat16)
    return jnp.dot(activated, weight_out, preferred_element_type=jnp.float32)

def backward_tile(gain_row, weight_in, weight_out, scale_row, packed):
    conv_tile, carried_tile, mask_tile = packed
    scaled, inverse_result, normed = normalize(conv_tile, gain_row)
    hidden_pre = jnp.dot(normed, weight_in, preferred_element_type=jnp.float32)
    activated = gelu_tanh(hidden_pre).astype(jnp.bfloat16)
    branch = jnp.dot(activated, weight_out, preferred_element_type=jnp.float32)
    masked = mask_tile * carried_tile
    grad_scale = lax.optimization_barrier(jnp.sum(masked * branch, axis=0))
    grad_branch = (masked * scale_row).astype(jnp.bfloat16)
    grad_wout = jnp.dot(activated.T, grad_branch, preferred_element_type=jnp.float32)
    grad_pre = (jnp.dot(grad_branch, weight_out.T, preferred_element_type=jnp.float32) * gelu_slope(hidden_pre)).astype(jnp.bfloat16)
    grad_win = jnp.dot(normed.T, grad_pre, preferred_element_type=jnp.float32)
    grad_normed = jnp.dot(grad_pre, weight_in.T, preferred_element_type=jnp.float32)
    grad_gain = lax.optimization_barrier(jnp.sum(grad_normed * scaled, axis=0))
    grad_scaled = grad_normed * gain_row
    grad_conv = inverse_result * (grad_scaled - lax.optimization_barrier(jnp.mean(grad_scaled, axis=-1, keepdims=True)) - scaled * lax.optimization_barrier(jnp.mean(grad_scaled * scaled, axis=-1, keepdims=True)))
    rounded = lax.optimization_barrier(grad_conv.astype(jnp.bfloat16)).astype(jnp.float32)
    return (rounded, masked, grad_scale, grad_wout, grad_win, grad_gain)

def reference(levels, ocean, stem, dw_kernel, ln_gain, w_in, w_out, layer_scale, upstream):
    land_mask = ocean.astype(jnp.float32)[:, :, None]
    embedded = lax.map(partial(embed_tile, stem), levels)
    stream_field = (land_mask * embedded).astype(jnp.bfloat16)
    inputs = []
    convs = []
    for layer_index in range(LAYERS):
        conv_out = depthwise(stream_field.astype(jnp.float32), dw_kernel[layer_index])
        branch = lax.map(partial(forward_tile, ln_gain[layer_index], w_in[layer_index], w_out[layer_index]), conv_out)
        inputs.append(stream_field)
        convs.append(conv_out)
        stream_field = (land_mask * (stream_field.astype(jnp.float32) + layer_scale[layer_index] * branch)).astype(jnp.bfloat16)
    result = stream_field
    carried = upstream.astype(jnp.float32) * (1.0 / math.sqrt(TILES * CELLS))
    kernel_list = [None] * LAYERS
    gain_list = [None] * LAYERS
    win_list = [None] * LAYERS
    wout_list = [None] * LAYERS
    layer_scales = [None] * LAYERS
    for layer_index in reversed(range(LAYERS)):
        train_step_function = partial(backward_tile, ln_gain[layer_index], w_in[layer_index], w_out[layer_index], layer_scale[layer_index])
        rounded, masked, grad_scale, grad_wout, grad_win, grad_gain = lax.map(train_step_function, (convs[layer_index], carried, land_mask))
        conv_again, pullback = jax.vjp(depthwise, inputs[layer_index].astype(jnp.float32), dw_kernel[layer_index])
        grad_input, grad_kernel = pullback(rounded)
        carried = masked + grad_input
        kernel_list[layer_index] = grad_kernel
        gain_list[layer_index] = lax.optimization_barrier(jnp.sum(grad_gain, axis=0))
        win_list[layer_index] = lax.optimization_barrier(jnp.sum(grad_win, axis=0))
        wout_list[layer_index] = lax.optimization_barrier(jnp.sum(grad_wout, axis=0))
        layer_scales[layer_index] = lax.optimization_barrier(jnp.sum(grad_scale, axis=0))
    stem_contribution = (land_mask * carried).astype(jnp.bfloat16)
    stem_gradient = jnp.einsum('hei,hiu->eu', levels.astype(jnp.float32), stem_contribution.astype(jnp.float32))
    return (result, stem_gradient, jnp.stack(kernel_list), jnp.stack(gain_list), jnp.stack(win_list), jnp.stack(wout_list), jnp.stack(layer_scales))
```

```python
import functools
import math

import jax
import jax.numpy as jnp
from jax import lax
from jax.experimental import pallas as pl
from jax.experimental.pallas import tpu as pltpu
from jax.sharding import PartitionSpec as P

TH = 16
TW = 32
TX = 8
LANES = 128

RIM = 6
PADC = 8
EH, EW = TH + 2 * RIM, TW + 2 * PADC
RH, RW = TH + 6, 40
RING_COL = 5

C0 = 0.7978845608028654
C1 = 0.7978845608028654 * 0.044715
NORM_STABILIZER = 1e-06

WIN_ROW, WOUT_ROW, SMALL_ROW = 0, 1024, 2048
STEM_AT, KERNEL_AT, GAIN_AT, SCALE_AT = 0, (80, 136), 192, 194
SMALL_ROWS = 256
PACKED = SMALL_ROW + SMALL_ROWS

BF = jnp.bfloat16
F32 = jnp.float32


def vmem(count):
    return [pl.BlockSpec(memory_space=pltpu.VMEM)] * count


def smem():
    return pl.BlockSpec(memory_space=pltpu.SMEM)


def contract_rows(left, right):
    return lax.dot_general(left, right, (((0,), (0,)), ((), ())), preferred_element_type=F32)


def contract_cols(left, right):
    return lax.dot_general(left, right, (((1,), (1,)), ((), ())), preferred_element_type=F32)


def prepare_kernel(levels_ref, ocean_ref, tile_ref, west_ref, east_ref, stage):
    count = levels_ref.shape[0]
    stage[...] = jnp.zeros_like(stage)
    stage[0:count, :] = levels_ref[...].astype(F32)
    stage[count : count + 1, :] = ocean_ref[...].astype(F32)
    rows = lax.broadcasted_iota(jnp.int32, (LANES, LANES), 0)
    cols = lax.broadcasted_iota(jnp.int32, (LANES, LANES), 1)
    eye = (rows == cols).astype(BF)
    turned = contract_rows(stage[...].astype(BF), eye).reshape(TH, TW, LANES)
    tile_ref[...] = turned.astype(BF)
    west_ref[...] = turned[:, :PADC].astype(BF)
    east_ref[...] = turned[:, TW - PADC :].astype(BF)


def load_column(ref, row, start):
    return ref[row, pl.ds(start, 8), :]


def conv_block(ref, taps, start, out_rows, in_rows, taps_of):
    totals = {o: None for o in out_rows}
    needed = sorted({o + a for o in out_rows for a in range(7) if o + a in in_rows})
    for d in range(7):
        column = {r: load_column(ref, r - in_rows.start, start + d) for r in needed}
        for a in range(7):
            held = {}
            for o in out_rows:
                r = o + a
                if r not in column:
                    continue
                which, index = taps_of(o, r, a, d)
                if (which, index) not in held:
                    held[(which, index)] = taps[which][index]
                term = held[(which, index)] * column[r]
                totals[o] = term if totals[o] is None else totals[o] + term
    return totals


def main_kernel(
    two_rows,
    rescale,
    top_ref,
    tile_ref,
    west_ref,
    east_ref,
    south_ref,
    north_ref,
    fold_ref,
    stem_ref,
    dw_ref,
    gain_ref,
    win_ref,
    wout_ref,
    scale_ref,
    up_ref,
    out_ref,
    packed_ref,
    ext,
    x0,
    m6,
    x1,
    weights,
    taps0,
    taps0n,
    taps1,
    conv0,
    xhat0,
    rinv0,
    branch0,
    normed0,
    act0,
    slope0,
    conv1,
    xhat1,
    rinv1,
    branch1,
    normed1,
    act1,
    slope1,
    wide,
    thin,
    gpre,
    pad0,
    pad1,
    g1,
    h0,
    gk0,
    gk0n,
    gk1,
    small,
):
    top = top_ref[0] == 1
    levels_count = stem_ref.shape[0]

    def mirrored(step):
        rows = lax.broadcasted_iota(jnp.int32, (EW, EW), 0)
        cols = lax.broadcasted_iota(jnp.int32, (EW, EW), 1)
        swap = (rows + cols == EW - 1).astype(BF)
        return jnp.dot(swap, fold_ref[RIM - 1 - step], preferred_element_type=F32)

    for step in range(RIM):
        south = south_ref[step].astype(F32)
        if two_rows:
            south = jnp.where(top, south, 0.0)
        ext[step] = south
        ext[RIM + TH + step] = jnp.where(top, mirrored(step), north_ref[step].astype(F32))
    ext[RIM : RIM + TH, 0:PADC] = west_ref[...].astype(F32)
    ext[RIM : RIM + TH, PADC : PADC + TW] = tile_ref[...].astype(F32)
    ext[RIM : RIM + TH, PADC + TW :] = east_ref[...].astype(F32)

    weights[...] = jnp.zeros_like(weights)
    weights[0:levels_count, 0:LANES] = stem_ref[...].astype(F32)
    weights[levels_count : levels_count + 1, LANES:] = jnp.ones((1, LANES), F32)
    joint = weights[...].astype(BF)

    def embed(row, _):
        both = jnp.dot(ext[row].astype(BF), joint, preferred_element_type=F32)
        mask = both[:, LANES:]
        m6[row] = mask
        x0[row] = (mask * both[:, :LANES]).astype(BF).astype(F32)
        return 0

    lax.fori_loop(0, EH, embed, 0)

    for t in range(49):
        first = dw_ref[0, t : t + 1, :]
        turned = dw_ref[0, 48 - t : 49 - t, :]
        taps0[t] = jnp.broadcast_to(first, (8, LANES))
        taps0n[t] = jnp.broadcast_to(jnp.where(top, turned, first), (8, LANES))
        taps1[t] = jnp.broadcast_to(dw_ref[1, t : t + 1, :], (8, LANES))

    north_at = 3 + TH

    def conv0_block(block, _):
        start = pl.multiple_of(block * 8, 8)
        for rows in (range(0, 10), range(10, 19), range(19, 22)):
            totals = conv_block(
                x0,
                (taps0, taps0n),
                start + 2,
                rows,
                range(0, EH),
                lambda o, r, a, d: (1 if o >= north_at else 0, a * 7 + d),
            )
            for o in rows:
                conv0[o, pl.ds(start, 8), :] = totals[o]
        return 0

    lax.fori_loop(0, RW // 8, conv0_block, 0)

    def norm_rows(conv, xhat, rinv, normed, gain):
        def step(row, _):
            values = conv[row]
            width = values.shape[0]
            average = jnp.mean(values, axis=-1, keepdims=True)
            centered = values - average
            inverse = lax.rsqrt(jnp.mean(centered * centered, axis=-1, keepdims=True) + NORM_STABILIZER)
            scaled = centered * inverse
            xhat[row] = scaled
            rinv[row] = jnp.broadcast_to(inverse, (width, LANES))
            normed[row] = (scaled * gain).astype(BF)
            return 0

        lax.fori_loop(0, conv.shape[0], step, 0)

    def gelu_rows(pre, act, slope, count):
        def step(index, _):
            at = pl.ds(pl.multiple_of(index * 16, 16), 16)
            v = pre[at, :]
            square = v * v
            inner = v * (C0 + C1 * square)
            half = 0.5 * jnp.tanh(inner) + 0.5
            active = v * half
            act[at, :] = active.astype(BF)
            slope[at, :] = half + active * (1.0 - half) * (2.0 * C0 + (6.0 * C1) * square)
            return 0

        lax.fori_loop(0, count // 16, step, 0)

    count0, count1 = RH * RW, TH * TW
    norm_rows(conv0, xhat0, rinv0, normed0, gain_ref[0:1, :])
    wide[0:count0] = jnp.dot(
        normed0[...].astype(F32).reshape(count0, LANES).astype(BF), win_ref[0], preferred_element_type=F32
    )
    gelu_rows(wide, act0, slope0, count0)
    branch0[...] = jnp.dot(act0[...], wout_ref[0], preferred_element_type=F32).reshape(RH, RW, LANES)

    def next0(row, _):
        mask = m6[row + 3, pl.ds(RING_COL, RW), :]
        held = x0[row + 3, pl.ds(RING_COL, RW), :]
        x1[row] = (mask * (held + scale_ref[0:1, :] * branch0[row])).astype(BF).astype(F32)
        return 0

    lax.fori_loop(0, RH, next0, 0)

    def conv1_block(block, _):
        start = pl.multiple_of(block * 8, 8)
        for rows in (range(0, 8), range(8, 16)):
            totals = conv_block(
                x1, (taps1,), start, rows, range(0, RH), lambda o, r, a, d: (0, a * 7 + d)
            )
            for o in rows:
                conv1[o, pl.ds(start, 8), :] = totals[o]
        return 0

    lax.fori_loop(0, TW // 8, conv1_block, 0)
    norm_rows(conv1, xhat1, rinv1, normed1, gain_ref[1:2, :])
    wide[0:count1] = jnp.dot(
        normed1[...].reshape(count1, LANES), win_ref[1], preferred_element_type=F32
    )
    gelu_rows(wide, act1, slope1, count1)
    branch1[...] = jnp.dot(act1[...], wout_ref[1], preferred_element_type=F32).reshape(TH, TW, LANES)

    small[...] = jnp.zeros_like(small)
    g1[...] = jnp.zeros_like(g1)

    def next1(row, total):
        mask = m6[row + RIM, pl.ds(PADC, TW), :]
        held = x1[row + 3, pl.ds(3, TW), :]
        branch = branch1[row]
        out_ref[row] = (mask * (held + scale_ref[1:2, :] * branch)).astype(BF)
        masked = mask * (up_ref[row].astype(F32) * rescale)
        g1[row + 3, pl.ds(3, TW), :] = masked
        thin[pl.ds(pl.multiple_of(row * TW, TW), TW), :] = (masked * scale_ref[1:2, :]).astype(BF)
        return total + jnp.sum((masked * branch).reshape(TW // 8, 8, LANES), axis=0)

    total = lax.fori_loop(0, TH, next1, jnp.zeros((8, LANES), F32))
    small[SCALE_AT + 1 : SCALE_AT + 2, :] = jnp.sum(total, axis=0, keepdims=True)

    def mlp_backward(layer, count, shape, normed, act, slope, xhat, rinv, store):
        gb = thin[0:count]
        packed_ref[WOUT_ROW + 512 * layer : WOUT_ROW + 512 * layer + 512, :] = contract_rows(
            act[...], gb
        ).astype(BF)
        wide[0:count] = contract_cols(gb, wout_ref[layer])

        def step(index, _):
            at = pl.ds(pl.multiple_of(index * 16, 16), 16)
            gpre[at, :] = (wide[at, :] * slope[at, :]).astype(BF)
            return 0

        lax.fori_loop(0, count // 16, step, 0)
        gp = gpre[0:count]
        grad_in = contract_rows(normed, gp).astype(BF)
        for part in range(4):
            at = WIN_ROW + 512 * layer + 128 * part
            packed_ref[at : at + 128, :] = grad_in[:, 128 * part : 128 * part + 128]
        wide[0:count, 0:LANES] = contract_cols(gp, win_ref[layer])
        rows, width = shape
        gain = gain_ref[layer : layer + 1, :]

        def finish(row, total):
            gn = wide[pl.ds(pl.multiple_of(row * width, 8), width), 0:LANES]
            scaled = xhat[row]
            gx = gn * gain
            both = gx - jnp.mean(gx, axis=-1, keepdims=True)
            both = both - scaled * jnp.mean(gx * scaled, axis=-1, keepdims=True)
            store(row, (rinv[row] * both).astype(BF).astype(F32))
            return total + jnp.sum((gn * scaled).reshape(width // 8, 8, LANES), axis=0)

        total = lax.fori_loop(0, rows, finish, jnp.zeros((8, LANES), F32))
        small[GAIN_AT + layer : GAIN_AT + layer + 1, :] = jnp.sum(total, axis=0, keepdims=True)

    pad1[...] = jnp.zeros_like(pad1)

    def store1(row, value):
        pad1[row, pl.ds(PADC, TW), :] = value

    mlp_backward(
        1, count1, (TH, TW), normed1[...].reshape(count1, LANES), act1, slope1, xhat1, rinv1, store1
    )

    gk1[...] = jnp.zeros_like(gk1)

    def kernel1_block(block, _):
        start = pl.multiple_of(block * 8, 8)
        grads = [pad1[j, pl.ds(start + PADC, 8), :] for j in range(TH)]
        for d in range(7):
            column = [load_column(x1, r, start + d) for r in range(RH)]
            for a in range(7):
                total = gk1[a * 7 + d]
                for j in range(TH):
                    total = total + grads[j] * column[j + a]
                gk1[a * 7 + d] = total
        return 0

    lax.fori_loop(0, TW // 8, kernel1_block, 0)

    def back1_block(block, _):
        start = pl.multiple_of(block * 8, 8)
        for rows in (range(0, 11), range(11, 22)):
            totals = conv_block(
                pad1, (taps1,), start + 2, rows, range(6, 6 + TH), lambda o, r, a, d: (0, 48 - (a * 7 + d))
            )
            for o in rows:
                g1[o, pl.ds(start, 8), :] += totals[o]
        return 0

    lax.fori_loop(0, RW // 8, back1_block, 0)

    def masked0(row, total):
        masked = m6[row + 3, pl.ds(RING_COL, RW), :] * g1[row]
        g1[row] = masked
        gpad = (masked * scale_ref[0:1, :]).astype(BF)
        normed_at = pl.ds(pl.multiple_of(row * RW, 8), RW)
        h0[normed_at, :] = gpad.astype(F32)
        return total + jnp.sum((masked * branch0[row]).reshape(RW // 8, 8, LANES), axis=0)

    total = lax.fori_loop(0, RH, masked0, jnp.zeros((8, LANES), F32))
    small[SCALE_AT : SCALE_AT + 1, :] = jnp.sum(total, axis=0, keepdims=True)
    thin[0:count0] = h0[0:count0].astype(BF)
    pad0[...] = jnp.zeros_like(pad0)

    def store0(row, value):
        pad0[row, pl.ds(PADC, RW), :] = value

    mlp_backward(
        0,
        count0,
        (RH, RW),
        normed0[...].astype(F32).reshape(count0, LANES).astype(BF),
        act0,
        slope0,
        xhat0,
        rinv0,
        store0,
    )

    gk0[...] = jnp.zeros_like(gk0)
    gk0n[...] = jnp.zeros_like(gk0n)

    def kernel0_block(block, _):
        start = pl.multiple_of(block * 8, 8)
        grads = [pad0[j, pl.ds(start + PADC, 8), :] for j in range(RH)]
        for d in range(7):
            column = [load_column(x0, r, start + 2 + d) for r in range(EH)]
            for a in range(7):
                total = gk0[a * 7 + d]
                for j in range(north_at):
                    total = total + grads[j] * column[j + a]
                gk0[a * 7 + d] = total
                total = gk0n[a * 7 + d]
                for j in range(north_at, RH):
                    total = total + grads[j] * column[j + a]
                gk0n[a * 7 + d] = total
        return 0

    lax.fori_loop(0, RW // 8, kernel0_block, 0)
    for t in range(49):
        north = jnp.where(top, gk0n[48 - t], gk0n[t])
        small[KERNEL_AT[0] + t : KERNEL_AT[0] + t + 1, :] = jnp.sum(gk0[t] + north, axis=0, keepdims=True)
        small[KERNEL_AT[1] + t : KERNEL_AT[1] + t + 1, :] = jnp.sum(gk1[t], axis=0, keepdims=True)

    def back0_block(block, _):
        start = pl.multiple_of(block * 8, 8)
        for rows in (range(0, 7), range(7, 14), range(14, 21), range(21, 28)):
            totals = conv_block(
                pad0,
                (taps0, taps0n),
                start,
                rows,
                range(6, 6 + RH),
                lambda o, r, a, d: (1 if r - 6 >= north_at else 0, 48 - (a * 7 + d)),
            )
            for o in rows:
                h0[pl.ds(pl.multiple_of(o * EW + start, 8), 8), :] = totals[o]
        return 0

    lax.fori_loop(0, EW // 8, back0_block, 0)

    def carry0(row, _):
        at = pl.multiple_of((row + 3) * EW, 8) + RING_COL
        h0[pl.ds(at, RW), :] += g1[row]
        return 0

    lax.fori_loop(0, RH, carry0, 0)
    stem_side = (m6[...].reshape(EH * EW, LANES) * h0[...]).astype(BF)
    stem_grad = contract_rows(ext[...].reshape(EH * EW, LANES).astype(BF), stem_side)
    small[STEM_AT : STEM_AT + 80, :] = stem_grad[0:80, :]
    packed_ref[SMALL_ROW : SMALL_ROW + SMALL_ROWS, :] = small[...].astype(BF)


def unpack_kernel(order_ref, pieces_ref, stem_ref, kernel_ref, gain_ref, win_ref, wout_ref, scale_ref, rows):
    count, size = pieces_ref.shape[0], pieces_ref.shape[1]
    for index in range(count):
        rows[index * size : (index + 1) * size, :] = pieces_ref[order_ref[index]].astype(F32)
    for layer in range(2):
        for part in range(4):
            at = WIN_ROW + 512 * layer + 128 * part
            win_ref[layer, :, 128 * part : 128 * part + 128] = rows[at : at + 128, :]
        at = WOUT_ROW + 512 * layer
        wout_ref[layer] = rows[at : at + 512, :]
        at = SMALL_ROW + KERNEL_AT[layer]
        kernel_ref[layer] = rows[at : at + 49, :]
    at = SMALL_ROW + STEM_AT
    stem_ref[...] = rows[at : at + stem_ref.shape[0], :]
    gain_ref[...] = rows[SMALL_ROW + GAIN_AT : SMALL_ROW + GAIN_AT + 2, :]
    scale_ref[...] = rows[SMALL_ROW + SCALE_AT : SMALL_ROW + SCALE_AT + 2, :]


def permuted(value, pairs):
    return lax.ppermute(value, "gy", pairs)


def crossed(value, bits):
    return permuted(value, [(i, i ^ bits) for i in range(lax.axis_size("gy"))])


def summed_pieces(packed):
    size = lax.axis_size("gy")
    if size != 16:
        return lax.psum(packed.astype(F32), "gy").astype(BF)[None], jnp.zeros((1,), jnp.int32)
    me = lax.axis_index("gy")
    core, side, deep = me & 1, (me >> 1) & 1, me >> 2

    def halves(value, bit):
        half = value.shape[0] // 2
        low, high = value[:half], value[half:]
        return jnp.where(bit == 0, low, high), jnp.where(bit == 0, high, low)

    keep, send = halves(packed, core)
    total = keep.astype(F32) + crossed(send, 1).astype(F32)
    keep, send = halves(total, side)
    total = keep + crossed(send.astype(BF), 2).astype(F32)
    quarter = total.shape[0] // 4

    def shard(step):
        return lax.dynamic_slice_in_dim(total, (deep ^ step) * quarter, quarter, 0)

    arrived = [crossed(shard(step).astype(BF), 4 * step) for step in (1, 2, 3)]
    mine = shard(0)
    for other in arrived:
        mine = mine + other.astype(F32)
    mine = mine.astype(BF)
    pieces = jnp.stack([mine] + [crossed(mine, 4 * step) for step in (1, 2, 3)])
    pieces = jnp.concatenate([pieces, crossed(pieces, 2)], axis=0)
    pieces = jnp.concatenate([pieces, crossed(pieces, 1)], axis=0)
    index = jnp.arange(16, dtype=jnp.int32)
    mixed = (core << 3) | (side << 2) | deep
    return pieces, index ^ mixed.astype(jnp.int32)


def shards(levels, ocean, stem, dw_kernel, ln_gain, w_in, w_out, layer_scale, upstream):
    size = lax.axis_size("gy")
    rows = size // TX
    me = lax.axis_index("gy")
    is_top = me // TX == rows - 1
    count = levels.shape[2]
    tile, west_cols, east_cols = pl.pallas_call(
        prepare_kernel,
        out_shape=[
            jax.ShapeDtypeStruct((TH, TW, LANES), BF),
            jax.ShapeDtypeStruct((TH, PADC, LANES), BF),
            jax.ShapeDtypeStruct((TH, PADC, LANES), BF),
        ],
        in_specs=vmem(2),
        out_specs=vmem(3),
        scratch_shapes=[pltpu.VMEM((LANES, count), F32)],
    )(levels[0], ocean)

    def column_pairs(step):
        return [(i, i // TX * TX + (i % TX + step) % TX) for i in range(size)]

    west = permuted(east_cols, column_pairs(1))
    east = permuted(west_cols, column_pairs(-1))
    upper = jnp.concatenate([west[-RIM:], tile[-RIM:], east[-RIM:]], axis=1)
    lower = jnp.concatenate([west[:RIM], tile[:RIM], east[:RIM]], axis=1)
    fold = permuted(upper, [(i, i // TX * TX + TX - 1 - i % TX) for i in range(size - TX, size)])
    two_rows = rows == 2
    if two_rows:
        south = north = permuted(
            jnp.where(is_top, lower, upper), [(i, (i + TX) % size) for i in range(size)]
        )
    else:
        south = permuted(upper, [(i, i + TX) for i in range(size - TX)])
        north = permuted(lower, [(i + TX, i) for i in range(size - TX)])

    def scratch(*shape, dtype=F32):
        return pltpu.VMEM(shape, dtype)

    count0 = RH * RW
    hidden = w_in.shape[2]
    result, packed = pl.pallas_call(
        functools.partial(main_kernel, two_rows, 1.0 / math.sqrt(size * count)),
        out_shape=[
            jax.ShapeDtypeStruct((TH, TW, LANES), BF),
            jax.ShapeDtypeStruct((PACKED, LANES), BF),
        ],
        in_specs=[smem()] + vmem(13),
        out_specs=vmem(2),
        scratch_shapes=[
            scratch(EH, EW, LANES),
            scratch(EH, EW, LANES),
            scratch(EH, EW, LANES),
            scratch(RH, RW, LANES),
            scratch(LANES, 2 * LANES),
            scratch(49, 8, LANES),
            scratch(49, 8, LANES),
            scratch(49, 8, LANES),
            scratch(RH, RW, LANES),
            scratch(RH, RW, LANES),
            scratch(RH, RW, LANES),
            scratch(RH, RW, LANES),
            scratch(RH, RW, LANES, dtype=BF),
            scratch(count0, hidden, dtype=BF),
            scratch(count0, hidden),
            scratch(TH, TW, LANES),
            scratch(TH, TW, LANES),
            scratch(TH, TW, LANES),
            scratch(TH, TW, LANES),
            scratch(TH, TW, LANES, dtype=BF),
            scratch(count, hidden, dtype=BF),
            scratch(count, hidden),
            scratch(count0, hidden),
            scratch(count0, LANES, dtype=BF),
            scratch(count0, hidden, dtype=BF),
            scratch(RH, EW + 8, LANES),
            scratch(TH, EW, LANES),
            scratch(RH, RW, LANES),
            scratch(EH * EW, LANES),
            scratch(49, 8, LANES),
            scratch(49, 8, LANES),
            scratch(49, 8, LANES),
            scratch(SMALL_ROWS, LANES),
        ],
        compiler_params=pltpu.CompilerParams(vmem_limit_bytes=40 << 20),
    )(
        is_top.astype(jnp.int32)[None],
        tile,
        west,
        east,
        south,
        north,
        fold,
        stem,
        dw_kernel,
        ln_gain,
        w_in,
        w_out,
        layer_scale,
        upstream[0].reshape(TH, TW, LANES),
    )
    pieces, order = summed_pieces(packed)
    shapes = [stem, dw_kernel, ln_gain, w_in, w_out, layer_scale]
    grads = pl.pallas_call(
        unpack_kernel,
        out_shape=[jax.ShapeDtypeStruct(array.shape, F32) for array in shapes],
        in_specs=[smem()] + vmem(1),
        out_specs=vmem(6),
        scratch_shapes=[scratch(PACKED, LANES)],
    )(order, pieces)
    return (result.reshape(1, TH * TW, LANES), *grads)


def solution(mesh):
    in_specs = (
        P(("groups", "gy"), None, None),
        P(("groups", "gy"), None),
        P(),
        P(),
        P(),
        P(),
        P(),
        P(),
        P(("groups", "gy"), None, None),
    )
    out_specs = (
        P(("groups", "gy"), None, None),
        P("groups", None),
        P("groups", None, None),
        P("groups", None),
        P("groups", None, None),
        P("groups", None, None),
        P("groups", None),
    )
    return jax.shard_map(shards, mesh=mesh, in_specs=in_specs, out_specs=out_specs, check_vma=False)
```

```python
import functools
import math

import jax
import jax.numpy as jnp
from jax import lax
from jax.experimental import pallas as pl
from jax.experimental.pallas import tpu as pltpu
from jax.sharding import PartitionSpec as P

TH = 16
TW = 32
TX = 8
LANES = 128

RIM = 6
PADC = 8
EH, EW = TH + 2 * RIM, TW + 2 * PADC
RH, RW = TH + 6, 40
RING_COL = 5

C0 = 0.7978845608028654
C1 = 0.7978845608028654 * 0.044715
NORM_STABILIZER = 1e-06

WIN_ROW, WOUT_ROW, SMALL_ROW = 0, 1024, 2048
STEM_AT, KERNEL_AT, GAIN_AT, SCALE_AT = 0, (80, 136), 192, 194
SMALL_ROWS = 256
PACKED = SMALL_ROW + SMALL_ROWS

BF = jnp.bfloat16
F32 = jnp.float32


def vmem(count):
    return [pl.BlockSpec(memory_space=pltpu.VMEM)] * count


def smem():
    return pl.BlockSpec(memory_space=pltpu.SMEM)


def contract_rows(left, right):
    return lax.dot_general(left, right, (((0,), (0,)), ((), ())), preferred_element_type=F32)


def contract_cols(left, right):
    return lax.dot_general(left, right, (((1,), (1,)), ((), ())), preferred_element_type=F32)


def prepare_kernel(top_ref, levels_ref, ocean_ref, tile_ref, strip_ref, fold_ref, stage):
    count, cells = levels_ref.shape
    stage[...] = jnp.zeros_like(stage)
    stage[0:count, :] = levels_ref[...].astype(F32)
    stage[count : count + 1, :] = ocean_ref[...].astype(F32)
    rows = lax.broadcasted_iota(jnp.int32, (LANES, LANES), 0)
    cols = lax.broadcasted_iota(jnp.int32, (LANES, LANES), 1)
    eye = (rows == cols).astype(BF)
    turned = contract_rows(stage[...].astype(BF), eye)
    tile_ref[...] = turned.reshape(TH, TW, LANES).astype(BF)
    side = RIM * TW
    lower, upper = turned[0:side], turned[cells - side :]
    strip_ref[...] = jnp.where(top_ref[0] == 1, lower, upper).reshape(RIM, TW, LANES).astype(BF)
    rows = lax.broadcasted_iota(jnp.int32, (side, side), 0)
    cols = lax.broadcasted_iota(jnp.int32, (side, side), 1)
    swap = (rows + cols == side - 1).astype(BF)
    fold_ref[...] = jnp.dot(swap, upper.astype(BF), preferred_element_type=F32).reshape(RIM, TW, LANES).astype(BF)


def load_column(ref, row, start):
    return ref[row, pl.ds(start, 8), :]


def conv_block(ref, taps, start, out_rows, in_rows, taps_of):
    totals = {o: None for o in out_rows}
    needed = sorted({o + a for o in out_rows for a in range(7) if o + a in in_rows})
    for d in range(7):
        column = {r: load_column(ref, r - in_rows.start, start + d) for r in needed}
        for a in range(7):
            held = {}
            for o in out_rows:
                r = o + a
                if r not in column:
                    continue
                which, index = taps_of(o, r, a, d)
                if (which, index) not in held:
                    held[(which, index)] = taps[which][index]
                term = held[(which, index)] * column[r]
                totals[o] = term if totals[o] is None else totals[o] + term
    return totals


def main_kernel(
    rescale,
    top_ref,
    tile_ref,
    west_ref,
    east_ref,
    south_ref,
    north_ref,
    stem_hbm,
    dw_hbm,
    gain_hbm,
    win_hbm,
    wout_hbm,
    scale_hbm,
    up_hbm,
    out_ref,
    packed_ref,
    ext,
    x0,
    m6,
    x1,
    weights,
    taps0,
    taps0n,
    taps1,
    conv0,
    xhat0,
    rinv0,
    branch0,
    normed0,
    act0,
    slope0,
    conv1,
    xhat1,
    rinv1,
    branch1,
    normed1,
    act1,
    slope1,
    wide,
    thin,
    gpre,
    pad0,
    pad1,
    g1,
    h0,
    gk0,
    gk0n,
    gk1,
    small,
    stem_ref,
    dw_ref,
    gain_ref,
    win_ref,
    wout_ref,
    scale_ref,
    up_ref,
    arrived,
):
    top = top_ref[0] == 1
    levels_count = stem_ref.shape[0]
    count0, count1 = RH * RW, TH * TW

    loads = [
        pltpu.make_async_copy(source, target, arrived.at[index])
        for index, (source, target) in enumerate(
            (
                (stem_hbm, stem_ref),
                (dw_hbm, dw_ref),
                (gain_hbm, gain_ref),
                (win_hbm, win_ref),
                (wout_hbm, wout_ref),
                (scale_hbm, scale_ref),
                (up_hbm, up_ref),
            )
        )
    ]
    for load in loads:
        load.start()

    ext[0:RIM, PADC : PADC + TW] = south_ref[...].astype(F32)
    ext[RIM : RIM + TH, PADC : PADC + TW] = tile_ref[...].astype(F32)
    ext[RIM + TH :, PADC : PADC + TW] = north_ref[...].astype(F32)
    ext[:, 0:PADC] = west_ref[...].astype(F32)
    ext[:, PADC + TW :] = east_ref[...].astype(F32)

    weights[...] = jnp.zeros_like(weights)
    loads[0].wait()
    weights[0:levels_count, 0:LANES] = stem_ref[...].astype(F32)
    weights[levels_count : levels_count + 1, LANES:] = jnp.ones((1, LANES), F32)
    joint = weights[...].astype(BF)

    for index in range(EH // 4):
        at = slice(index * 4, index * 4 + 4)
        both = jnp.dot(
            ext[at].reshape(4 * EW, LANES).astype(BF), joint, preferred_element_type=F32
        )
        mask = both[:, LANES:]
        m6[at] = mask.reshape(4, EW, LANES)
        x0[at] = (mask * both[:, :LANES]).astype(BF).astype(F32).reshape(4, EW, LANES)

    for load in loads[1:]:
        load.wait()
    for t in range(49):
        first = dw_ref[t, 0:1, :]
        turned = dw_ref[48 - t, 0:1, :]
        taps0[t] = jnp.broadcast_to(first, (8, LANES))
        taps0n[t] = jnp.broadcast_to(jnp.where(top, turned, first), (8, LANES))
        taps1[t] = jnp.broadcast_to(dw_ref[t, 1:2, :], (8, LANES))

    north_at = 3 + TH

    def conv0_block(block, _):
        start = pl.multiple_of(block * 8, 8)
        for rows in (range(0, 19), range(19, 22)):
            totals = conv_block(
                x0,
                (taps0, taps0n),
                start + 2,
                rows,
                range(0, EH),
                lambda o, r, a, d: (1 if o >= north_at else 0, a * 7 + d),
            )
            for o in rows:
                conv0[pl.ds(pl.multiple_of(o * RW + start, 8), 8), :] = totals[o]
        return 0

    lax.fori_loop(0, RW // 8, conv0_block, 0)

    def chunks(count, size, body):
        def run(carry):
            for index in range(count // size):
                carry = body(index, slice(index * size, index * size + size), carry)
            return carry

        return run

    def norm_rows(conv, xhat, rinv, normed, gain, count, size):
        def step(index, at, _):
            values = conv[at, :]
            average = jnp.mean(values, axis=-1, keepdims=True)
            centered = values - average
            inverse = lax.rsqrt(jnp.mean(centered * centered, axis=-1, keepdims=True) + NORM_STABILIZER)
            scaled = centered * inverse
            xhat[at, :] = scaled
            rinv[at, :] = jnp.broadcast_to(inverse, (size, LANES))
            normed[at, :] = (scaled * gain).astype(BF)
            return 0

        chunks(count, size, step)(0)

    def gelu_rows(pre, act, slope, count, size):
        def step(index, at, _):
            for part in range(size // 16):
                here = slice(index * size + part * 16, index * size + part * 16 + 16)
                v = pre[here, :]
                square = v * v
                inner = v * (C0 + C1 * square)
                half = 0.5 * jnp.tanh(inner) + 0.5
                active = v * half
                act[here, :] = active.astype(BF)
                slope[here, :] = half + active * (1.0 - half) * (2.0 * C0 + (6.0 * C1) * square)
            return 0

        chunks(count, size, step)(0)

    norm_rows(conv0, xhat0, rinv0, normed0, gain_ref[0:1, :], count0, 80)
    wide[0:count0] = jnp.dot(normed0[...], win_ref[0], preferred_element_type=F32)
    gelu_rows(wide, act0, slope0, count0, 80)
    branch0[...] = jnp.dot(act0[...], wout_ref[0], preferred_element_type=F32)

    def next0(index, at, _):
        rows = pl.ds(index * 2 + 3, 2)
        mask = m6[rows, RING_COL : RING_COL + RW, :]
        held = x0[rows, RING_COL : RING_COL + RW, :]
        branch = branch0[at, :].reshape(2, RW, LANES)
        x1[pl.ds(index * 2, 2)] = (mask * (held + scale_ref[0:1, :] * branch)).astype(BF).astype(F32)
        return 0

    chunks(count0, 2 * RW, next0)(0)

    def conv1_block(block, _):
        start = pl.multiple_of(block * 8, 8)
        for rows in (range(0, 16),):
            totals = conv_block(
                x1, (taps1,), start, rows, range(0, RH), lambda o, r, a, d: (0, a * 7 + d)
            )
            for o in rows:
                conv1[pl.ds(pl.multiple_of(o * TW + start, 8), 8), :] = totals[o]
        return 0

    lax.fori_loop(0, TW // 8, conv1_block, 0)
    norm_rows(conv1, xhat1, rinv1, normed1, gain_ref[1:2, :], count1, 64)
    wide[0:count1] = jnp.dot(normed1[...], win_ref[1], preferred_element_type=F32)
    gelu_rows(wide, act1, slope1, count1, 64)
    branch1[...] = jnp.dot(act1[...], wout_ref[1], preferred_element_type=F32)

    small[...] = jnp.zeros_like(small)
    g1[...] = jnp.zeros_like(g1)

    def folded(value):
        return jnp.sum(value.reshape(-1, 8, LANES), axis=0)

    def next1(index, at, total):
        rows = 2
        mask = m6[pl.ds(index * rows + RIM, rows), PADC : PADC + TW, :]
        held = x1[pl.ds(index * rows + 3, rows), 3 : 3 + TW, :]
        branch = branch1[at, :].reshape(rows, TW, LANES)
        out_ref[at, :] = (mask * (held + scale_ref[1:2, :] * branch)).astype(BF).reshape(rows * TW, LANES)
        masked = mask * (up_ref[at, :].astype(F32) * rescale).reshape(rows, TW, LANES)
        g1[pl.ds(index * rows + 3, rows), 3 : 3 + TW, :] = masked
        thin[at, :] = (masked * scale_ref[1:2, :]).reshape(rows * TW, LANES).astype(BF)
        return total + folded(masked * branch)

    total = chunks(count1, 2 * TW, next1)(jnp.zeros((8, LANES), F32))
    small[SCALE_AT + 1 : SCALE_AT + 2, :] = jnp.sum(total, axis=0, keepdims=True)

    def grad_wout(layer, count, act):
        packed_ref[WOUT_ROW + 512 * layer : WOUT_ROW + 512 * layer + 512, :] = contract_rows(
            act[...], thin[0:count]
        ).astype(BF)

    def grad_pre(layer, count, size, slope):
        wide[0:count] = contract_cols(thin[0:count], wout_ref[layer])

        def step(index, at, _):
            for part in range(size // 16):
                here = slice(index * size + part * 16, index * size + part * 16 + 16)
                gpre[here, :] = (wide[here, :] * slope[here, :]).astype(BF)
            return 0

        chunks(count, size, step)(0)

    def grad_win(layer, count, normed):
        gp = gpre[0:count]
        grad_in = contract_rows(normed[...], gp).astype(BF)
        for part in range(4):
            at = WIN_ROW + 512 * layer + 128 * part
            packed_ref[at : at + 128, :] = grad_in[:, 128 * part : 128 * part + 128]
        wide[0:count, 0:LANES] = contract_cols(gp, win_ref[layer])

    def grad_conv(layer, count, shape, xhat, rinv, pad):
        rows, width = shape
        gain = gain_ref[layer : layer + 1, :]

        def step(index, at, total):
            gn = wide[at, 0:LANES]
            scaled = xhat[at, :]
            gx = gn * gain
            first = jnp.mean(gx, axis=-1, keepdims=True)
            second = jnp.mean(gx * scaled, axis=-1, keepdims=True)
            value = (rinv[at, :] * (gx - first - scaled * second)).astype(BF).astype(F32)
            pad[pl.ds(index * rows, rows), PADC : PADC + width, :] = value.reshape(rows, width, LANES)
            return total + folded(gn * scaled)

        total = chunks(count, rows * width, step)(jnp.zeros((8, LANES), F32))
        small[GAIN_AT + layer : GAIN_AT + layer + 1, :] = jnp.sum(total, axis=0, keepdims=True)

    pad1[...] = jnp.zeros_like(pad1)
    grad_wout(1, count1, act1)
    grad_pre(1, count1, 64, slope1)
    grad_win(1, count1, normed1)
    grad_conv(1, count1, (2, TW), xhat1, rinv1, pad1)

    gk1[...] = jnp.zeros_like(gk1)

    def kernel1_block(block, _):
        start = pl.multiple_of(block * 8, 8)
        grads = [pad1[j, pl.ds(start + PADC, 8), :] for j in range(TH)]
        for d in range(7):
            column = [load_column(x1, r, start + d) for r in range(RH)]
            for a in range(7):
                total = gk1[a * 7 + d]
                for j in range(TH):
                    total = total + grads[j] * column[j + a]
                gk1[a * 7 + d] = total
        return 0

    lax.fori_loop(0, TW // 8, kernel1_block, 0)

    def back1_block(block, _):
        start = pl.multiple_of(block * 8, 8)
        for rows in (range(0, 22),):
            totals = conv_block(
                pad1, (taps1,), start + 2, rows, range(6, 6 + TH), lambda o, r, a, d: (0, 48 - (a * 7 + d))
            )
            for o in rows:
                g1[o, pl.ds(start, 8), :] += totals[o]
        return 0

    lax.fori_loop(0, RW // 8, back1_block, 0)

    def masked0(index, at, total):
        rows = pl.ds(index * 2, 2)
        masked = m6[pl.ds(index * 2 + 3, 2), RING_COL : RING_COL + RW, :] * g1[rows]
        g1[rows] = masked
        flat = masked.reshape(2 * RW, LANES)
        thin[at, :] = (flat * scale_ref[0:1, :]).astype(BF)
        return total + folded(flat * branch0[at, :])

    total = chunks(count0, 2 * RW, masked0)(jnp.zeros((8, LANES), F32))
    small[SCALE_AT : SCALE_AT + 1, :] = jnp.sum(total, axis=0, keepdims=True)
    pad0[...] = jnp.zeros_like(pad0)
    grad_wout(0, count0, act0)
    grad_pre(0, count0, 80, slope0)
    grad_win(0, count0, normed0)
    grad_conv(0, count0, (2, RW), xhat0, rinv0, pad0)

    gk0[...] = jnp.zeros_like(gk0)
    gk0n[...] = jnp.zeros_like(gk0n)

    def kernel0_block(block, _):
        start = pl.multiple_of(block * 8, 8)
        grads = [pad0[j, pl.ds(start + PADC, 8), :] for j in range(RH)]
        for d in range(7):
            column = [load_column(x0, r, start + 2 + d) for r in range(EH)]
            for a in range(7):
                total = gk0[a * 7 + d]
                for j in range(north_at):
                    total = total + grads[j] * column[j + a]
                gk0[a * 7 + d] = total
                total = gk0n[a * 7 + d]
                for j in range(north_at, RH):
                    total = total + grads[j] * column[j + a]
                gk0n[a * 7 + d] = total
        return 0

    lax.fori_loop(0, RW // 8, kernel0_block, 0)
    for t in range(49):
        north = jnp.where(top, gk0n[48 - t], gk0n[t])
        small[KERNEL_AT[0] + t : KERNEL_AT[0] + t + 1, :] = jnp.sum(gk0[t] + north, axis=0, keepdims=True)
        small[KERNEL_AT[1] + t : KERNEL_AT[1] + t + 1, :] = jnp.sum(gk1[t], axis=0, keepdims=True)

    def back0_block(block, _):
        start = pl.multiple_of(block * 8, 8)
        for rows in (range(0, 14), range(14, 28)):
            totals = conv_block(
                pad0,
                (taps0, taps0n),
                start,
                rows,
                range(6, 6 + RH),
                lambda o, r, a, d: (1 if r - 6 >= north_at else 0, 48 - (a * 7 + d)),
            )
            for o in rows:
                h0[o, pl.ds(start, 8), :] = totals[o]
        return 0

    lax.fori_loop(0, EW // 8, back0_block, 0)
    def carry0(index, _):
        h0[pl.ds(index * 2 + 3, 2), RING_COL : RING_COL + RW, :] += g1[pl.ds(index * 2, 2)]
        return 0

    lax.fori_loop(0, RH // 2, carry0, 0)
    stem_side = (m6[...].reshape(EH * EW, LANES) * h0[...].reshape(EH * EW, LANES)).astype(BF)
    stem_grad = contract_rows(ext[...].reshape(EH * EW, LANES).astype(BF), stem_side)
    small[STEM_AT : STEM_AT + 80, :] = stem_grad[0:80, :]
    packed_ref[SMALL_ROW : SMALL_ROW + SMALL_ROWS, :] = small[...].astype(BF)


def unpack_kernel(order_ref, pieces_ref, stem_ref, kernel_ref, gain_ref, win_ref, wout_ref, scale_ref, rows):
    count, size = pieces_ref.shape[0], pieces_ref.shape[1]
    for index in range(count):
        rows[index * size : (index + 1) * size, :] = pieces_ref[order_ref[index]].astype(F32)
    for layer in range(2):
        for part in range(4):
            at = WIN_ROW + 512 * layer + 128 * part
            win_ref[layer, :, 128 * part : 128 * part + 128] = rows[at : at + 128, :]
        at = WOUT_ROW + 512 * layer
        wout_ref[layer] = rows[at : at + 512, :]
        at = SMALL_ROW + KERNEL_AT[layer]
        kernel_ref[:, layer, :] = rows[at : at + 49, :]
    at = SMALL_ROW + STEM_AT
    stem_ref[...] = rows[at : at + stem_ref.shape[0], :]
    gain_ref[...] = rows[SMALL_ROW + GAIN_AT : SMALL_ROW + GAIN_AT + 2, :]
    scale_ref[...] = rows[SMALL_ROW + SCALE_AT : SMALL_ROW + SCALE_AT + 2, :]


def permuted(value, pairs):
    return lax.ppermute(value, "gy", pairs)


def crossed(value, bits):
    return permuted(value, [(i, i ^ bits) for i in range(lax.axis_size("gy"))])


def summed_pieces(packed):
    size = lax.axis_size("gy")
    if size != 16:
        return lax.psum(packed.astype(F32), "gy").astype(BF)[None], jnp.zeros((1,), jnp.int32)
    me = lax.axis_index("gy")
    core, side, deep = me & 1, (me >> 1) & 1, me >> 2

    def halves(value, bit):
        half = value.shape[0] // 2
        low, high = value[:half], value[half:]
        return jnp.where(bit == 0, low, high), jnp.where(bit == 0, high, low)

    keep, send = halves(packed, core)
    total = keep.astype(F32) + crossed(send, 1).astype(F32)
    keep, send = halves(total, side)
    total = keep + crossed(send.astype(BF), 2).astype(F32)
    quarter = total.shape[0] // 4

    def shard(step):
        return lax.dynamic_slice_in_dim(total, (deep ^ step) * quarter, quarter, 0)

    arrived = [crossed(shard(step).astype(BF), 4 * step) for step in (1, 2, 3)]
    mine = shard(0)
    for other in arrived:
        mine = mine + other.astype(F32)
    mine = mine.astype(BF)
    pieces = jnp.stack([mine] + [crossed(mine, 4 * step) for step in (1, 2, 3)])
    pieces = jnp.concatenate([pieces, crossed(pieces, 2)], axis=0)
    pieces = jnp.concatenate([pieces, crossed(pieces, 1)], axis=0)
    index = jnp.arange(16, dtype=jnp.int32)
    mixed = (core << 3) | (side << 2) | deep
    return pieces, index ^ mixed.astype(jnp.int32)


def shards(levels, ocean, stem, dw_kernel, ln_gain, w_in, w_out, layer_scale, upstream):
    size = lax.axis_size("gy")
    rows = size // TX
    me = lax.axis_index("gy")
    is_top = me // TX == rows - 1
    count = levels.shape[2]
    top = is_top.astype(jnp.int32)[None]
    tile, strip, folded = pl.pallas_call(
        prepare_kernel,
        out_shape=[
            jax.ShapeDtypeStruct((TH, TW, LANES), BF),
            jax.ShapeDtypeStruct((RIM, TW, LANES), BF),
            jax.ShapeDtypeStruct((RIM, TW, LANES), BF),
        ],
        in_specs=[smem()] + vmem(2),
        out_specs=vmem(3),
        scratch_shapes=[pltpu.VMEM((LANES, count), F32)],
        compiler_params=pltpu.CompilerParams(vmem_limit_bytes=4 << 20),
    )(top, levels[0], ocean)
    if rows == 2:
        south = north = permuted(strip, [(i, (i + TX) % size) for i in range(size)])
        south = jnp.where(is_top, south, jnp.zeros_like(south))
    else:
        south = permuted(tile[-RIM:], [(i, i + TX) for i in range(size - TX)])
        north = permuted(tile[:RIM], [(i + TX, i) for i in range(size - TX)])
    folded = permuted(folded, [(i, i // TX * TX + TX - 1 - i % TX) for i in range(size - TX, size)])
    north = jnp.where(is_top, folded, north)

    def columns(at):
        return jnp.concatenate([south[:, at], tile[:, at], north[:, at]], axis=0)

    def column_pairs(step):
        return [(i, i // TX * TX + (i % TX + step) % TX) for i in range(size)]

    west = permuted(columns(slice(TW - PADC, TW)), column_pairs(1))
    east = permuted(columns(slice(0, PADC)), column_pairs(-1))

    def scratch(*shape, dtype=F32):
        return pltpu.VMEM(shape, dtype)

    count0 = RH * RW
    hidden = w_in.shape[2]
    result, packed = pl.pallas_call(
        functools.partial(main_kernel, 1.0 / math.sqrt(size * count)),
        out_shape=[
            jax.ShapeDtypeStruct((count, LANES), BF),
            jax.ShapeDtypeStruct((PACKED, LANES), BF),
        ],
        in_specs=[smem()] + vmem(5) + [pl.BlockSpec(memory_space=pltpu.HBM)] * 7,
        out_specs=vmem(2),
        scratch_shapes=[
            scratch(EH, EW, LANES),
            scratch(EH, EW, LANES),
            scratch(EH, EW, LANES),
            scratch(RH, RW, LANES),
            scratch(LANES, 2 * LANES),
            scratch(49, 8, LANES),
            scratch(49, 8, LANES),
            scratch(49, 8, LANES),
            scratch(count0, LANES),
            scratch(count0, LANES),
            scratch(count0, LANES),
            scratch(count0, LANES),
            scratch(count0, LANES, dtype=BF),
            scratch(count0, hidden, dtype=BF),
            scratch(count0, hidden),
            scratch(count, LANES),
            scratch(count, LANES),
            scratch(count, LANES),
            scratch(count, LANES),
            scratch(count, LANES, dtype=BF),
            scratch(count, hidden, dtype=BF),
            scratch(count, hidden),
            scratch(count0, hidden),
            scratch(count0, LANES, dtype=BF),
            scratch(count0, hidden, dtype=BF),
            scratch(RH, EW + 8, LANES),
            scratch(TH, EW, LANES),
            scratch(RH, RW, LANES),
            scratch(EH, EW, LANES),
            scratch(49, 8, LANES),
            scratch(49, 8, LANES),
            scratch(49, 8, LANES),
            scratch(SMALL_ROWS, LANES),
            pltpu.VMEM(stem.shape, BF),
            scratch(dw_kernel.shape[1], dw_kernel.shape[0], LANES),
            scratch(*ln_gain.shape),
            scratch(*w_in.shape, dtype=BF),
            scratch(*w_out.shape, dtype=BF),
            scratch(*layer_scale.shape),
            scratch(count, LANES, dtype=BF),
            pltpu.SemaphoreType.DMA((7,)),
        ],
        compiler_params=pltpu.CompilerParams(vmem_limit_bytes=28 << 20),
    )(
        top,
        tile,
        west,
        east,
        south,
        north,
        stem,
        dw_kernel.transpose(1, 0, 2),
        ln_gain,
        w_in,
        w_out,
        layer_scale,
        upstream[0],
    )
    pieces, order = summed_pieces(packed)
    shapes = [array.shape for array in (stem, dw_kernel, ln_gain, w_in, w_out, layer_scale)]
    shapes[1] = (shapes[1][1], shapes[1][0], shapes[1][2])
    grads = pl.pallas_call(
        unpack_kernel,
        out_shape=[jax.ShapeDtypeStruct(shape, F32) for shape in shapes],
        in_specs=[smem()] + vmem(1),
        out_specs=vmem(6),
        scratch_shapes=[scratch(PACKED, LANES)],
        compiler_params=pltpu.CompilerParams(vmem_limit_bytes=8 << 20),
    )(order, pieces)
    grads = list(grads)
    grads[1] = grads[1].transpose(1, 0, 2)
    return (result[None], *grads)


def solution(mesh):
    in_specs = (
        P(("groups", "gy"), None, None),
        P(("groups", "gy"), None),
        P(),
        P(),
        P(),
        P(),
        P(),
        P(),
        P(("groups", "gy"), None, None),
    )
    out_specs = (
        P(("groups", "gy"), None, None),
        P("groups", None),
        P("groups", None, None),
        P("groups", None),
        P("groups", None, None),
        P("groups", None, None),
        P("groups", None),
    )
    return jax.shard_map(shards, mesh=mesh, in_specs=in_specs, out_specs=out_specs, check_vma=False)
```

```python
import functools
import math

import jax
import jax.numpy as jnp
from jax import lax
from jax.experimental import pallas as pl
from jax.experimental.pallas import tpu as pltpu
from jax.sharding import PartitionSpec as P

TH = 16
TW = 32
TX = 8
LANES = 128

RIM = 6
PADC = 8
EH, EW = TH + 2 * RIM, TW + 2 * PADC
RH, RW = TH + 6, 40
RING_COL = 5

C0 = 0.7978845608028654
C1 = 0.7978845608028654 * 0.044715
NORM_STABILIZER = 1e-06

WIN_ROW, WOUT_ROW, BULK = 0, 1024, 2048
STEM_AT, KERNEL_AT, GAIN_AT, SCALE_AT = 0, (75, 124), 173, 175
SMALL = 192

BF = jnp.bfloat16
F32 = jnp.float32


def vmem(count):
    return [pl.BlockSpec(memory_space=pltpu.VMEM)] * count


def smem():
    return pl.BlockSpec(memory_space=pltpu.SMEM)


def contract_rows(left, right):
    return lax.dot_general(left, right, (((0,), (0,)), ((), ())), preferred_element_type=F32)


def contract_cols(left, right):
    return lax.dot_general(left, right, (((1,), (1,)), ((), ())), preferred_element_type=F32)


def prepare_kernel(top_ref, levels_ref, ocean_ref, tile_ref, strip_ref, fold_ref, stage):
    count, cells = levels_ref.shape
    stage[...] = jnp.zeros_like(stage)
    stage[0:count, :] = levels_ref[...].astype(F32)
    stage[count : count + 1, :] = ocean_ref[...].astype(F32)
    rows = lax.broadcasted_iota(jnp.int32, (LANES, LANES), 0)
    cols = lax.broadcasted_iota(jnp.int32, (LANES, LANES), 1)
    eye = (rows == cols).astype(BF)
    turned = contract_rows(stage[...].astype(BF), eye)
    tile_ref[...] = turned.reshape(TH, TW, LANES).astype(BF)
    side = RIM * TW
    lower, upper = turned[0:side], turned[cells - side :]
    strip_ref[...] = jnp.where(top_ref[0] == 1, lower, upper).reshape(RIM, TW, LANES).astype(BF)
    rows = lax.broadcasted_iota(jnp.int32, (side, side), 0)
    cols = lax.broadcasted_iota(jnp.int32, (side, side), 1)
    swap = (rows + cols == side - 1).astype(BF)
    fold_ref[...] = jnp.dot(swap, upper.astype(BF), preferred_element_type=F32).reshape(RIM, TW, LANES).astype(BF)


def load_column(ref, row, start):
    return ref[row, pl.ds(start, 8), :]


def conv_block(ref, taps, start, out_rows, in_rows, taps_of):
    totals = {o: None for o in out_rows}
    needed = sorted({o + a for o in out_rows for a in range(7) if o + a in in_rows})
    for d in range(7):
        column = {r: load_column(ref, r - in_rows.start, start + d) for r in needed}
        for a in range(7):
            held = {}
            for o in out_rows:
                r = o + a
                if r not in column:
                    continue
                which, index = taps_of(o, r, a, d)
                if (which, index) not in held:
                    held[(which, index)] = taps[which][index]
                term = held[(which, index)] * column[r]
                totals[o] = term if totals[o] is None else totals[o] + term
    return totals


def spread_taps(dw_ref, layer, taps, top=None):
    for t in range(49):
        row = dw_ref[t, layer : layer + 1, :]
        if top is not None:
            row = jnp.where(top, dw_ref[48 - t, layer : layer + 1, :], row)
        taps[t] = jnp.broadcast_to(row, (8, LANES))


def padded(flat, pad, width):
    rows = flat.shape[0] // width
    pad[:, 0:PADC, :] = jnp.zeros((rows, PADC, LANES), F32)
    pad[:, PADC + width :, :] = jnp.zeros((rows, pad.shape[1] - PADC - width, LANES), F32)
    for row in range(0, rows, 2):
        value = flat[row * width : (row + 2) * width, :].astype(F32)
        pad[row : row + 2, PADC : PADC + width, :] = value.reshape(2, width, LANES)


def main_kernel(
    rescale,
    top_ref,
    tile_ref,
    west_ref,
    east_ref,
    south_ref,
    north_ref,
    stem_hbm,
    dw_hbm,
    gain_hbm,
    win_hbm,
    wout_hbm,
    scale_hbm,
    up_hbm,
    out_ref,
    packed_ref,
    sums,
    cells,
    flat0,
    flat1,
    grad0,
    grad1,
    carry0,
    x0,
    m6,
    x1,
    taps0,
    taps0n,
    pad1,
    g1,
    ext,
    weights,
    taps1,
    conv0,
    xhat0,
    rinv0,
    branch0,
    normed0,
    act0,
    slope0,
    conv1,
    xhat1,
    rinv1,
    branch1,
    normed1,
    act1,
    slope1,
    wide,
    thin,
    gpre,
    stem_ref,
    dw_ref,
    gain_ref,
    win_ref,
    wout_ref,
    scale_ref,
    up_ref,
    arrived,
):
    top = top_ref[0] == 1
    levels_count = stem_ref.shape[0]
    count0, count1 = RH * RW, TH * TW

    loads = [
        pltpu.make_async_copy(source, target, arrived.at[index])
        for index, (source, target) in enumerate(
            (
                (stem_hbm, stem_ref),
                (dw_hbm, dw_ref),
                (gain_hbm, gain_ref),
                (win_hbm, win_ref),
                (wout_hbm, wout_ref),
                (scale_hbm, scale_ref),
                (up_hbm, up_ref),
            )
        )
    ]
    for load in loads:
        load.start()

    ext[0:RIM, PADC : PADC + TW] = south_ref[...].astype(F32)
    ext[RIM : RIM + TH, PADC : PADC + TW] = tile_ref[...].astype(F32)
    ext[RIM + TH :, PADC : PADC + TW] = north_ref[...].astype(F32)
    ext[:, 0:PADC] = west_ref[...].astype(F32)
    ext[:, PADC + TW :] = east_ref[...].astype(F32)

    weights[...] = jnp.zeros_like(weights)
    loads[0].wait()
    weights[0:levels_count, 0:LANES] = stem_ref[...].astype(F32)
    weights[levels_count : levels_count + 1, LANES:] = jnp.ones((1, LANES), F32)
    joint = weights[...].astype(BF)

    for index in range(EH // 4):
        at = slice(index * 4, index * 4 + 4)
        here = ext[at].reshape(4 * EW, LANES).astype(BF)
        cells[index * 4 * EW : (index + 1) * 4 * EW, :] = here
        both = jnp.dot(here, joint, preferred_element_type=F32)
        mask = both[:, LANES:]
        m6[at] = mask.reshape(4, EW, LANES)
        value = (mask * both[:, :LANES]).astype(BF)
        flat0[index * 4 * EW : (index + 1) * 4 * EW, :] = value
        x0[at] = value.astype(F32).reshape(4, EW, LANES)

    for load in loads[1:]:
        load.wait()
    spread_taps(dw_ref, 0, taps0)
    spread_taps(dw_ref, 0, taps0n, top)
    spread_taps(dw_ref, 1, taps1)

    north_at = 3 + TH

    def conv0_block(block, _):
        start = pl.multiple_of(block * 8, 8)
        for rows in (range(0, 19), range(19, 22)):
            totals = conv_block(
                x0,
                (taps0, taps0n),
                start + 2,
                rows,
                range(0, EH),
                lambda o, r, a, d: (1 if o >= north_at else 0, a * 7 + d),
            )
            for o in rows:
                conv0[pl.ds(pl.multiple_of(o * RW + start, 8), 8), :] = totals[o]
        return 0

    lax.fori_loop(0, RW // 8, conv0_block, 0)

    def chunks(count, size, body):
        def run(carry):
            for index in range(count // size):
                carry = body(index, slice(index * size, index * size + size), carry)
            return carry

        return run

    def norm_rows(conv, xhat, rinv, normed, gain, count, size):
        def step(index, at, _):
            values = conv[at, :]
            average = jnp.mean(values, axis=-1, keepdims=True)
            centered = values - average
            inverse = lax.rsqrt(jnp.mean(centered * centered, axis=-1, keepdims=True) + NORM_STABILIZER)
            scaled = centered * inverse
            xhat[at, :] = scaled
            rinv[at, :] = jnp.broadcast_to(inverse, (size, LANES))
            normed[at, :] = (scaled * gain).astype(BF)
            return 0

        chunks(count, size, step)(0)

    def gelu_rows(pre, act, slope, count, size):
        def step(index, at, _):
            for part in range(size // 16):
                here = slice(index * size + part * 16, index * size + part * 16 + 16)
                v = pre[here, :]
                square = v * v
                inner = v * (C0 + C1 * square)
                half = 0.5 * jnp.tanh(inner) + 0.5
                active = v * half
                act[here, :] = active.astype(BF)
                slope[here, :] = half + active * (1.0 - half) * (2.0 * C0 + (6.0 * C1) * square)
            return 0

        chunks(count, size, step)(0)

    norm_rows(conv0, xhat0, rinv0, normed0, gain_ref[0:1, :], count0, 80)
    wide[0:count0] = jnp.dot(normed0[...], win_ref[0], preferred_element_type=F32)
    gelu_rows(wide, act0, slope0, count0, 80)
    branch0[...] = jnp.dot(act0[...], wout_ref[0], preferred_element_type=F32)

    def next0(index, at, _):
        rows = pl.ds(index * 2 + 3, 2)
        mask = m6[rows, RING_COL : RING_COL + RW, :]
        held = x0[rows, RING_COL : RING_COL + RW, :]
        branch = branch0[at, :].reshape(2, RW, LANES)
        value = (mask * (held + scale_ref[0:1, :] * branch)).astype(BF)
        flat1[at, :] = value.reshape(2 * RW, LANES)
        x1[pl.ds(index * 2, 2)] = value.astype(F32)
        return 0

    chunks(count0, 2 * RW, next0)(0)

    def conv1_block(block, _):
        start = pl.multiple_of(block * 8, 8)
        for rows in (range(0, 16),):
            totals = conv_block(
                x1, (taps1,), start, rows, range(0, RH), lambda o, r, a, d: (0, a * 7 + d)
            )
            for o in rows:
                conv1[pl.ds(pl.multiple_of(o * TW + start, 8), 8), :] = totals[o]
        return 0

    lax.fori_loop(0, TW // 8, conv1_block, 0)
    norm_rows(conv1, xhat1, rinv1, normed1, gain_ref[1:2, :], count1, 64)
    wide[0:count1] = jnp.dot(normed1[...], win_ref[1], preferred_element_type=F32)
    gelu_rows(wide, act1, slope1, count1, 64)
    branch1[...] = jnp.dot(act1[...], wout_ref[1], preferred_element_type=F32)

    sums[...] = jnp.zeros_like(sums)
    g1[...] = jnp.zeros_like(g1)

    def folded(value):
        return jnp.sum(value.reshape(-1, 8, LANES), axis=0)

    def next1(index, at, total):
        rows = 2
        mask = m6[pl.ds(index * rows + RIM, rows), PADC : PADC + TW, :]
        held = x1[pl.ds(index * rows + 3, rows), 3 : 3 + TW, :]
        branch = branch1[at, :].reshape(rows, TW, LANES)
        out_ref[at, :] = (mask * (held + scale_ref[1:2, :] * branch)).astype(BF).reshape(rows * TW, LANES)
        masked = mask * (up_ref[at, :].astype(F32) * rescale).reshape(rows, TW, LANES)
        g1[pl.ds(index * rows + 3, rows), 3 : 3 + TW, :] = masked
        thin[at, :] = (masked * scale_ref[1:2, :]).reshape(rows * TW, LANES).astype(BF)
        return total + folded(masked * branch)

    total = chunks(count1, 2 * TW, next1)(jnp.zeros((8, LANES), F32))
    sums[3:4, :] = jnp.sum(total, axis=0, keepdims=True)

    def grad_wout(layer, count, act):
        packed_ref[WOUT_ROW + 512 * layer : WOUT_ROW + 512 * layer + 512, :] = contract_rows(
            act[...], thin[0:count]
        ).astype(BF)

    def grad_pre(layer, count, size, slope):
        wide[0:count] = contract_cols(thin[0:count], wout_ref[layer])

        def step(index, at, _):
            for part in range(size // 16):
                here = slice(index * size + part * 16, index * size + part * 16 + 16)
                gpre[here, :] = (wide[here, :] * slope[here, :]).astype(BF)
            return 0

        chunks(count, size, step)(0)

    def grad_win(layer, count, normed):
        gp = gpre[0:count]
        grad_in = contract_rows(normed[...], gp).astype(BF)
        for part in range(4):
            at = WIN_ROW + 512 * layer + 128 * part
            packed_ref[at : at + 128, :] = grad_in[:, 128 * part : 128 * part + 128]
        wide[0:count, 0:LANES] = contract_cols(gp, win_ref[layer])

    def grad_conv(layer, count, size, xhat, rinv, grad):
        gain = gain_ref[layer : layer + 1, :]

        def step(index, at, total):
            gn = wide[at, 0:LANES]
            scaled = xhat[at, :]
            gx = gn * gain
            first = jnp.mean(gx, axis=-1, keepdims=True)
            second = jnp.mean(gx * scaled, axis=-1, keepdims=True)
            grad[at, :] = (rinv[at, :] * (gx - first - scaled * second)).astype(BF)
            return total + folded(gn * scaled)

        total = chunks(count, size, step)(jnp.zeros((8, LANES), F32))
        sums[layer : layer + 1, :] = jnp.sum(total, axis=0, keepdims=True)

    grad_wout(1, count1, act1)
    grad_pre(1, count1, 64, slope1)
    grad_win(1, count1, normed1)
    grad_conv(1, count1, 2 * TW, xhat1, rinv1, grad1)
    padded(grad1, pad1, TW)

    def back1_block(block, _):
        start = pl.multiple_of(block * 8, 8)
        for rows in (range(0, 22),):
            totals = conv_block(
                pad1, (taps1,), start + 2, rows, range(6, 6 + TH), lambda o, r, a, d: (0, 48 - (a * 7 + d))
            )
            for o in rows:
                g1[o, pl.ds(start, 8), :] += totals[o]
        return 0

    lax.fori_loop(0, RW // 8, back1_block, 0)

    def masked0(index, at, total):
        rows = pl.ds(index * 2, 2)
        masked = m6[pl.ds(index * 2 + 3, 2), RING_COL : RING_COL + RW, :] * g1[rows]
        flat = masked.reshape(2 * RW, LANES)
        carry0[at, :] = flat
        thin[at, :] = (flat * scale_ref[0:1, :]).astype(BF)
        return total + folded(flat * branch0[at, :])

    total = chunks(count0, 2 * RW, masked0)(jnp.zeros((8, LANES), F32))
    sums[2:3, :] = jnp.sum(total, axis=0, keepdims=True)
    grad_wout(0, count0, act0)
    grad_pre(0, count0, 80, slope0)
    grad_win(0, count0, normed0)
    grad_conv(0, count0, 2 * RW, xhat0, rinv0, grad0)


def rest_kernel(
    top_ref,
    dw_ref,
    sums,
    cells,
    flat0,
    flat1,
    grad0,
    grad1,
    carry0,
    small_ref,
    small,
    x0,
    x1,
    pad0,
    pad1,
    taps0,
    taps0n,
    h0,
    gk0,
    gk0n,
    gk1,
):
    top = top_ref[0] == 1
    north_at = 3 + TH
    levels_count = KERNEL_AT[0] - STEM_AT

    for row in range(0, EH, 4):
        x0[row : row + 4] = flat0[row * EW : (row + 4) * EW, :].astype(F32).reshape(4, EW, LANES)
    for row in range(0, RH, 2):
        x1[row : row + 2] = flat1[row * RW : (row + 2) * RW, :].astype(F32).reshape(2, RW, LANES)
    padded(grad0, pad0, RW)
    padded(grad1, pad1, TW)
    spread_taps(dw_ref, 0, taps0)
    spread_taps(dw_ref, 0, taps0n, top)

    gk1[...] = jnp.zeros_like(gk1)

    def kernel1_block(block, _):
        start = pl.multiple_of(block * 8, 8)
        grads = [pad1[j, pl.ds(start + PADC, 8), :] for j in range(TH)]
        for d in range(7):
            column = [load_column(x1, r, start + d) for r in range(RH)]
            for a in range(7):
                total = gk1[a * 7 + d]
                for j in range(TH):
                    total = total + grads[j] * column[j + a]
                gk1[a * 7 + d] = total
        return 0

    lax.fori_loop(0, TW // 8, kernel1_block, 0)

    gk0[...] = jnp.zeros_like(gk0)
    gk0n[...] = jnp.zeros_like(gk0n)

    def kernel0_block(block, _):
        start = pl.multiple_of(block * 8, 8)
        grads = [pad0[j, pl.ds(start + PADC, 8), :] for j in range(RH)]
        for d in range(7):
            column = [load_column(x0, r, start + 2 + d) for r in range(EH)]
            for a in range(7):
                total = gk0[a * 7 + d]
                for j in range(north_at):
                    total = total + grads[j] * column[j + a]
                gk0[a * 7 + d] = total
                total = gk0n[a * 7 + d]
                for j in range(north_at, RH):
                    total = total + grads[j] * column[j + a]
                gk0n[a * 7 + d] = total
        return 0

    lax.fori_loop(0, RW // 8, kernel0_block, 0)
    for t in range(49):
        north = jnp.where(top, gk0n[48 - t], gk0n[t])
        small[KERNEL_AT[0] + t : KERNEL_AT[0] + t + 1, :] = jnp.sum(gk0[t] + north, axis=0, keepdims=True)
        small[KERNEL_AT[1] + t : KERNEL_AT[1] + t + 1, :] = jnp.sum(gk1[t], axis=0, keepdims=True)

    def back0_block(block, _):
        start = pl.multiple_of(block * 8, 8)
        for rows in (range(0, 14), range(14, 28)):
            totals = conv_block(
                pad0,
                (taps0, taps0n),
                start,
                rows,
                range(6, 6 + RH),
                lambda o, r, a, d: (1 if r - 6 >= north_at else 0, 48 - (a * 7 + d)),
            )
            for o in rows:
                h0[o, pl.ds(start, 8), :] = totals[o]
        return 0

    lax.fori_loop(0, EW // 8, back0_block, 0)
    for row in range(0, RH, 2):
        h0[row + 3 : row + 5, RING_COL : RING_COL + RW, :] += carry0[
            row * RW : (row + 2) * RW, :
        ].reshape(2, RW, LANES)
    rows = lax.broadcasted_iota(jnp.int32, (LANES, LANES), 0)
    mask = jnp.dot(cells[...], (rows == levels_count).astype(BF), preferred_element_type=F32)
    stem_side = (mask * h0[...].reshape(EH * EW, LANES)).astype(BF)
    stem_grad = contract_rows(cells[...], stem_side)
    small[STEM_AT : KERNEL_AT[0], :] = stem_grad[0:levels_count, :]
    small[GAIN_AT : GAIN_AT + 4, :] = sums[0:4, :]
    small[GAIN_AT + 4 :, :] = jnp.zeros((SMALL - GAIN_AT - 4, LANES), F32)
    small_ref[...] = small[...].astype(BF)


def unpack_kernel(
    order_ref, pieces_ref, mine_ref, other_ref, stem_ref, kernel_ref, gain_ref, win_ref, wout_ref, scale_ref, rows, small
):
    count, size = pieces_ref.shape[0], pieces_ref.shape[1]
    for index in range(count):
        rows[index * size : (index + 1) * size, :] = pieces_ref[order_ref[index]].astype(F32)
    count, size = mine_ref.shape[0], mine_ref.shape[1]
    for index in range(count):
        at = order_ref[pieces_ref.shape[0] + index]
        small[index * size : (index + 1) * size, :] = mine_ref[at].astype(F32) + other_ref[at].astype(F32)
    for layer in range(2):
        for part in range(4):
            at = WIN_ROW + 512 * layer + 128 * part
            win_ref[layer, :, 128 * part : 128 * part + 128] = rows[at : at + 128, :]
        at = WOUT_ROW + 512 * layer
        wout_ref[layer] = rows[at : at + 512, :]
        at = KERNEL_AT[layer]
        kernel_ref[:, layer, :] = small[at : at + 49, :]
    stem_ref[...] = small[STEM_AT : STEM_AT + stem_ref.shape[0], :]
    gain_ref[...] = small[GAIN_AT : GAIN_AT + 2, :]
    scale_ref[...] = small[SCALE_AT : SCALE_AT + 2, :]


def permuted(value, pairs):
    return lax.ppermute(value, "gy", pairs)


def crossed(value, bits):
    return permuted(value, [(i, i ^ bits) for i in range(lax.axis_size("gy"))])


def summed_pieces(packed, top, rest):
    size = lax.axis_size("gy")
    if size != 16:
        bulk, small = lax.psum((packed.astype(F32), rest(top).astype(F32)), "gy")
        small = small.astype(BF)[None]
        return bulk.astype(BF)[None], small, jnp.zeros_like(small), jnp.zeros((2,), jnp.int32)
    me = lax.axis_index("gy")
    core, side, deep = me & 1, (me >> 1) & 1, me >> 2

    def halves(value, bit):
        half = value.shape[0] // 2
        low, high = value[:half], value[half:]
        return jnp.where(bit == 0, low, high), jnp.where(bit == 0, high, low)

    keep, send = halves(packed, core)
    came = crossed(send, 1)
    came, top = lax.optimization_barrier((came, top))
    small = rest(top)
    keep, send = halves(keep.astype(F32) + came.astype(F32), side)
    total = keep + crossed(send.astype(BF), 2).astype(F32)
    quarter = total.shape[0] // 4
    part = small.shape[0] // 4

    def shard(step):
        at = deep ^ step
        return jnp.concatenate(
            [
                lax.dynamic_slice_in_dim(total, at * quarter, quarter, 0).astype(BF),
                lax.dynamic_slice_in_dim(small, at * part, part, 0),
            ],
            axis=0,
        )

    arrived = [crossed(shard(step), 4 * step) for step in (1, 2, 3)]
    bulk = lax.dynamic_slice_in_dim(total, deep * quarter, quarter, 0)
    rest_sum = lax.dynamic_slice_in_dim(small, deep * part, part, 0).astype(F32)
    for other in arrived:
        bulk = bulk + other[:quarter].astype(F32)
        rest_sum = rest_sum + other[quarter:].astype(F32)
    mine = jnp.concatenate([bulk.astype(BF), rest_sum.astype(BF)], axis=0)
    pieces = jnp.stack([mine] + [crossed(mine, 4 * step) for step in (1, 2, 3)])
    came = crossed(pieces, 2)
    bulk = jnp.concatenate([pieces[:, :quarter], came[:, :quarter]], axis=0)
    small = (pieces[:, quarter:].astype(F32) + came[:, quarter:].astype(F32)).astype(BF)
    rows = bulk.shape[0] * quarter
    joined = jnp.concatenate([bulk.reshape(rows, LANES), small.reshape(4 * part, LANES)], axis=0)
    came = crossed(joined, 1)
    bulk = jnp.concatenate([bulk, came[:rows].reshape(bulk.shape)], axis=0)
    mixed = ((core << 3) | (side << 2) | deep).astype(jnp.int32)
    order = jnp.arange(20, dtype=jnp.int32) & 15
    order = order ^ jnp.where(jnp.arange(20) < 16, mixed, deep.astype(jnp.int32))
    return bulk, small, came[rows:].reshape(small.shape), order


def shards(levels, ocean, stem, dw_kernel, ln_gain, w_in, w_out, layer_scale, upstream):
    size = lax.axis_size("gy")
    rows = size // TX
    me = lax.axis_index("gy")
    is_top = me // TX == rows - 1
    count = levels.shape[2]
    top = is_top.astype(jnp.int32)[None]
    taps = dw_kernel.transpose(1, 0, 2)
    tile, strip, folded = pl.pallas_call(
        prepare_kernel,
        out_shape=[
            jax.ShapeDtypeStruct((TH, TW, LANES), BF),
            jax.ShapeDtypeStruct((RIM, TW, LANES), BF),
            jax.ShapeDtypeStruct((RIM, TW, LANES), BF),
        ],
        in_specs=[smem()] + vmem(2),
        out_specs=vmem(3),
        scratch_shapes=[pltpu.VMEM((LANES, count), F32)],
        compiler_params=pltpu.CompilerParams(vmem_limit_bytes=4 << 20),
    )(top, levels[0], ocean)
    if rows == 2:
        south = north = permuted(strip, [(i, (i + TX) % size) for i in range(size)])
        south = jnp.where(is_top, south, jnp.zeros_like(south))
    else:
        south = permuted(tile[-RIM:], [(i, i + TX) for i in range(size - TX)])
        north = permuted(tile[:RIM], [(i + TX, i) for i in range(size - TX)])
    folded = permuted(folded, [(i, i // TX * TX + TX - 1 - i % TX) for i in range(size - TX, size)])
    north = jnp.where(is_top, folded, north)

    def columns(at):
        return jnp.concatenate([south[:, at], tile[:, at], north[:, at]], axis=0)

    def column_pairs(step):
        return [(i, i // TX * TX + (i % TX + step) % TX) for i in range(size)]

    west = permuted(columns(slice(TW - PADC, TW)), column_pairs(1))
    east = permuted(columns(slice(0, PADC)), column_pairs(-1))

    def scratch(*shape, dtype=F32):
        return pltpu.VMEM(shape, dtype)

    count0 = RH * RW
    hidden = w_in.shape[2]
    ring_shapes = [
        jax.ShapeDtypeStruct((8, LANES), F32),
        jax.ShapeDtypeStruct((EH * EW, LANES), BF),
        jax.ShapeDtypeStruct((EH * EW, LANES), BF),
        jax.ShapeDtypeStruct((RH * RW, LANES), BF),
        jax.ShapeDtypeStruct((RH * RW, LANES), BF),
        jax.ShapeDtypeStruct((TH * TW, LANES), BF),
        jax.ShapeDtypeStruct((RH * RW, LANES), F32),
    ]
    result, packed, *ring = pl.pallas_call(
        functools.partial(main_kernel, 1.0 / math.sqrt(size * count)),
        out_shape=[
            jax.ShapeDtypeStruct((count, LANES), BF),
            jax.ShapeDtypeStruct((BULK, LANES), BF),
        ]
        + ring_shapes,
        in_specs=[smem()] + vmem(5) + [pl.BlockSpec(memory_space=pltpu.HBM)] * 7,
        out_specs=vmem(9),
        scratch_shapes=[
            scratch(EH, EW, LANES),
            scratch(EH, EW, LANES),
            scratch(RH, RW, LANES),
            scratch(49, 8, LANES),
            scratch(49, 8, LANES),
            scratch(TH, EW, LANES),
            scratch(RH, RW, LANES),
            scratch(EH, EW, LANES),
            scratch(LANES, 2 * LANES),
            scratch(49, 8, LANES),
            scratch(count0, LANES),
            scratch(count0, LANES),
            scratch(count0, LANES),
            scratch(count0, LANES),
            scratch(count0, LANES, dtype=BF),
            scratch(count0, hidden, dtype=BF),
            scratch(count0, hidden),
            scratch(count, LANES),
            scratch(count, LANES),
            scratch(count, LANES),
            scratch(count, LANES),
            scratch(count, LANES, dtype=BF),
            scratch(count, hidden, dtype=BF),
            scratch(count, hidden),
            scratch(count0, hidden),
            scratch(count0, LANES, dtype=BF),
            scratch(count0, hidden, dtype=BF),
            pltpu.VMEM(stem.shape, BF),
            scratch(dw_kernel.shape[1], dw_kernel.shape[0], LANES),
            scratch(*ln_gain.shape),
            scratch(*w_in.shape, dtype=BF),
            scratch(*w_out.shape, dtype=BF),
            scratch(*layer_scale.shape),
            scratch(count, LANES, dtype=BF),
            pltpu.SemaphoreType.DMA((7,)),
        ],
        compiler_params=pltpu.CompilerParams(vmem_limit_bytes=20 << 20),
    )(
        top,
        tile,
        west,
        east,
        south,
        north,
        stem,
        taps,
        ln_gain,
        w_in,
        w_out,
        layer_scale,
        upstream[0],
    )

    def rest(top):
        return pl.pallas_call(
            rest_kernel,
            out_shape=jax.ShapeDtypeStruct((SMALL, LANES), BF),
            in_specs=[smem()] + vmem(8),
            out_specs=vmem(1)[0],
            scratch_shapes=[
                scratch(SMALL, LANES),
                scratch(EH, EW, LANES),
                scratch(RH, RW, LANES),
                scratch(RH, EW + 8, LANES),
                scratch(TH, EW, LANES),
                scratch(49, 8, LANES),
                scratch(49, 8, LANES),
                scratch(EH, EW, LANES),
                scratch(49, 8, LANES),
                scratch(49, 8, LANES),
                scratch(49, 8, LANES),
            ],
            compiler_params=pltpu.CompilerParams(vmem_limit_bytes=10 << 20),
            cost_estimate=pl.CostEstimate(flops=10_000_000_000, bytes_accessed=4_000_000, transcendentals=0),
        )(top, taps, *ring)

    pieces, mine, other, order = summed_pieces(packed, top, rest)
    shapes = [array.shape for array in (stem, dw_kernel, ln_gain, w_in, w_out, layer_scale)]
    shapes[1] = (shapes[1][1], shapes[1][0], shapes[1][2])
    grads = pl.pallas_call(
        unpack_kernel,
        out_shape=[jax.ShapeDtypeStruct(shape, F32) for shape in shapes],
        in_specs=[smem()] + vmem(3),
        out_specs=vmem(6),
        scratch_shapes=[scratch(BULK, LANES), scratch(SMALL, LANES)],
        compiler_params=pltpu.CompilerParams(vmem_limit_bytes=8 << 20),
    )(order, pieces, mine, other)
    grads = list(grads)
    grads[1] = grads[1].transpose(1, 0, 2)
    return (result[None], *grads)


def solution(mesh):
    in_specs = (
        P(("groups", "gy"), None, None),
        P(("groups", "gy"), None),
        P(),
        P(),
        P(),
        P(),
        P(),
        P(),
        P(("groups", "gy"), None, None),
    )
    out_specs = (
        P(("groups", "gy"), None, None),
        P("groups", None),
        P("groups", None, None),
        P("groups", None),
        P("groups", None, None),
        P("groups", None, None),
        P("groups", None),
    )
    return jax.shard_map(shards, mesh=mesh, in_specs=in_specs, out_specs=out_specs, check_vma=False)
```

```python
import functools
import math

import jax
import jax.numpy as jnp
from jax import lax
from jax.experimental import pallas as pl
from jax.experimental.pallas import tpu as pltpu
from jax.sharding import PartitionSpec as P

TH = 16
TW = 32
TX = 8
LANES = 128

RIM = 6
PADC = 8
EH, EW = TH + 2 * RIM, TW + 2 * PADC
RH, RW = TH + 6, 40
RING_COL = 5
MID, MID_ROWS = 6, 10

C0 = 0.7978845608028654
C1 = 0.7978845608028654 * 0.044715
NORM_STABILIZER = 1e-06

WIN_ROW, WOUT_ROW, BULK = 0, 1024, 2048
STEM_AT, KERNEL_AT, GAIN_AT, SCALE_AT = 0, (75, 124), 173, 175
SMALL = 192

STEPS = (3, 2, 1)

BF = jnp.bfloat16
F32 = jnp.float32


def vmem(count):
    return [pl.BlockSpec(memory_space=pltpu.VMEM)] * count


def smem():
    return pl.BlockSpec(memory_space=pltpu.SMEM)


def contract_rows(left, right):
    return lax.dot_general(left, right, (((0,), (0,)), ((), ())), preferred_element_type=F32)


def contract_cols(left, right):
    return lax.dot_general(left, right, (((1,), (1,)), ((), ())), preferred_element_type=F32)


def prepare_kernel(levels_hbm, ocean_hbm, tile_ref, west_ref, east_ref, fold_ref, stage, levels_ref, ocean_ref, arrived):
    count, cells = levels_ref.shape
    loads = [
        pltpu.make_async_copy(levels_hbm, levels_ref, arrived.at[0]),
        pltpu.make_async_copy(ocean_hbm, ocean_ref, arrived.at[1]),
    ]
    for load in loads:
        load.start()
    stage[...] = jnp.zeros_like(stage)
    for load in loads:
        load.wait()
    stage[0:count, :] = levels_ref[...].astype(F32)
    stage[count : count + 1, :] = ocean_ref[...].astype(F32)
    rows = lax.broadcasted_iota(jnp.int32, (LANES, LANES), 0)
    cols = lax.broadcasted_iota(jnp.int32, (LANES, LANES), 1)
    eye = (rows == cols).astype(BF)
    turned = contract_rows(stage[...].astype(BF), eye)
    side = RIM * TW
    rows = lax.broadcasted_iota(jnp.int32, (side, side), 0)
    cols = lax.broadcasted_iota(jnp.int32, (side, side), 1)
    swap = (rows + cols == side - 1).astype(BF)
    fold = jnp.dot(swap, turned[cells - side :].astype(BF), preferred_element_type=F32).reshape(RIM, TW, LANES)
    tile = turned.reshape(TH, TW, LANES)
    tile_ref[...] = tile.astype(BF)
    fold_ref[...] = fold.astype(BF)
    west_ref[0:TH] = tile[:, 0:PADC].astype(BF)
    west_ref[TH:] = fold[:, TW - PADC :].astype(BF)
    east_ref[0:TH] = tile[:, TW - PADC :].astype(BF)
    east_ref[TH:] = fold[:, 0:PADC].astype(BF)


def load_column(ref, row, start):
    return ref[row, pl.ds(start, 8), :]


def conv_block(ref, taps, start, out_rows, in_rows, taps_of):
    totals = {o: None for o in out_rows}
    needed = sorted({o + a for o in out_rows for a in range(7) if o + a in in_rows})
    for d in range(7):
        column = {r: load_column(ref, r - in_rows.start, start + d) for r in needed}
        for a in range(7):
            held = {}
            for o in out_rows:
                r = o + a
                if r not in column:
                    continue
                which, index = taps_of(o, r, a, d)
                if (which, index) not in held:
                    held[(which, index)] = taps[which][index]
                term = held[(which, index)] * column[r]
                totals[o] = term if totals[o] is None else totals[o] + term
    return totals


def chunks(spans, body):
    def run(carry):
        for at in spans:
            carry = body(at.start // (at.stop - at.start), at, carry)
        return carry

    return run


def spans_of(count, size):
    return [slice(at, at + size) for at in range(0, count, size)]


def norm_rows(conv, xhat, rinv, normed, gain, spans):
    for at in spans:
        values = conv[at, :]
        average = jnp.mean(values, axis=-1, keepdims=True)
        centered = values - average
        inverse = lax.rsqrt(jnp.mean(centered * centered, axis=-1, keepdims=True) + NORM_STABILIZER)
        scaled = centered * inverse
        xhat[at, :] = scaled
        rinv[at, :] = jnp.broadcast_to(inverse, values.shape)
        normed[at, :] = (scaled * gain).astype(BF)


def gelu_rows(pre, act, slope, spans):
    for at in spans:
        for start in range(at.start, at.stop, 16):
            here = slice(start, start + 16)
            v = pre[here, :]
            square = v * v
            inner = v * (C0 + C1 * square)
            half = 0.5 * jnp.tanh(inner) + 0.5
            active = v * half
            act[here, :] = active.astype(BF)
            slope[here, :] = half + active * (1.0 - half) * (2.0 * C0 + (6.0 * C1) * square)


def joint_weights(stem_ref, weights):
    count = stem_ref.shape[0]
    weights[...] = jnp.zeros_like(weights)
    weights[0:count, 0:LANES] = stem_ref[...].astype(F32)
    weights[count : count + 1, LANES:] = jnp.ones((1, LANES), F32)
    return weights[...].astype(BF)


def middle_kernel(
    tile_ref,
    west_ref,
    east_ref,
    table_ref,
    stem_ref,
    win_ref,
    wout_ref,
    flat,
    xhat,
    rinv,
    normed,
    act,
    slope,
    branch,
    ext,
    x0,
    m6,
    weights,
    taps,
    conv,
    wide,
):
    joint = joint_weights(stem_ref, weights)
    spread_taps(table_ref, 0, taps)
    ext[:, 0:PADC] = west_ref[0:TH].astype(F32)
    ext[:, PADC : PADC + TW] = tile_ref[...].astype(F32)
    ext[:, PADC + TW :] = east_ref[0:TH].astype(F32)
    for row in range(0, TH, 4):
        at = slice(row, row + 4)
        both = jnp.dot(ext[at].reshape(4 * EW, LANES).astype(BF), joint, preferred_element_type=F32)
        mask = both[:, LANES:]
        m6[at] = mask.reshape(4, EW, LANES)
        x0[at] = (mask * both[:, :LANES]).astype(BF).astype(F32).reshape(4, EW, LANES)

    def conv_columns(block, _):
        start = pl.multiple_of(block * 8, 8)
        rows = range(MID, MID + MID_ROWS)
        totals = conv_block(x0, (taps,), start + 2, rows, range(RIM, RIM + TH), lambda o, r, a, d: (0, a * 7 + d))
        for o in rows:
            conv[pl.ds(pl.multiple_of((o - MID) * RW + start, 8), 8), :] = totals[o]
        return 0

    lax.fori_loop(0, RW // 8, conv_columns, 0)
    count = MID_ROWS * RW
    spans = spans_of(count, 2 * RW)
    norm_rows(conv, xhat, rinv, normed, table_ref[49, 0:1, :], spans)
    wide[...] = jnp.dot(normed[...], win_ref[0], preferred_element_type=F32)
    gelu_rows(wide, act, slope, spans)
    branch[...] = jnp.dot(act[...], wout_ref[0], preferred_element_type=F32)
    for index, at in enumerate(spans):
        rows = slice(index * 2 + MID + 3 - RIM, index * 2 + MID + 5 - RIM)
        mask = m6[rows, RING_COL : RING_COL + RW, :]
        held = x0[rows, RING_COL : RING_COL + RW, :]
        value = mask * (held + table_ref[50, 0:1, :] * branch[at, :].reshape(2, RW, LANES))
        flat[at, :] = value.reshape(2 * RW, LANES).astype(BF)


def spread_taps(dw_ref, layer, taps, top=None):
    for t in range(49):
        row = dw_ref[t, layer : layer + 1, :]
        if top is not None:
            row = jnp.where(top, dw_ref[48 - t, layer : layer + 1, :], row)
        taps[t] = jnp.broadcast_to(row, (8, LANES))


def padded(flat, pad, width):
    rows = flat.shape[0] // width
    pad[:, 0:PADC, :] = jnp.zeros((rows, PADC, LANES), F32)
    pad[:, PADC + width :, :] = jnp.zeros((rows, pad.shape[1] - PADC - width, LANES), F32)
    for row in range(0, rows, 2):
        value = flat[row * width : (row + 2) * width, :].astype(F32)
        pad[row : row + 2, PADC : PADC + width, :] = value.reshape(2, width, LANES)


def main_kernel(
    rescale,
    top_ref,
    tile_ref,
    west_ref,
    east_ref,
    south_ref,
    north_ref,
    table_ref,
    stem_ref,
    win_ref,
    wout_ref,
    up_ref,
    mid_flat,
    mid_xhat,
    mid_rinv,
    mid_normed,
    mid_act,
    mid_slope,
    mid_branch,
    out_ref,
    packed_ref,
    sums,
    cells,
    flat0,
    flat1,
    grad0,
    grad1,
    carry0,
    x0,
    m6,
    x1,
    taps0,
    taps0n,
    pad1,
    g1,
    ext,
    weights,
    taps1,
    conv0,
    xhat0,
    rinv0,
    branch0,
    normed0,
    act0,
    slope0,
    conv1,
    xhat1,
    rinv1,
    branch1,
    normed1,
    act1,
    slope1,
    wide,
    thin,
    gpre,
):
    top = top_ref[0] == 1
    count0, count1 = RH * RW, TH * TW
    all0, all1 = spans_of(count0, 2 * RW), spans_of(count1, 2 * TW)
    middle = slice(MID * RW, (MID + MID_ROWS) * RW)
    rims = [slice(0, middle.start), slice(middle.stop, count0)]
    rim0 = [at for at in all0 if at.stop <= middle.start or at.start >= middle.stop]

    def from_middle(at):
        return middle.start <= at.start < middle.stop

    def pick(mid, ref, at):
        if from_middle(at):
            return mid[at.start - middle.start : at.stop - middle.start, :]
        return ref[at, :]

    ext[0:RIM] = south_ref[...].astype(F32)
    ext[RIM : RIM + TH, PADC : PADC + TW] = tile_ref[...].astype(F32)
    ext[RIM : RIM + TH, 0:PADC] = west_ref[0:TH].astype(F32)
    ext[RIM : RIM + TH, PADC + TW :] = east_ref[0:TH].astype(F32)
    ext[RIM + TH :] = north_ref[...].astype(F32)

    joint = joint_weights(stem_ref, weights)

    for index in range(EH // 4):
        at = slice(index * 4, index * 4 + 4)
        here = ext[at].reshape(4 * EW, LANES).astype(BF)
        cells[index * 4 * EW : (index + 1) * 4 * EW, :] = here
        both = jnp.dot(here, joint, preferred_element_type=F32)
        mask = both[:, LANES:]
        m6[at] = mask.reshape(4, EW, LANES)
        value = (mask * both[:, :LANES]).astype(BF)
        flat0[index * 4 * EW : (index + 1) * 4 * EW, :] = value
        x0[at] = value.astype(F32).reshape(4, EW, LANES)

    spread_taps(table_ref, 0, taps0)
    spread_taps(table_ref, 0, taps0n, top)
    spread_taps(table_ref, 1, taps1)

    north_at = 3 + TH

    def conv0_block(block, _):
        start = pl.multiple_of(block * 8, 8)
        for rows in (range(0, MID), range(MID + MID_ROWS, north_at), range(north_at, RH)):
            totals = conv_block(
                x0,
                (taps0, taps0n),
                start + 2,
                rows,
                range(0, EH),
                lambda o, r, a, d: (1 if o >= north_at else 0, a * 7 + d),
            )
            for o in rows:
                conv0[pl.ds(pl.multiple_of(o * RW + start, 8), 8), :] = totals[o]
        return 0

    lax.fori_loop(0, RW // 8, conv0_block, 0)

    norm_rows(conv0, xhat0, rinv0, normed0, table_ref[49, 0:1, :], rim0)
    normed0[middle] = mid_normed[...]
    act0[middle] = mid_act[...]
    for at in rims:
        wide[at] = jnp.dot(normed0[at], win_ref[0], preferred_element_type=F32)
    gelu_rows(wide, act0, slope0, rim0)
    for at in rims:
        branch0[at] = jnp.dot(act0[at], wout_ref[0], preferred_element_type=F32)

    flat1[middle] = mid_flat[...]
    for index, at in enumerate(all0):
        if not from_middle(at):
            rows = slice(index * 2 + 3, index * 2 + 5)
            mask = m6[rows, RING_COL : RING_COL + RW, :]
            held = x0[rows, RING_COL : RING_COL + RW, :]
            value = mask * (held + table_ref[50, 0:1, :] * branch0[at, :].reshape(2, RW, LANES))
            flat1[at, :] = value.reshape(2 * RW, LANES).astype(BF)
        x1[index * 2 : index * 2 + 2] = flat1[at, :].astype(F32).reshape(2, RW, LANES)

    def conv1_block(block, _):
        start = pl.multiple_of(block * 8, 8)
        for rows in (range(0, 16),):
            totals = conv_block(
                x1, (taps1,), start, rows, range(0, RH), lambda o, r, a, d: (0, a * 7 + d)
            )
            for o in rows:
                conv1[pl.ds(pl.multiple_of(o * TW + start, 8), 8), :] = totals[o]
        return 0

    lax.fori_loop(0, TW // 8, conv1_block, 0)
    norm_rows(conv1, xhat1, rinv1, normed1, table_ref[49, 1:2, :], all1)
    wide[0:count1] = jnp.dot(normed1[...], win_ref[1], preferred_element_type=F32)
    gelu_rows(wide, act1, slope1, all1)
    branch1[...] = jnp.dot(act1[...], wout_ref[1], preferred_element_type=F32)

    sums[...] = jnp.zeros_like(sums)
    g1[...] = jnp.zeros_like(g1)

    def folded(value):
        return jnp.sum(value.reshape(-1, 8, LANES), axis=0)

    def next1(index, at, total):
        rows = 2
        mask = m6[pl.ds(index * rows + RIM, rows), PADC : PADC + TW, :]
        held = x1[pl.ds(index * rows + 3, rows), 3 : 3 + TW, :]
        branch = branch1[at, :].reshape(rows, TW, LANES)
        out_ref[at, :] = (mask * (held + table_ref[50, 1:2, :] * branch)).astype(BF).reshape(rows * TW, LANES)
        masked = mask * (up_ref[at, :].astype(F32) * rescale).reshape(rows, TW, LANES)
        g1[pl.ds(index * rows + 3, rows), 3 : 3 + TW, :] = masked
        thin[at, :] = (masked * table_ref[50, 1:2, :]).reshape(rows * TW, LANES).astype(BF)
        return total + folded(masked * branch)

    total = chunks(all1, next1)(jnp.zeros((8, LANES), F32))
    sums[3:4, :] = jnp.sum(total, axis=0, keepdims=True)

    def grad_wout(layer, count, act):
        packed_ref[WOUT_ROW + 512 * layer : WOUT_ROW + 512 * layer + 512, :] = contract_rows(
            act[...], thin[0:count]
        ).astype(BF)

    def grad_pre(layer, count, slope):
        wide[0:count] = contract_cols(thin[0:count], wout_ref[layer])

        for at in spans_of(count, 16):
            gpre[at, :] = (wide[at, :] * slope(at)).astype(BF)

    def grad_win(layer, count, normed):
        gp = gpre[0:count]
        grad_in = contract_rows(normed[...], gp).astype(BF)
        for part in range(4):
            at = WIN_ROW + 512 * layer + 128 * part
            packed_ref[at : at + 128, :] = grad_in[:, 128 * part : 128 * part + 128]
        wide[0:count, 0:LANES] = contract_cols(gp, win_ref[layer])

    def grad_conv(layer, count, size, xhat, rinv, grad):
        gain = table_ref[49, layer : layer + 1, :]

        def step(index, at, total):
            gn = wide[at, 0:LANES]
            scaled = xhat(at)
            gx = gn * gain
            first = jnp.mean(gx, axis=-1, keepdims=True)
            second = jnp.mean(gx * scaled, axis=-1, keepdims=True)
            grad[at, :] = (rinv(at) * (gx - first - scaled * second)).astype(BF)
            return total + folded(gn * scaled)

        total = chunks(spans_of(count, size), step)(jnp.zeros((8, LANES), F32))
        sums[layer : layer + 1, :] = jnp.sum(total, axis=0, keepdims=True)

    grad_wout(1, count1, act1)
    grad_pre(1, count1, lambda at: slope1[at, :])
    grad_win(1, count1, normed1)
    grad_conv(1, count1, 2 * TW, lambda at: xhat1[at, :], lambda at: rinv1[at, :], grad1)
    padded(grad1, pad1, TW)

    def back1_block(block, _):
        start = pl.multiple_of(block * 8, 8)
        for rows in (range(0, 22),):
            totals = conv_block(
                pad1, (taps1,), start + 2, rows, range(6, 6 + TH), lambda o, r, a, d: (0, 48 - (a * 7 + d))
            )
            for o in rows:
                g1[o, pl.ds(start, 8), :] += totals[o]
        return 0

    lax.fori_loop(0, RW // 8, back1_block, 0)

    def masked0(index, at, total):
        rows = pl.ds(index * 2, 2)
        masked = m6[pl.ds(index * 2 + 3, 2), RING_COL : RING_COL + RW, :] * g1[rows]
        flat = masked.reshape(2 * RW, LANES)
        carry0[at, :] = flat
        thin[at, :] = (flat * table_ref[50, 0:1, :]).astype(BF)
        return total + folded(flat * pick(mid_branch, branch0, at))

    total = chunks(all0, masked0)(jnp.zeros((8, LANES), F32))
    sums[2:3, :] = jnp.sum(total, axis=0, keepdims=True)
    grad_wout(0, count0, act0)
    grad_pre(0, count0, lambda at: pick(mid_slope, slope0, at))
    grad_win(0, count0, normed0)
    grad_conv(
        0,
        count0,
        2 * RW,
        lambda at: pick(mid_xhat, xhat0, at),
        lambda at: pick(mid_rinv, rinv0, at),
        grad0,
    )


def taps1_kernel(flat1, grad1, gk1, x1, pad1):
    for row in range(0, RH, 2):
        x1[row : row + 2] = flat1[row * RW : (row + 2) * RW, :].astype(F32).reshape(2, RW, LANES)
    padded(grad1, pad1, TW)
    gk1[...] = jnp.zeros_like(gk1)

    def kernel1_block(block, _):
        start = pl.multiple_of(block * 8, 8)
        grads = [pad1[j, pl.ds(start + PADC, 8), :] for j in range(TH)]
        for d in range(7):
            column = [load_column(x1, r, start + d) for r in range(RH)]
            for a in range(7):
                total = gk1[a * 7 + d]
                for j in range(TH):
                    total = total + grads[j] * column[j + a]
                gk1[a * 7 + d] = total
        return 0

    lax.fori_loop(0, TW // 8, kernel1_block, 0)


def rest_kernel(
    top_ref,
    dw_ref,
    sums,
    cells,
    flat0,
    grad0,
    carry0,
    gk1,
    small_ref,
    small,
    x0,
    pad0,
    taps0,
    taps0n,
    h0,
    gk0,
    gk0n,
):
    top = top_ref[0] == 1
    north_at = 3 + TH
    levels_count = KERNEL_AT[0] - STEM_AT

    for row in range(0, EH, 4):
        x0[row : row + 4] = flat0[row * EW : (row + 4) * EW, :].astype(F32).reshape(4, EW, LANES)
    padded(grad0, pad0, RW)
    spread_taps(dw_ref, 0, taps0)
    spread_taps(dw_ref, 0, taps0n, top)

    gk0[...] = jnp.zeros_like(gk0)
    gk0n[...] = jnp.zeros_like(gk0n)

    def kernel0_block(block, _):
        start = pl.multiple_of(block * 8, 8)
        grads = [pad0[j, pl.ds(start + PADC, 8), :] for j in range(RH)]
        for d in range(7):
            column = [load_column(x0, r, start + 2 + d) for r in range(EH)]
            for a in range(7):
                total = gk0[a * 7 + d]
                for j in range(north_at):
                    total = total + grads[j] * column[j + a]
                gk0[a * 7 + d] = total
                total = gk0n[a * 7 + d]
                for j in range(north_at, RH):
                    total = total + grads[j] * column[j + a]
                gk0n[a * 7 + d] = total
        return 0

    lax.fori_loop(0, RW // 8, kernel0_block, 0)
    for t in range(49):
        north = jnp.where(top, gk0n[48 - t], gk0n[t])
        small[KERNEL_AT[0] + t : KERNEL_AT[0] + t + 1, :] = jnp.sum(gk0[t] + north, axis=0, keepdims=True)
        small[KERNEL_AT[1] + t : KERNEL_AT[1] + t + 1, :] = jnp.sum(gk1[t], axis=0, keepdims=True)

    def back0_block(block, _):
        start = pl.multiple_of(block * 8, 8)
        for rows in (range(0, 14), range(14, 28)):
            totals = conv_block(
                pad0,
                (taps0, taps0n),
                start,
                rows,
                range(6, 6 + RH),
                lambda o, r, a, d: (1 if r - 6 >= north_at else 0, 48 - (a * 7 + d)),
            )
            for o in rows:
                h0[o, pl.ds(start, 8), :] = totals[o]
        return 0

    lax.fori_loop(0, EW // 8, back0_block, 0)
    for row in range(0, RH, 2):
        h0[row + 3 : row + 5, RING_COL : RING_COL + RW, :] += carry0[
            row * RW : (row + 2) * RW, :
        ].reshape(2, RW, LANES)
    rows = lax.broadcasted_iota(jnp.int32, (LANES, LANES), 0)
    mask = jnp.dot(cells[...], (rows == levels_count).astype(BF), preferred_element_type=F32)
    stem_side = (mask * h0[...].reshape(EH * EW, LANES)).astype(BF)
    stem_grad = contract_rows(cells[...], stem_side)
    small[STEM_AT : KERNEL_AT[0], :] = stem_grad[0:levels_count, :]
    small[GAIN_AT : GAIN_AT + 4, :] = sums[0:4, :]
    small[GAIN_AT + 4 :, :] = jnp.zeros((SMALL - GAIN_AT - 4, LANES), F32)
    small_ref[...] = small[...].astype(BF)


def unpack_kernel(
    order_ref,
    pieces_ref,
    mine_ref,
    other_ref,
    stem_out,
    kernel_out,
    gain_out,
    win_out,
    wout_out,
    scale_out,
    stem_ref,
    kernel_ref,
    gain_ref,
    win_ref,
    wout_ref,
    scale_ref,
    small,
    sent,
):
    count, size = pieces_ref.shape[0], pieces_ref.shape[1]
    stores = [
        pltpu.make_async_copy(source, target, sent.at[index])
        for index, (source, target) in enumerate(
            [(win_ref.at[layer], win_out.at[layer]) for layer in range(2)]
            + [(wout_ref.at[layer], wout_out.at[layer]) for layer in range(2)]
            + [(stem_ref, stem_out), (kernel_ref, kernel_out), (gain_ref, gain_out), (scale_ref, scale_out)]
        )
    ]

    def rows(at, length):
        return [
            pieces_ref[order_ref[index]].astype(F32) if count > 1 else pieces_ref[0, index * 128 : index * 128 + 128].astype(F32)
            for index in range(at // 128, (at + length) // 128)
        ]

    for layer in range(2):
        for part, block in enumerate(rows(WIN_ROW + 512 * layer, 512)):
            win_ref[layer, :, 128 * part : 128 * part + 128] = block
        stores[layer].start()
    for layer in range(2):
        for part, block in enumerate(rows(WOUT_ROW + 512 * layer, 512)):
            wout_ref[layer, 128 * part : 128 * part + 128, :] = block
        stores[2 + layer].start()
    places, size = mine_ref.shape[0], mine_ref.shape[1]
    for index in range(places):
        at = order_ref[count + index]
        small[index * size : (index + 1) * size, :] = mine_ref[at].astype(F32) + other_ref[at].astype(F32)
    for layer in range(2):
        kernel_ref[:, layer, :] = small[KERNEL_AT[layer] : KERNEL_AT[layer] + 49, :]
    stem_ref[...] = small[STEM_AT : STEM_AT + stem_ref.shape[0], :]
    gain_ref[...] = small[GAIN_AT : GAIN_AT + 2, :]
    scale_ref[...] = small[SCALE_AT : SCALE_AT + 2, :]
    for store in stores[4:]:
        store.start()
    for store in stores:
        store.wait()


def permuted(value, pairs):
    return lax.ppermute(value, "gy", pairs)


def crossed(value, bits):
    return permuted(value, [(i, i ^ bits) for i in range(lax.axis_size("gy"))])


def summed_pieces(packed, top, rest):
    size = lax.axis_size("gy")
    if size != 16:
        bulk, small = lax.psum((packed.astype(F32), rest(top).astype(F32)), "gy")
        small = small.astype(BF)[None]
        return bulk.astype(BF)[None], small, jnp.zeros_like(small), jnp.zeros((2,), jnp.int32)
    me = lax.axis_index("gy")
    core, side, deep = me & 1, (me >> 1) & 1, me >> 2

    def halves(value, bit):
        half = value.shape[0] // 2
        low, high = value[:half], value[half:]
        return jnp.where(bit == 0, low, high), jnp.where(bit == 0, high, low)

    keep, send = halves(packed, core)
    came = crossed(send, 1)
    came, top = lax.optimization_barrier((came, top))
    small = rest(top)
    keep, send = halves(keep.astype(F32) + came.astype(F32), side)
    total = keep + crossed(send.astype(BF), 2).astype(F32)
    quarter = total.shape[0] // 4
    part = small.shape[0] // 4

    def shard(step):
        at = deep ^ step
        return jnp.concatenate(
            [
                lax.dynamic_slice_in_dim(total, at * quarter, quarter, 0).astype(BF),
                lax.dynamic_slice_in_dim(small, at * part, part, 0),
            ],
            axis=0,
        )

    arrived = [crossed(shard(step), 4 * step) for step in STEPS]
    bulk = lax.dynamic_slice_in_dim(total, deep * quarter, quarter, 0)
    rest_sum = lax.dynamic_slice_in_dim(small, deep * part, part, 0).astype(F32)
    for other in arrived:
        bulk = bulk + other[:quarter].astype(F32)
        rest_sum = rest_sum + other[quarter:].astype(F32)
    mine = jnp.concatenate([bulk.astype(BF), rest_sum.astype(BF)], axis=0)
    pieces = jnp.stack([mine] + [crossed(mine, 4 * step) for step in STEPS][::-1])
    came = crossed(pieces, 2)
    bulk = jnp.concatenate([pieces[:, :quarter], came[:, :quarter]], axis=0)
    small = (pieces[:, quarter:].astype(F32) + came[:, quarter:].astype(F32)).astype(BF)
    rows = bulk.shape[0] * quarter
    joined = jnp.concatenate([bulk.reshape(rows, LANES), small.reshape(4 * part, LANES)], axis=0)
    came = crossed(joined, 1)
    bulk = jnp.concatenate([bulk, came[:rows].reshape(bulk.shape)], axis=0)
    mixed = ((core << 3) | (side << 2) | deep).astype(jnp.int32)
    order = jnp.arange(20, dtype=jnp.int32) & 15
    order = order ^ jnp.where(jnp.arange(20) < 16, mixed, deep.astype(jnp.int32))
    return bulk, small, came[rows:].reshape(small.shape), order


def shards(levels, ocean, stem, dw_kernel, ln_gain, w_in, w_out, layer_scale, upstream):
    size = lax.axis_size("gy")
    rows = size // TX
    me = lax.axis_index("gy")
    is_top = me // TX == rows - 1
    count = levels.shape[2]
    top = is_top.astype(jnp.int32)[None]
    table = jnp.concatenate([dw_kernel.transpose(1, 0, 2), ln_gain[None], layer_scale[None]])
    tile, to_west, to_east, folded = pl.pallas_call(
        prepare_kernel,
        out_shape=[
            jax.ShapeDtypeStruct((TH, TW, LANES), BF),
            jax.ShapeDtypeStruct((TH + RIM, PADC, LANES), BF),
            jax.ShapeDtypeStruct((TH + RIM, PADC, LANES), BF),
            jax.ShapeDtypeStruct((RIM, TW, LANES), BF),
        ],
        in_specs=[pl.BlockSpec(memory_space=pltpu.HBM)] * 2,
        out_specs=vmem(4),
        scratch_shapes=[
            pltpu.VMEM((LANES, count), F32),
            pltpu.VMEM(levels.shape[1:], BF),
            pltpu.VMEM(ocean.shape, jnp.int32),
            pltpu.SemaphoreType.DMA((2,)),
        ],
        compiler_params=pltpu.CompilerParams(vmem_limit_bytes=4 << 20),
    )(levels[0], ocean)

    def column_pairs(step):
        return [(i, i // TX * TX + (i % TX + step) % TX) for i in range(size)]

    west = permuted(to_east, column_pairs(1))
    east = permuted(to_west, column_pairs(-1))

    def wide_rows(at):
        return jnp.concatenate([west[at], tile[at], east[at]], axis=1)

    lower, upper = wide_rows(slice(0, RIM)), wide_rows(slice(TH - RIM, TH))
    folded = jnp.concatenate([east[TH:], folded, west[TH:]], axis=1)
    folded = permuted(folded, [(i, i // TX * TX + TX - 1 - i % TX) for i in range(size - TX, size)])
    if rows == 2:
        north = permuted(jnp.where(is_top, lower, upper), [(i, (i + TX) % size) for i in range(size)])
        south = jnp.where(is_top, north, jnp.zeros_like(north))
    else:
        south = permuted(upper, [(i, i + TX) for i in range(size - TX)])
        north = permuted(lower, [(i + TX, i) for i in range(size - TX)])
    north = jnp.where(is_top, folded, north)

    def scratch(*shape, dtype=F32):
        return pltpu.VMEM(shape, dtype)

    count0 = RH * RW
    hidden = w_in.shape[2]
    count_mid = MID_ROWS * RW
    mid_shapes = [
        jax.ShapeDtypeStruct((count_mid, LANES), BF),
        jax.ShapeDtypeStruct((count_mid, LANES), F32),
        jax.ShapeDtypeStruct((count_mid, LANES), F32),
        jax.ShapeDtypeStruct((count_mid, LANES), BF),
        jax.ShapeDtypeStruct((count_mid, hidden), BF),
        jax.ShapeDtypeStruct((count_mid, hidden), F32),
        jax.ShapeDtypeStruct((count_mid, LANES), F32),
    ]
    middle = pl.pallas_call(
        middle_kernel,
        out_shape=mid_shapes,
        in_specs=vmem(7),
        out_specs=vmem(7),
        scratch_shapes=[
            scratch(TH, EW, LANES),
            scratch(TH, EW, LANES),
            scratch(TH, EW, LANES),
            scratch(LANES, 2 * LANES),
            scratch(49, 8, LANES),
            scratch(count_mid, LANES),
            scratch(count_mid, hidden),
        ],
        compiler_params=pltpu.CompilerParams(vmem_limit_bytes=10 << 20),
        cost_estimate=pl.CostEstimate(flops=4_000_000_000, bytes_accessed=3_000_000, transcendentals=0),
    )(tile, west, east, table, stem, w_in, w_out)

    ring_shapes = [
        jax.ShapeDtypeStruct((8, LANES), F32),
        jax.ShapeDtypeStruct((EH * EW, LANES), BF),
        jax.ShapeDtypeStruct((EH * EW, LANES), BF),
        jax.ShapeDtypeStruct((RH * RW, LANES), BF),
        jax.ShapeDtypeStruct((RH * RW, LANES), BF),
        jax.ShapeDtypeStruct((TH * TW, LANES), BF),
        jax.ShapeDtypeStruct((RH * RW, LANES), F32),
    ]
    result, packed, *ring = pl.pallas_call(
        functools.partial(main_kernel, 1.0 / math.sqrt(size * count)),
        out_shape=[
            jax.ShapeDtypeStruct((count, LANES), BF),
            jax.ShapeDtypeStruct((BULK, LANES), BF),
        ]
        + ring_shapes,
        in_specs=[smem()] + vmem(17),
        out_specs=vmem(9),
        scratch_shapes=[
            scratch(EH, EW, LANES),
            scratch(EH, EW, LANES),
            scratch(RH, RW, LANES),
            scratch(49, 8, LANES),
            scratch(49, 8, LANES),
            scratch(TH, EW, LANES),
            scratch(RH, RW, LANES),
            scratch(EH, EW, LANES),
            scratch(LANES, 2 * LANES),
            scratch(49, 8, LANES),
            scratch(count0, LANES),
            scratch(count0, LANES),
            scratch(count0, LANES),
            scratch(count0, LANES),
            scratch(count0, LANES, dtype=BF),
            scratch(count0, hidden, dtype=BF),
            scratch(count0, hidden),
            scratch(count, LANES),
            scratch(count, LANES),
            scratch(count, LANES),
            scratch(count, LANES),
            scratch(count, LANES, dtype=BF),
            scratch(count, hidden, dtype=BF),
            scratch(count, hidden),
            scratch(count0, hidden),
            scratch(count0, LANES, dtype=BF),
            scratch(count0, hidden, dtype=BF),
        ],
        compiler_params=pltpu.CompilerParams(vmem_limit_bytes=20 << 20),
    )(
        top,
        tile,
        west,
        east,
        south,
        north,
        table,
        stem,
        w_in,
        w_out,
        upstream[0],
        *middle,
    )

    sums, cells, flat0, flat1, grad0, grad1, carry0 = ring
    grad_taps1 = pl.pallas_call(
        taps1_kernel,
        out_shape=jax.ShapeDtypeStruct((49, 8, LANES), F32),
        in_specs=vmem(2),
        out_specs=vmem(1)[0],
        scratch_shapes=[scratch(RH, RW, LANES), scratch(TH, EW, LANES)],
        compiler_params=pltpu.CompilerParams(vmem_limit_bytes=6 << 20),
        cost_estimate=pl.CostEstimate(flops=2_000_000_000, bytes_accessed=500_000, transcendentals=0),
    )(flat1, grad1)

    def rest(top):
        return pl.pallas_call(
            rest_kernel,
            out_shape=jax.ShapeDtypeStruct((SMALL, LANES), BF),
            in_specs=[smem()] + vmem(7),
            out_specs=vmem(1)[0],
            scratch_shapes=[
                scratch(SMALL, LANES),
                scratch(EH, EW, LANES),
                scratch(RH, EW + 8, LANES),
                scratch(49, 8, LANES),
                scratch(49, 8, LANES),
                scratch(EH, EW, LANES),
                scratch(49, 8, LANES),
                scratch(49, 8, LANES),
            ],
            compiler_params=pltpu.CompilerParams(vmem_limit_bytes=10 << 20),
            cost_estimate=pl.CostEstimate(flops=10_000_000_000, bytes_accessed=4_000_000, transcendentals=0),
        )(top, table, sums, cells, flat0, grad0, carry0, grad_taps1)

    pieces, mine, other, order = summed_pieces(packed, top, rest)
    shapes = [array.shape for array in (stem, dw_kernel, ln_gain, w_in, w_out, layer_scale)]
    shapes[1] = (shapes[1][1], shapes[1][0], shapes[1][2])
    grads = pl.pallas_call(
        unpack_kernel,
        out_shape=[jax.ShapeDtypeStruct(shape, F32) for shape in shapes],
        in_specs=[smem()] + vmem(3),
        out_specs=[pl.BlockSpec(memory_space=pltpu.HBM)] * 6,
        scratch_shapes=[scratch(*shape) for shape in shapes]
        + [scratch(SMALL, LANES), pltpu.SemaphoreType.DMA((8,))],
        compiler_params=pltpu.CompilerParams(vmem_limit_bytes=8 << 20),
    )(order, pieces, mine, other)
    grads = list(grads)
    grads[1] = grads[1].transpose(1, 0, 2)
    return (result[None], *grads)


def solution(mesh):
    in_specs = (
        P(("groups", "gy"), None, None),
        P(("groups", "gy"), None),
        P(),
        P(),
        P(),
        P(),
        P(),
        P(),
        P(("groups", "gy"), None, None),
    )
    out_specs = (
        P(("groups", "gy"), None, None),
        P("groups", None),
        P("groups", None, None),
        P("groups", None),
        P("groups", None, None),
        P("groups", None, None),
        P("groups", None),
    )
    return jax.shard_map(shards, mesh=mesh, in_specs=in_specs, out_specs=out_specs, check_vma=False)
```

```python
import functools
import math

import jax
import jax.numpy as jnp
from jax import lax
from jax.experimental import pallas as pl
from jax.experimental.pallas import tpu as pltpu
from jax.sharding import PartitionSpec as P

TH = 16
TW = 32
TX = 8
LANES = 128

RIM = 6
PADC = 8
EH, EW = TH + 2 * RIM, TW + 2 * PADC
RH, RW = TH + 6, 40
RING_COL = 5
MID, MID_ROWS = 6, 10

C0 = 0.7978845608028654
C1 = 0.7978845608028654 * 0.044715
NORM_STABILIZER = 1e-06

WIN_ROW, WOUT_ROW, BULK = 0, 1024, 2048
STEM_AT, KERNEL_AT, GAIN_AT, SCALE_AT = 0, (75, 124), 173, 175
SMALL = 192

STEPS = (3, 2, 1)

BF = jnp.bfloat16
F32 = jnp.float32


def vmem(count):
    return [pl.BlockSpec(memory_space=pltpu.VMEM)] * count


def smem():
    return pl.BlockSpec(memory_space=pltpu.SMEM)


def contract_rows(left, right):
    return lax.dot_general(left, right, (((0,), (0,)), ((), ())), preferred_element_type=F32)


def contract_cols(left, right):
    return lax.dot_general(left, right, (((1,), (1,)), ((), ())), preferred_element_type=F32)


def prepare_kernel(levels_ref, ocean_ref, tile_ref, west_ref, east_ref, fold_ref, stage):
    count, cells = levels_ref.shape
    stage[...] = jnp.zeros_like(stage)
    stage[0:count, :] = levels_ref[...].astype(F32)
    stage[count : count + 1, :] = ocean_ref[...]
    rows = lax.broadcasted_iota(jnp.int32, (LANES, LANES), 0)
    cols = lax.broadcasted_iota(jnp.int32, (LANES, LANES), 1)
    eye = (rows == cols).astype(BF)
    turned = contract_rows(stage[...].astype(BF), eye)
    side = RIM * TW
    rows = lax.broadcasted_iota(jnp.int32, (side, side), 0)
    cols = lax.broadcasted_iota(jnp.int32, (side, side), 1)
    swap = (rows + cols == side - 1).astype(BF)
    fold = jnp.dot(swap, turned[cells - side :].astype(BF), preferred_element_type=F32).reshape(RIM, TW, LANES)
    tile = turned.reshape(TH, TW, LANES)
    tile_ref[...] = tile.astype(BF)
    fold_ref[...] = fold.astype(BF)
    west_ref[0:TH] = tile[:, 0:PADC].astype(BF)
    west_ref[TH:] = fold[:, TW - PADC :].astype(BF)
    east_ref[0:TH] = tile[:, TW - PADC :].astype(BF)
    east_ref[TH:] = fold[:, 0:PADC].astype(BF)


def pack_kernel(used, tile_ref, west_ref, east_ref, fold_ref, lower_ref, upper_ref, folded_ref):
    spare, halo = LANES - used, RIM * PADC
    over = used - spare

    def kept(value, low, high):
        lane = lax.broadcasted_iota(jnp.int32, value.shape, 1)
        return jnp.where((lane >= low) & (lane < high), value, 0.0)

    def store(ref, own, first, last):
        own = own.astype(F32).reshape(RIM * TW, LANES)
        first, last = [value.astype(F32).reshape(halo, LANES) for value in (first, last)]
        extra = [
            kept(pltpu.roll(first, used, 1), used, LANES),
            kept(pltpu.roll(last, used, 1), used, LANES),
            kept(pltpu.roll(first, used - spare, 1), used, used + over)
            + kept(pltpu.roll(last, used - spare + over, 1), used + over, used + 2 * over),
        ]
        for index, value in enumerate(extra):
            at = slice(index * halo, (index + 1) * halo)
            ref[at] = (own[at] + value).astype(BF)
        ref[3 * halo :] = own[3 * halo :].astype(BF)

    for ref, at in ((lower_ref, slice(0, RIM)), (upper_ref, slice(TH - RIM, TH))):
        store(ref, tile_ref[at], west_ref[at], east_ref[at])
    store(folded_ref, fold_ref[...], east_ref[TH:], west_ref[TH:])


def unpack_rows(used, packed_ref, ext, at):
    spare, halo = LANES - used, RIM * PADC
    over = used - spare
    rows = packed_ref[...].astype(F32)
    lane = lax.broadcasted_iota(jnp.int32, (halo, LANES), 1)
    own = jnp.where(lax.broadcasted_iota(jnp.int32, rows.shape, 1) < used, rows, 0.0)
    ext[at : at + RIM, PADC : PADC + TW] = own.reshape(RIM, TW, LANES)
    tail = rows[2 * halo : 3 * halo]
    for index, (start, shift) in enumerate(((0, used - spare), (PADC + TW, used - spare + over))):
        front = pltpu.roll(rows[index * halo : (index + 1) * halo], LANES - used, 1)
        back = pltpu.roll(tail, LANES - shift, 1)
        value = jnp.where(lane < spare, front, jnp.where(lane < used, back, 0.0))
        ext[at : at + RIM, start : start + PADC] = value.reshape(RIM, PADC, LANES)


def load_column(ref, row, start):
    return ref[row, pl.ds(start, 8), :]


def conv_block(ref, taps, start, out_rows, in_rows, taps_of):
    totals = {o: None for o in out_rows}
    needed = sorted({o + a for o in out_rows for a in range(7) if o + a in in_rows})
    for d in range(7):
        column = {r: load_column(ref, r - in_rows.start, start + d) for r in needed}
        for a in range(7):
            held = {}
            for o in out_rows:
                r = o + a
                if r not in column:
                    continue
                which, index = taps_of(o, r, a, d)
                if (which, index) not in held:
                    held[(which, index)] = taps[which][index]
                term = held[(which, index)] * column[r]
                totals[o] = term if totals[o] is None else totals[o] + term
    return totals


def chunks(spans, body):
    def run(carry):
        for at in spans:
            carry = body(at.start // (at.stop - at.start), at, carry)
        return carry

    return run


def spans_of(count, size):
    return [slice(at, at + size) for at in range(0, count, size)]


def norm_rows(conv, xhat, rinv, normed, gain, spans):
    for at in spans:
        values = conv[at, :]
        average = jnp.mean(values, axis=-1, keepdims=True)
        centered = values - average
        inverse = lax.rsqrt(jnp.mean(centered * centered, axis=-1, keepdims=True) + NORM_STABILIZER)
        scaled = centered * inverse
        xhat[at, :] = scaled
        rinv[at, :] = jnp.broadcast_to(inverse, values.shape)
        normed[at, :] = (scaled * gain).astype(BF)


def gelu_rows(pre, act, slope, spans):
    for at in spans:
        for start in range(at.start, at.stop, 16):
            here = slice(start, start + 16)
            v = pre[here, :]
            square = v * v
            inner = v * (C0 + C1 * square)
            half = 0.5 * jnp.tanh(inner) + 0.5
            active = v * half
            act[here, :] = active.astype(BF)
            slope[here, :] = half + active * (1.0 - half) * (2.0 * C0 + (6.0 * C1) * square)


def joint_weights(stem_ref, weights):
    count = stem_ref.shape[0]
    weights[...] = jnp.zeros_like(weights)
    weights[0:count, 0:LANES] = stem_ref[...].astype(F32)
    weights[count : count + 1, LANES:] = jnp.ones((1, LANES), F32)
    return weights[...].astype(BF)


def middle_kernel(
    tile_ref,
    west_ref,
    east_ref,
    table_ref,
    stem_ref,
    win_ref,
    wout_ref,
    flat,
    xhat,
    rinv,
    normed,
    act,
    slope,
    branch,
    ext,
    x0,
    m6,
    weights,
    taps,
    conv,
    wide,
):
    joint = joint_weights(stem_ref, weights)
    spread_taps(table_ref, 0, taps)
    ext[:, 0:PADC] = west_ref[0:TH].astype(F32)
    ext[:, PADC : PADC + TW] = tile_ref[...].astype(F32)
    ext[:, PADC + TW :] = east_ref[0:TH].astype(F32)
    for row in range(0, TH, 4):
        at = slice(row, row + 4)
        both = jnp.dot(ext[at].reshape(4 * EW, LANES).astype(BF), joint, preferred_element_type=F32)
        mask = both[:, LANES:]
        m6[at] = mask.reshape(4, EW, LANES)
        x0[at] = (mask * both[:, :LANES]).astype(BF).astype(F32).reshape(4, EW, LANES)

    def conv_columns(block, _):
        start = pl.multiple_of(block * 8, 8)
        rows = range(MID, MID + MID_ROWS)
        totals = conv_block(x0, (taps,), start + 2, rows, range(RIM, RIM + TH), lambda o, r, a, d: (0, a * 7 + d))
        for o in rows:
            conv[pl.ds(pl.multiple_of((o - MID) * RW + start, 8), 8), :] = totals[o]
        return 0

    lax.fori_loop(0, RW // 8, conv_columns, 0)
    count = MID_ROWS * RW
    spans = spans_of(count, 2 * RW)
    norm_rows(conv, xhat, rinv, normed, table_ref[49, 0:1, :], spans)
    wide[...] = jnp.dot(normed[...], win_ref[0], preferred_element_type=F32)
    gelu_rows(wide, act, slope, spans)
    branch[...] = jnp.dot(act[...], wout_ref[0], preferred_element_type=F32)
    for index, at in enumerate(spans):
        rows = slice(index * 2 + MID + 3 - RIM, index * 2 + MID + 5 - RIM)
        mask = m6[rows, RING_COL : RING_COL + RW, :]
        held = x0[rows, RING_COL : RING_COL + RW, :]
        value = mask * (held + table_ref[50, 0:1, :] * branch[at, :].reshape(2, RW, LANES))
        flat[at, :] = value.reshape(2 * RW, LANES).astype(BF)


def spread_taps(dw_ref, layer, taps, top=None):
    for t in range(49):
        row = dw_ref[t, layer : layer + 1, :]
        if top is not None:
            row = jnp.where(top, dw_ref[48 - t, layer : layer + 1, :], row)
        taps[t] = jnp.broadcast_to(row, (8, LANES))


def padded(flat, pad, width):
    rows = flat.shape[0] // width
    pad[:, 0:PADC, :] = jnp.zeros((rows, PADC, LANES), F32)
    pad[:, PADC + width :, :] = jnp.zeros((rows, pad.shape[1] - PADC - width, LANES), F32)
    for row in range(0, rows, 2):
        value = flat[row * width : (row + 2) * width, :].astype(F32)
        pad[row : row + 2, PADC : PADC + width, :] = value.reshape(2, width, LANES)


def main_kernel(
    rescale,
    top_ref,
    tile_ref,
    west_ref,
    east_ref,
    south_ref,
    north_ref,
    table_ref,
    stem_ref,
    win_ref,
    wout_ref,
    up_ref,
    mid_flat,
    mid_xhat,
    mid_rinv,
    mid_normed,
    mid_act,
    mid_slope,
    mid_branch,
    out_ref,
    packed_ref,
    sums,
    cells,
    flat0,
    flat1,
    grad0,
    grad1,
    carry0,
    x0,
    m6,
    x1,
    taps0,
    taps0n,
    pad1,
    g1,
    ext,
    weights,
    taps1,
    conv0,
    xhat0,
    rinv0,
    branch0,
    normed0,
    act0,
    slope0,
    conv1,
    xhat1,
    rinv1,
    branch1,
    normed1,
    act1,
    slope1,
    wide,
    thin,
    gpre,
):
    top = top_ref[0] == 1
    count0, count1 = RH * RW, TH * TW
    all0, all1 = spans_of(count0, 2 * RW), spans_of(count1, 2 * TW)
    middle = slice(MID * RW, (MID + MID_ROWS) * RW)
    rims = [slice(0, middle.start), slice(middle.stop, count0)]
    rim0 = [at for at in all0 if at.stop <= middle.start or at.start >= middle.stop]

    def from_middle(at):
        return middle.start <= at.start < middle.stop

    def pick(mid, ref, at):
        if from_middle(at):
            return mid[at.start - middle.start : at.stop - middle.start, :]
        return ref[at, :]

    unpack_rows(stem_ref.shape[0] + 1, south_ref, ext, 0)
    unpack_rows(stem_ref.shape[0] + 1, north_ref, ext, RIM + TH)
    ext[RIM : RIM + TH, PADC : PADC + TW] = tile_ref[...].astype(F32)
    ext[RIM : RIM + TH, 0:PADC] = west_ref[0:TH].astype(F32)
    ext[RIM : RIM + TH, PADC + TW :] = east_ref[0:TH].astype(F32)

    joint = joint_weights(stem_ref, weights)

    for index in range(EH // 4):
        at = slice(index * 4, index * 4 + 4)
        here = ext[at].reshape(4 * EW, LANES).astype(BF)
        cells[index * 4 * EW : (index + 1) * 4 * EW, :] = here
        both = jnp.dot(here, joint, preferred_element_type=F32)
        mask = both[:, LANES:]
        m6[at] = mask.reshape(4, EW, LANES)
        value = (mask * both[:, :LANES]).astype(BF)
        flat0[index * 4 * EW : (index + 1) * 4 * EW, :] = value
        x0[at] = value.astype(F32).reshape(4, EW, LANES)

    spread_taps(table_ref, 0, taps0)
    spread_taps(table_ref, 0, taps0n, top)
    spread_taps(table_ref, 1, taps1)

    north_at = 3 + TH

    def conv0_block(block, _):
        start = pl.multiple_of(block * 8, 8)
        for rows in (range(0, MID), range(MID + MID_ROWS, north_at), range(north_at, RH)):
            totals = conv_block(
                x0,
                (taps0, taps0n),
                start + 2,
                rows,
                range(0, EH),
                lambda o, r, a, d: (1 if o >= north_at else 0, a * 7 + d),
            )
            for o in rows:
                conv0[pl.ds(pl.multiple_of(o * RW + start, 8), 8), :] = totals[o]
        return 0

    lax.fori_loop(0, RW // 8, conv0_block, 0)

    norm_rows(conv0, xhat0, rinv0, normed0, table_ref[49, 0:1, :], rim0)
    normed0[middle] = mid_normed[...]
    act0[middle] = mid_act[...]
    for at in rims:
        wide[at] = jnp.dot(normed0[at], win_ref[0], preferred_element_type=F32)
    gelu_rows(wide, act0, slope0, rim0)
    for at in rims:
        branch0[at] = jnp.dot(act0[at], wout_ref[0], preferred_element_type=F32)

    flat1[middle] = mid_flat[...]
    for index, at in enumerate(all0):
        if not from_middle(at):
            rows = slice(index * 2 + 3, index * 2 + 5)
            mask = m6[rows, RING_COL : RING_COL + RW, :]
            held = x0[rows, RING_COL : RING_COL + RW, :]
            value = mask * (held + table_ref[50, 0:1, :] * branch0[at, :].reshape(2, RW, LANES))
            flat1[at, :] = value.reshape(2 * RW, LANES).astype(BF)
        x1[index * 2 : index * 2 + 2] = flat1[at, :].astype(F32).reshape(2, RW, LANES)

    def conv1_block(block, _):
        start = pl.multiple_of(block * 8, 8)
        for rows in (range(0, 16),):
            totals = conv_block(
                x1, (taps1,), start, rows, range(0, RH), lambda o, r, a, d: (0, a * 7 + d)
            )
            for o in rows:
                conv1[pl.ds(pl.multiple_of(o * TW + start, 8), 8), :] = totals[o]
        return 0

    lax.fori_loop(0, TW // 8, conv1_block, 0)
    norm_rows(conv1, xhat1, rinv1, normed1, table_ref[49, 1:2, :], all1)
    wide[0:count1] = jnp.dot(normed1[...], win_ref[1], preferred_element_type=F32)
    gelu_rows(wide, act1, slope1, all1)
    branch1[...] = jnp.dot(act1[...], wout_ref[1], preferred_element_type=F32)

    sums[...] = jnp.zeros_like(sums)
    g1[...] = jnp.zeros_like(g1)

    def folded(value):
        return jnp.sum(value.reshape(-1, 8, LANES), axis=0)

    def next1(index, at, total):
        rows = 2
        mask = m6[pl.ds(index * rows + RIM, rows), PADC : PADC + TW, :]
        held = x1[pl.ds(index * rows + 3, rows), 3 : 3 + TW, :]
        branch = branch1[at, :].reshape(rows, TW, LANES)
        out_ref[at, :] = (mask * (held + table_ref[50, 1:2, :] * branch)).astype(BF).reshape(rows * TW, LANES)
        masked = mask * (up_ref[at, :].astype(F32) * rescale).reshape(rows, TW, LANES)
        g1[pl.ds(index * rows + 3, rows), 3 : 3 + TW, :] = masked
        thin[at, :] = (masked * table_ref[50, 1:2, :]).reshape(rows * TW, LANES).astype(BF)
        return total + folded(masked * branch)

    total = chunks(all1, next1)(jnp.zeros((8, LANES), F32))
    sums[3:4, :] = jnp.sum(total, axis=0, keepdims=True)

    def grad_wout(layer, count, act):
        packed_ref[WOUT_ROW + 512 * layer : WOUT_ROW + 512 * layer + 512, :] = contract_rows(
            act[...], thin[0:count]
        ).astype(BF)

    def grad_pre(layer, count, slope):
        wide[0:count] = contract_cols(thin[0:count], wout_ref[layer])

        for at in spans_of(count, 16):
            gpre[at, :] = (wide[at, :] * slope(at)).astype(BF)

    def grad_win(layer, count, normed):
        gp = gpre[0:count]
        grad_in = contract_rows(normed[...], gp).astype(BF)
        for part in range(4):
            at = WIN_ROW + 512 * layer + 128 * part
            packed_ref[at : at + 128, :] = grad_in[:, 128 * part : 128 * part + 128]
        wide[0:count, 0:LANES] = contract_cols(gp, win_ref[layer])

    def grad_conv(layer, count, size, xhat, rinv, grad):
        gain = table_ref[49, layer : layer + 1, :]

        def step(index, at, total):
            gn = wide[at, 0:LANES]
            scaled = xhat(at)
            gx = gn * gain
            first = jnp.mean(gx, axis=-1, keepdims=True)
            second = jnp.mean(gx * scaled, axis=-1, keepdims=True)
            grad[at, :] = (rinv(at) * (gx - first - scaled * second)).astype(BF)
            return total + folded(gn * scaled)

        total = chunks(spans_of(count, size), step)(jnp.zeros((8, LANES), F32))
        sums[layer : layer + 1, :] = jnp.sum(total, axis=0, keepdims=True)

    grad_wout(1, count1, act1)
    grad_pre(1, count1, lambda at: slope1[at, :])
    grad_win(1, count1, normed1)
    grad_conv(1, count1, 2 * TW, lambda at: xhat1[at, :], lambda at: rinv1[at, :], grad1)
    padded(grad1, pad1, TW)

    def back1_block(block, _):
        start = pl.multiple_of(block * 8, 8)
        for rows in (range(0, 22),):
            totals = conv_block(
                pad1, (taps1,), start + 2, rows, range(6, 6 + TH), lambda o, r, a, d: (0, 48 - (a * 7 + d))
            )
            for o in rows:
                g1[o, pl.ds(start, 8), :] += totals[o]
        return 0

    lax.fori_loop(0, RW // 8, back1_block, 0)

    def masked0(index, at, total):
        rows = pl.ds(index * 2, 2)
        masked = m6[pl.ds(index * 2 + 3, 2), RING_COL : RING_COL + RW, :] * g1[rows]
        flat = masked.reshape(2 * RW, LANES)
        carry0[at, :] = flat
        thin[at, :] = (flat * table_ref[50, 0:1, :]).astype(BF)
        return total + folded(flat * pick(mid_branch, branch0, at))

    total = chunks(all0, masked0)(jnp.zeros((8, LANES), F32))
    sums[2:3, :] = jnp.sum(total, axis=0, keepdims=True)
    grad_wout(0, count0, act0)
    grad_pre(0, count0, lambda at: pick(mid_slope, slope0, at))
    grad_win(0, count0, normed0)
    grad_conv(
        0,
        count0,
        2 * RW,
        lambda at: pick(mid_xhat, xhat0, at),
        lambda at: pick(mid_rinv, rinv0, at),
        grad0,
    )


def taps1_kernel(flat1, grad1, gk1, x1, pad1):
    for row in range(0, RH, 2):
        x1[row : row + 2] = flat1[row * RW : (row + 2) * RW, :].astype(F32).reshape(2, RW, LANES)
    padded(grad1, pad1, TW)
    gk1[...] = jnp.zeros_like(gk1)

    def kernel1_block(block, _):
        start = pl.multiple_of(block * 8, 8)
        grads = [pad1[j, pl.ds(start + PADC, 8), :] for j in range(TH)]
        for d in range(7):
            column = [load_column(x1, r, start + d) for r in range(RH)]
            for a in range(7):
                total = gk1[a * 7 + d]
                for j in range(TH):
                    total = total + grads[j] * column[j + a]
                gk1[a * 7 + d] = total
        return 0

    lax.fori_loop(0, TW // 8, kernel1_block, 0)


def rest_kernel(
    top_ref,
    dw_ref,
    sums,
    cells,
    flat0,
    grad0,
    carry0,
    gk1,
    small_ref,
    small,
    x0,
    pad0,
    taps0,
    taps0n,
    h0,
    gk0,
    gk0n,
):
    top = top_ref[0] == 1
    north_at = 3 + TH
    levels_count = KERNEL_AT[0] - STEM_AT

    for row in range(0, EH, 4):
        x0[row : row + 4] = flat0[row * EW : (row + 4) * EW, :].astype(F32).reshape(4, EW, LANES)
    padded(grad0, pad0, RW)
    spread_taps(dw_ref, 0, taps0)
    spread_taps(dw_ref, 0, taps0n, top)

    gk0[...] = jnp.zeros_like(gk0)
    gk0n[...] = jnp.zeros_like(gk0n)

    def kernel0_block(block, _):
        start = pl.multiple_of(block * 8, 8)
        grads = [pad0[j, pl.ds(start + PADC, 8), :] for j in range(RH)]
        for d in range(7):
            column = [load_column(x0, r, start + 2 + d) for r in range(EH)]
            for a in range(7):
                total = gk0[a * 7 + d]
                for j in range(north_at):
                    total = total + grads[j] * column[j + a]
                gk0[a * 7 + d] = total
                total = gk0n[a * 7 + d]
                for j in range(north_at, RH):
                    total = total + grads[j] * column[j + a]
                gk0n[a * 7 + d] = total
        return 0

    lax.fori_loop(0, RW // 8, kernel0_block, 0)
    for t in range(49):
        north = jnp.where(top, gk0n[48 - t], gk0n[t])
        small[KERNEL_AT[0] + t : KERNEL_AT[0] + t + 1, :] = jnp.sum(gk0[t] + north, axis=0, keepdims=True)
        small[KERNEL_AT[1] + t : KERNEL_AT[1] + t + 1, :] = jnp.sum(gk1[t], axis=0, keepdims=True)

    def back0_block(block, _):
        start = pl.multiple_of(block * 8, 8)
        for rows in (range(0, 14), range(14, 28)):
            totals = conv_block(
                pad0,
                (taps0, taps0n),
                start,
                rows,
                range(6, 6 + RH),
                lambda o, r, a, d: (1 if r - 6 >= north_at else 0, 48 - (a * 7 + d)),
            )
            for o in rows:
                h0[o, pl.ds(start, 8), :] = totals[o]
        return 0

    lax.fori_loop(0, EW // 8, back0_block, 0)
    for row in range(0, RH, 2):
        h0[row + 3 : row + 5, RING_COL : RING_COL + RW, :] += carry0[
            row * RW : (row + 2) * RW, :
        ].reshape(2, RW, LANES)
    rows = lax.broadcasted_iota(jnp.int32, (LANES, LANES), 0)
    mask = jnp.dot(cells[...], (rows == levels_count).astype(BF), preferred_element_type=F32)
    stem_side = (mask * h0[...].reshape(EH * EW, LANES)).astype(BF)
    stem_grad = contract_rows(cells[...], stem_side)
    small[STEM_AT : KERNEL_AT[0], :] = stem_grad[0:levels_count, :]
    small[GAIN_AT : GAIN_AT + 4, :] = sums[0:4, :]
    small[GAIN_AT + 4 :, :] = jnp.zeros((SMALL - GAIN_AT - 4, LANES), F32)
    small_ref[...] = small[...].astype(BF)


def unpack_kernel(
    order_ref,
    pieces_ref,
    mine_ref,
    other_ref,
    stem_out,
    kernel_out,
    gain_out,
    win_out,
    wout_out,
    scale_out,
    stem_ref,
    kernel_ref,
    gain_ref,
    win_ref,
    wout_ref,
    scale_ref,
    small,
    sent,
):
    count, size = pieces_ref.shape[0], pieces_ref.shape[1]
    stores = [
        pltpu.make_async_copy(source, target, sent.at[index])
        for index, (source, target) in enumerate(
            [(win_ref.at[layer], win_out.at[layer]) for layer in range(2)]
            + [(wout_ref.at[layer], wout_out.at[layer]) for layer in range(2)]
            + [(stem_ref, stem_out), (kernel_ref, kernel_out), (gain_ref, gain_out), (scale_ref, scale_out)]
        )
    ]

    def rows(at, length):
        return [
            pieces_ref[order_ref[index]].astype(F32) if count > 1 else pieces_ref[0, index * 128 : index * 128 + 128].astype(F32)
            for index in range(at // 128, (at + length) // 128)
        ]

    for layer in range(2):
        for part, block in enumerate(rows(WIN_ROW + 512 * layer, 512)):
            win_ref[layer, :, 128 * part : 128 * part + 128] = block
        stores[layer].start()
    for layer in range(2):
        for part, block in enumerate(rows(WOUT_ROW + 512 * layer, 512)):
            wout_ref[layer, 128 * part : 128 * part + 128, :] = block
        stores[2 + layer].start()
    places, size = mine_ref.shape[0], mine_ref.shape[1]
    for index in range(places):
        at = order_ref[count + index]
        small[index * size : (index + 1) * size, :] = mine_ref[at].astype(F32) + other_ref[at].astype(F32)
    for layer in range(2):
        kernel_ref[:, layer, :] = small[KERNEL_AT[layer] : KERNEL_AT[layer] + 49, :]
    stem_ref[...] = small[STEM_AT : STEM_AT + stem_ref.shape[0], :]
    gain_ref[...] = small[GAIN_AT : GAIN_AT + 2, :]
    scale_ref[...] = small[SCALE_AT : SCALE_AT + 2, :]
    for store in stores[4:]:
        store.start()
    for store in stores:
        store.wait()


def permuted(value, pairs):
    return lax.ppermute(value, "gy", pairs)


def crossed(value, bits):
    return permuted(value, [(i, i ^ bits) for i in range(lax.axis_size("gy"))])


def summed_pieces(packed, top, rest):
    size = lax.axis_size("gy")
    if size != 16:
        bulk, small = lax.psum((packed.astype(F32), rest(top).astype(F32)), "gy")
        small = small.astype(BF)[None]
        return bulk.astype(BF)[None], small, jnp.zeros_like(small), jnp.zeros((2,), jnp.int32)
    me = lax.axis_index("gy")
    core, side, deep = me & 1, (me >> 1) & 1, me >> 2

    def halves(value, bit):
        half = value.shape[0] // 2
        low, high = value[:half], value[half:]
        return jnp.where(bit == 0, low, high), jnp.where(bit == 0, high, low)

    keep, send = halves(packed, core)
    came = crossed(send, 1)
    came, top = lax.optimization_barrier((came, top))
    small = rest(top)
    keep, send = halves(keep.astype(F32) + came.astype(F32), side)
    total = keep + crossed(send.astype(BF), 2).astype(F32)
    quarter = total.shape[0] // 4
    part = small.shape[0] // 4

    def shard(step):
        at = deep ^ step
        return jnp.concatenate(
            [
                lax.dynamic_slice_in_dim(total, at * quarter, quarter, 0).astype(BF),
                lax.dynamic_slice_in_dim(small, at * part, part, 0),
            ],
            axis=0,
        )

    arrived = [crossed(shard(step), 4 * step) for step in STEPS]
    bulk = lax.dynamic_slice_in_dim(total, deep * quarter, quarter, 0)
    rest_sum = lax.dynamic_slice_in_dim(small, deep * part, part, 0).astype(F32)
    for other in arrived:
        bulk = bulk + other[:quarter].astype(F32)
        rest_sum = rest_sum + other[quarter:].astype(F32)
    mine = jnp.concatenate([bulk.astype(BF), rest_sum.astype(BF)], axis=0)
    pieces = jnp.stack([mine] + [crossed(mine, 4 * step) for step in STEPS][::-1])
    came = crossed(pieces, 2)
    bulk = jnp.concatenate([pieces[:, :quarter], came[:, :quarter]], axis=0)
    small = (pieces[:, quarter:].astype(F32) + came[:, quarter:].astype(F32)).astype(BF)
    rows = bulk.shape[0] * quarter
    joined = jnp.concatenate([bulk.reshape(rows, LANES), small.reshape(4 * part, LANES)], axis=0)
    came = crossed(joined, 1)
    bulk = jnp.concatenate([bulk, came[:rows].reshape(bulk.shape)], axis=0)
    mixed = ((core << 3) | (side << 2) | deep).astype(jnp.int32)
    order = jnp.arange(20, dtype=jnp.int32) & 15
    order = order ^ jnp.where(jnp.arange(20) < 16, mixed, deep.astype(jnp.int32))
    return bulk, small, came[rows:].reshape(small.shape), order


def shards(levels, ocean, stem, dw_kernel, ln_gain, w_in, w_out, layer_scale, upstream):
    size = lax.axis_size("gy")
    rows = size // TX
    me = lax.axis_index("gy")
    is_top = me // TX == rows - 1
    count = levels.shape[2]
    top = is_top.astype(jnp.int32)[None]
    table = jnp.concatenate([dw_kernel.transpose(1, 0, 2), ln_gain[None], layer_scale[None]])
    tile, to_west, to_east, folded = pl.pallas_call(
        prepare_kernel,
        out_shape=[
            jax.ShapeDtypeStruct((TH, TW, LANES), BF),
            jax.ShapeDtypeStruct((TH + RIM, PADC, LANES), BF),
            jax.ShapeDtypeStruct((TH + RIM, PADC, LANES), BF),
            jax.ShapeDtypeStruct((RIM, TW, LANES), BF),
        ],
        in_specs=vmem(2),
        out_specs=vmem(4),
        scratch_shapes=[pltpu.VMEM((LANES, count), F32)],
        compiler_params=pltpu.CompilerParams(vmem_limit_bytes=4 << 20),
    )(levels[0], ocean.astype(F32))

    def column_pairs(step):
        return [(i, i // TX * TX + (i % TX + step) % TX) for i in range(size)]

    west = permuted(to_east, column_pairs(1))
    east = permuted(to_west, column_pairs(-1))

    lower, upper, folded = pl.pallas_call(
        functools.partial(pack_kernel, stem.shape[0] + 1),
        out_shape=[jax.ShapeDtypeStruct((RIM * TW, LANES), BF)] * 3,
        in_specs=vmem(4),
        out_specs=vmem(3),
        compiler_params=pltpu.CompilerParams(vmem_limit_bytes=4 << 20),
    )(tile, west, east, folded)
    folded = permuted(folded, [(i, i // TX * TX + TX - 1 - i % TX) for i in range(size - TX, size)])
    if rows == 2:
        north = permuted(jnp.where(is_top, lower, upper), [(i, (i + TX) % size) for i in range(size)])
        south = jnp.where(is_top, north, jnp.zeros_like(north))
    else:
        south = permuted(upper, [(i, i + TX) for i in range(size - TX)])
        north = permuted(lower, [(i + TX, i) for i in range(size - TX)])
    north = jnp.where(is_top, folded, north)

    def scratch(*shape, dtype=F32):
        return pltpu.VMEM(shape, dtype)

    count0 = RH * RW
    hidden = w_in.shape[2]
    count_mid = MID_ROWS * RW
    mid_shapes = [
        jax.ShapeDtypeStruct((count_mid, LANES), BF),
        jax.ShapeDtypeStruct((count_mid, LANES), F32),
        jax.ShapeDtypeStruct((count_mid, LANES), F32),
        jax.ShapeDtypeStruct((count_mid, LANES), BF),
        jax.ShapeDtypeStruct((count_mid, hidden), BF),
        jax.ShapeDtypeStruct((count_mid, hidden), F32),
        jax.ShapeDtypeStruct((count_mid, LANES), F32),
    ]
    middle = pl.pallas_call(
        middle_kernel,
        out_shape=mid_shapes,
        in_specs=vmem(7),
        out_specs=vmem(7),
        scratch_shapes=[
            scratch(TH, EW, LANES),
            scratch(TH, EW, LANES),
            scratch(TH, EW, LANES),
            scratch(LANES, 2 * LANES),
            scratch(49, 8, LANES),
            scratch(count_mid, LANES),
            scratch(count_mid, hidden),
        ],
        compiler_params=pltpu.CompilerParams(vmem_limit_bytes=10 << 20),
        cost_estimate=pl.CostEstimate(flops=4_000_000_000, bytes_accessed=3_000_000, transcendentals=0),
    )(tile, west, east, table, stem, w_in, w_out)

    ring_shapes = [
        jax.ShapeDtypeStruct((8, LANES), F32),
        jax.ShapeDtypeStruct((EH * EW, LANES), BF),
        jax.ShapeDtypeStruct((EH * EW, LANES), BF),
        jax.ShapeDtypeStruct((RH * RW, LANES), BF),
        jax.ShapeDtypeStruct((RH * RW, LANES), BF),
        jax.ShapeDtypeStruct((TH * TW, LANES), BF),
        jax.ShapeDtypeStruct((RH * RW, LANES), F32),
    ]
    result, packed, *ring = pl.pallas_call(
        functools.partial(main_kernel, 1.0 / math.sqrt(size * count)),
        out_shape=[
            jax.ShapeDtypeStruct((count, LANES), BF),
            jax.ShapeDtypeStruct((BULK, LANES), BF),
        ]
        + ring_shapes,
        in_specs=[smem()] + vmem(17),
        out_specs=vmem(9),
        scratch_shapes=[
            scratch(EH, EW, LANES),
            scratch(EH, EW, LANES),
            scratch(RH, RW, LANES),
            scratch(49, 8, LANES),
            scratch(49, 8, LANES),
            scratch(TH, EW, LANES),
            scratch(RH, RW, LANES),
            scratch(EH, EW, LANES),
            scratch(LANES, 2 * LANES),
            scratch(49, 8, LANES),
            scratch(count0, LANES),
            scratch(count0, LANES),
            scratch(count0, LANES),
            scratch(count0, LANES),
            scratch(count0, LANES, dtype=BF),
            scratch(count0, hidden, dtype=BF),
            scratch(count0, hidden),
            scratch(count, LANES),
            scratch(count, LANES),
            scratch(count, LANES),
            scratch(count, LANES),
            scratch(count, LANES, dtype=BF),
            scratch(count, hidden, dtype=BF),
            scratch(count, hidden),
            scratch(count0, hidden),
            scratch(count0, LANES, dtype=BF),
            scratch(count0, hidden, dtype=BF),
        ],
        compiler_params=pltpu.CompilerParams(vmem_limit_bytes=20 << 20),
    )(
        top,
        tile,
        west,
        east,
        south,
        north,
        table,
        stem,
        w_in,
        w_out,
        upstream[0],
        *middle,
    )

    sums, cells, flat0, flat1, grad0, grad1, carry0 = ring
    grad_taps1 = pl.pallas_call(
        taps1_kernel,
        out_shape=jax.ShapeDtypeStruct((49, 8, LANES), F32),
        in_specs=vmem(2),
        out_specs=vmem(1)[0],
        scratch_shapes=[scratch(RH, RW, LANES), scratch(TH, EW, LANES)],
        compiler_params=pltpu.CompilerParams(vmem_limit_bytes=6 << 20),
        cost_estimate=pl.CostEstimate(flops=2_000_000_000, bytes_accessed=500_000, transcendentals=0),
    )(flat1, grad1)

    def rest(top):
        return pl.pallas_call(
            rest_kernel,
            out_shape=jax.ShapeDtypeStruct((SMALL, LANES), BF),
            in_specs=[smem()] + vmem(7),
            out_specs=vmem(1)[0],
            scratch_shapes=[
                scratch(SMALL, LANES),
                scratch(EH, EW, LANES),
                scratch(RH, EW + 8, LANES),
                scratch(49, 8, LANES),
                scratch(49, 8, LANES),
                scratch(EH, EW, LANES),
                scratch(49, 8, LANES),
                scratch(49, 8, LANES),
            ],
            compiler_params=pltpu.CompilerParams(vmem_limit_bytes=10 << 20),
            cost_estimate=pl.CostEstimate(flops=10_000_000_000, bytes_accessed=4_000_000, transcendentals=0),
        )(top, table, sums, cells, flat0, grad0, carry0, grad_taps1)

    pieces, mine, other, order = summed_pieces(packed, top, rest)
    shapes = [array.shape for array in (stem, dw_kernel, ln_gain, w_in, w_out, layer_scale)]
    shapes[1] = (shapes[1][1], shapes[1][0], shapes[1][2])
    grads = pl.pallas_call(
        unpack_kernel,
        out_shape=[jax.ShapeDtypeStruct(shape, F32) for shape in shapes],
        in_specs=[smem()] + vmem(3),
        out_specs=[pl.BlockSpec(memory_space=pltpu.HBM)] * 6,
        scratch_shapes=[scratch(*shape) for shape in shapes]
        + [scratch(SMALL, LANES), pltpu.SemaphoreType.DMA((8,))],
        compiler_params=pltpu.CompilerParams(vmem_limit_bytes=8 << 20),
    )(order, pieces, mine, other)
    grads = list(grads)
    grads[1] = grads[1].transpose(1, 0, 2)
    return (result[None], *grads)


def solution(mesh):
    in_specs = (
        P(("groups", "gy"), None, None),
        P(("groups", "gy"), None),
        P(),
        P(),
        P(),
        P(),
        P(),
        P(),
        P(("groups", "gy"), None, None),
    )
    out_specs = (
        P(("groups", "gy"), None, None),
        P("groups", None),
        P("groups", None, None),
        P("groups", None),
        P("groups", None, None),
        P("groups", None, None),
        P("groups", None),
    )
    return jax.shard_map(shards, mesh=mesh, in_specs=in_specs, out_specs=out_specs, check_vma=False)
```

```python
import functools
import math

import jax
import jax.numpy as jnp
from jax import lax
from jax.experimental import pallas as pl
from jax.experimental.pallas import tpu as pltpu
from jax.sharding import PartitionSpec as P

TH = 16
TW = 32
TX = 8
LANES = 128

RIM = 6
PADC = 8
EH, EW = TH + 2 * RIM, TW + 2 * PADC
RH, RW = TH + 6, 40
RING_COL = 5
MID, MID_ROWS = 6, 10

C0 = 0.7978845608028654
C1 = 0.7978845608028654 * 0.044715
NORM_STABILIZER = 1e-06

WIN_ROW, WOUT_ROW, BULK = 0, 1024, 2048
STEM_AT, KERNEL_AT, GAIN_AT, SCALE_AT = 0, (75, 124), 173, 175
SMALL = 192

STEPS = (3, 2, 1)

BF = jnp.bfloat16
F32 = jnp.float32


def vmem(count):
    return [pl.BlockSpec(memory_space=pltpu.VMEM)] * count


def smem():
    return pl.BlockSpec(memory_space=pltpu.SMEM)


def contract_rows(left, right):
    return lax.dot_general(left, right, (((0,), (0,)), ((), ())), preferred_element_type=F32)


def contract_cols(left, right):
    return lax.dot_general(left, right, (((1,), (1,)), ((), ())), preferred_element_type=F32)


def prepare_kernel(levels_ref, ocean_ref, tile_ref, west_ref, east_ref, fold_ref, stage):
    count, cells = levels_ref.shape
    stage[...] = jnp.zeros_like(stage)
    stage[0:count, :] = levels_ref[...].astype(F32)
    stage[count : count + 1, :] = ocean_ref[...]
    rows = lax.broadcasted_iota(jnp.int32, (LANES, LANES), 0)
    cols = lax.broadcasted_iota(jnp.int32, (LANES, LANES), 1)
    eye = (rows == cols).astype(BF)
    turned = contract_rows(stage[...].astype(BF), eye)
    side = RIM * TW
    rows = lax.broadcasted_iota(jnp.int32, (side, side), 0)
    cols = lax.broadcasted_iota(jnp.int32, (side, side), 1)
    swap = (rows + cols == side - 1).astype(BF)
    fold = jnp.dot(swap, turned[cells - side :].astype(BF), preferred_element_type=F32).reshape(RIM, TW, LANES)
    tile = turned.reshape(TH, TW, LANES)
    tile_ref[...] = tile.astype(BF)
    fold_ref[...] = fold.astype(BF)
    west_ref[0:TH] = tile[:, 0:PADC].astype(BF)
    west_ref[TH:] = fold[:, TW - PADC :].astype(BF)
    east_ref[0:TH] = tile[:, TW - PADC :].astype(BF)
    east_ref[TH:] = fold[:, 0:PADC].astype(BF)


def pack_kernel(used, tile_ref, west_ref, east_ref, fold_ref, lower_ref, upper_ref, folded_ref):
    spare, halo = LANES - used, RIM * PADC
    over = used - spare

    def kept(value, low, high):
        lane = lax.broadcasted_iota(jnp.int32, value.shape, 1)
        return jnp.where((lane >= low) & (lane < high), value, 0.0)

    def store(ref, own, first, last):
        own = own.astype(F32).reshape(RIM * TW, LANES)
        first, last = [value.astype(F32).reshape(halo, LANES) for value in (first, last)]
        extra = [
            kept(pltpu.roll(first, used, 1), used, LANES),
            kept(pltpu.roll(last, used, 1), used, LANES),
            kept(pltpu.roll(first, used - spare, 1), used, used + over)
            + kept(pltpu.roll(last, used - spare + over, 1), used + over, used + 2 * over),
        ]
        for index, value in enumerate(extra):
            at = slice(index * halo, (index + 1) * halo)
            ref[at] = (own[at] + value).astype(BF)
        ref[3 * halo :] = own[3 * halo :].astype(BF)

    for ref, at in ((lower_ref, slice(0, RIM)), (upper_ref, slice(TH - RIM, TH))):
        store(ref, tile_ref[at], west_ref[at], east_ref[at])
    store(folded_ref, fold_ref[...], east_ref[TH:], west_ref[TH:])


def unpack_rows(used, packed_ref, ext, at):
    spare, halo = LANES - used, RIM * PADC
    over = used - spare
    rows = packed_ref[...].astype(F32)
    lane = lax.broadcasted_iota(jnp.int32, (halo, LANES), 1)
    own = jnp.where(lax.broadcasted_iota(jnp.int32, rows.shape, 1) < used, rows, 0.0)
    ext[at : at + RIM, PADC : PADC + TW] = own.reshape(RIM, TW, LANES)
    tail = rows[2 * halo : 3 * halo]
    for index, (start, shift) in enumerate(((0, used - spare), (PADC + TW, used - spare + over))):
        front = pltpu.roll(rows[index * halo : (index + 1) * halo], LANES - used, 1)
        back = pltpu.roll(tail, LANES - shift, 1)
        value = jnp.where(lane < spare, front, jnp.where(lane < used, back, 0.0))
        ext[at : at + RIM, start : start + PADC] = value.reshape(RIM, PADC, LANES)


def load_column(ref, row, start):
    return ref[row, pl.ds(start, 8), :]


def conv_block(ref, taps, start, out_rows, in_rows, taps_of):
    totals = {o: None for o in out_rows}
    needed = sorted({o + a for o in out_rows for a in range(7) if o + a in in_rows})
    for d in range(7):
        column = {r: load_column(ref, r - in_rows.start, start + d) for r in needed}
        for a in range(7):
            held = {}
            for o in out_rows:
                r = o + a
                if r not in column:
                    continue
                which, index = taps_of(o, r, a, d)
                if (which, index) not in held:
                    held[(which, index)] = taps[which][index]
                term = held[(which, index)] * column[r]
                totals[o] = term if totals[o] is None else totals[o] + term
    return totals


def chunks(spans, body):
    def run(carry):
        for at in spans:
            carry = body(at.start // (at.stop - at.start), at, carry)
        return carry

    return run


def spans_of(count, size):
    return [slice(at, at + size) for at in range(0, count, size)]


def norm_rows(conv, xhat, rinv, normed, gain, spans):
    for at in spans:
        values = conv[at, :]
        average = jnp.mean(values, axis=-1, keepdims=True)
        centered = values - average
        inverse = lax.rsqrt(jnp.mean(centered * centered, axis=-1, keepdims=True) + NORM_STABILIZER)
        scaled = centered * inverse
        xhat[at, :] = scaled
        rinv[at, :] = jnp.broadcast_to(inverse, values.shape)
        normed[at, :] = (scaled * gain).astype(BF)


def gelu_rows(pre, act, slope, spans):
    for at in spans:
        for start in range(at.start, at.stop, 16):
            here = slice(start, start + 16)
            v = pre[here, :]
            square = v * v
            inner = v * (C0 + C1 * square)
            half = 0.5 * jnp.tanh(inner) + 0.5
            active = v * half
            act[here, :] = active.astype(BF)
            slope[here, :] = half + active * (1.0 - half) * (2.0 * C0 + (6.0 * C1) * square)


def joint_weights(stem_ref, weights):
    count = stem_ref.shape[0]
    weights[...] = jnp.zeros_like(weights)
    weights[0:count, 0:LANES] = stem_ref[...].astype(F32)
    weights[count : count + 1, LANES:] = jnp.ones((1, LANES), F32)
    return weights[...].astype(BF)


def middle_kernel(
    tile_ref,
    west_ref,
    east_ref,
    table_ref,
    stem_ref,
    win_ref,
    wout_ref,
    flat,
    xhat,
    rinv,
    normed,
    act,
    slope,
    branch,
    ext,
    x0,
    m6,
    weights,
    taps,
    conv,
    wide,
):
    joint = joint_weights(stem_ref, weights)
    spread_taps(table_ref, 0, taps)
    ext[:, 0:PADC] = west_ref[0:TH].astype(F32)
    ext[:, PADC : PADC + TW] = tile_ref[...].astype(F32)
    ext[:, PADC + TW :] = east_ref[0:TH].astype(F32)
    for row in range(0, TH, 4):
        at = slice(row, row + 4)
        both = jnp.dot(ext[at].reshape(4 * EW, LANES).astype(BF), joint, preferred_element_type=F32)
        mask = both[:, LANES:]
        m6[at] = mask.reshape(4, EW, LANES)
        x0[at] = (mask * both[:, :LANES]).astype(BF).astype(F32).reshape(4, EW, LANES)

    def conv_columns(block, _):
        start = block * 8
        rows = range(MID, MID + MID_ROWS)
        totals = conv_block(x0, (taps,), start + 2, rows, range(RIM, RIM + TH), lambda o, r, a, d: (0, a * 7 + d))
        for o in rows:
            conv[pl.ds((o - MID) * RW + start, 8), :] = totals[o]
        return 0

    for block in range(RW // 8):
        conv_columns(block, 0)
    count = MID_ROWS * RW
    spans = spans_of(count, 2 * RW)
    norm_rows(conv, xhat, rinv, normed, table_ref[49, 0:1, :], spans)
    wide[...] = jnp.dot(normed[...], win_ref[0], preferred_element_type=F32)
    gelu_rows(wide, act, slope, spans)
    branch[...] = jnp.dot(act[...], wout_ref[0], preferred_element_type=F32)
    for index, at in enumerate(spans):
        rows = slice(index * 2 + MID + 3 - RIM, index * 2 + MID + 5 - RIM)
        mask = m6[rows, RING_COL : RING_COL + RW, :]
        held = x0[rows, RING_COL : RING_COL + RW, :]
        value = mask * (held + table_ref[50, 0:1, :] * branch[at, :].reshape(2, RW, LANES))
        flat[at, :] = value.reshape(2 * RW, LANES).astype(BF)


def spread_taps(dw_ref, layer, taps, top=None):
    for t in range(49):
        row = dw_ref[t, layer : layer + 1, :]
        if top is not None:
            row = jnp.where(top, dw_ref[48 - t, layer : layer + 1, :], row)
        taps[t] = jnp.broadcast_to(row, (8, LANES))


def padded(flat, pad, width):
    rows = flat.shape[0] // width
    pad[:, 0:PADC, :] = jnp.zeros((rows, PADC, LANES), F32)
    pad[:, PADC + width :, :] = jnp.zeros((rows, pad.shape[1] - PADC - width, LANES), F32)
    for row in range(0, rows, 2):
        value = flat[row * width : (row + 2) * width, :].astype(F32)
        pad[row : row + 2, PADC : PADC + width, :] = value.reshape(2, width, LANES)


def main_kernel(
    rescale,
    top_ref,
    tile_ref,
    west_ref,
    east_ref,
    south_ref,
    north_ref,
    table_ref,
    stem_ref,
    win_ref,
    wout_ref,
    up_ref,
    mid_flat,
    mid_xhat,
    mid_rinv,
    mid_normed,
    mid_act,
    mid_slope,
    mid_branch,
    out_ref,
    packed_ref,
    sums,
    cells,
    flat0,
    flat1,
    grad0,
    grad1,
    carry0,
    x0,
    m6,
    x1,
    taps0,
    taps0n,
    pad1,
    g1,
    ext,
    weights,
    taps1,
    conv0,
    xhat0,
    rinv0,
    branch0,
    normed0,
    act0,
    slope0,
    conv1,
    xhat1,
    rinv1,
    branch1,
    normed1,
    act1,
    slope1,
    wide,
    thin,
    gpre,
):
    top = top_ref[0] == 1
    count0, count1 = RH * RW, TH * TW
    all0, all1 = spans_of(count0, 2 * RW), spans_of(count1, 2 * TW)
    middle = slice(MID * RW, (MID + MID_ROWS) * RW)
    rims = [slice(0, middle.start), slice(middle.stop, count0)]
    rim0 = [at for at in all0 if at.stop <= middle.start or at.start >= middle.stop]

    def from_middle(at):
        return middle.start <= at.start < middle.stop

    def pick(mid, ref, at):
        if from_middle(at):
            return mid[at.start - middle.start : at.stop - middle.start, :]
        return ref[at, :]

    unpack_rows(stem_ref.shape[0] + 1, south_ref, ext, 0)
    unpack_rows(stem_ref.shape[0] + 1, north_ref, ext, RIM + TH)
    ext[RIM : RIM + TH, PADC : PADC + TW] = tile_ref[...].astype(F32)
    ext[RIM : RIM + TH, 0:PADC] = west_ref[0:TH].astype(F32)
    ext[RIM : RIM + TH, PADC + TW :] = east_ref[0:TH].astype(F32)

    joint = joint_weights(stem_ref, weights)

    for index in range(EH // 4):
        at = slice(index * 4, index * 4 + 4)
        here = ext[at].reshape(4 * EW, LANES).astype(BF)
        cells[index * 4 * EW : (index + 1) * 4 * EW, :] = here
        both = jnp.dot(here, joint, preferred_element_type=F32)
        mask = both[:, LANES:]
        m6[at] = mask.reshape(4, EW, LANES)
        value = (mask * both[:, :LANES]).astype(BF)
        flat0[index * 4 * EW : (index + 1) * 4 * EW, :] = value
        x0[at] = value.astype(F32).reshape(4, EW, LANES)

    spread_taps(table_ref, 0, taps0)
    spread_taps(table_ref, 0, taps0n, top)
    spread_taps(table_ref, 1, taps1)

    north_at = 3 + TH

    def conv0_block(block, _):
        start = block * 8
        for rows in (range(0, MID), range(MID + MID_ROWS, north_at), range(north_at, RH)):
            totals = conv_block(
                x0,
                (taps0, taps0n),
                start + 2,
                rows,
                range(0, EH),
                lambda o, r, a, d: (1 if o >= north_at else 0, a * 7 + d),
            )
            for o in rows:
                conv0[pl.ds(o * RW + start, 8), :] = totals[o]
        return 0

    for block in range(RW // 8):
        conv0_block(block, 0)

    norm_rows(conv0, xhat0, rinv0, normed0, table_ref[49, 0:1, :], rim0)
    normed0[middle] = mid_normed[...]
    act0[middle] = mid_act[...]
    for at in rims:
        wide[at] = jnp.dot(normed0[at], win_ref[0], preferred_element_type=F32)
    gelu_rows(wide, act0, slope0, rim0)
    for at in rims:
        branch0[at] = jnp.dot(act0[at], wout_ref[0], preferred_element_type=F32)

    flat1[middle] = mid_flat[...]
    for index, at in enumerate(all0):
        if not from_middle(at):
            rows = slice(index * 2 + 3, index * 2 + 5)
            mask = m6[rows, RING_COL : RING_COL + RW, :]
            held = x0[rows, RING_COL : RING_COL + RW, :]
            value = mask * (held + table_ref[50, 0:1, :] * branch0[at, :].reshape(2, RW, LANES))
            flat1[at, :] = value.reshape(2 * RW, LANES).astype(BF)
        x1[index * 2 : index * 2 + 2] = flat1[at, :].astype(F32).reshape(2, RW, LANES)

    def conv1_block(block, _):
        start = block * 8
        for rows in (range(0, 16),):
            totals = conv_block(
                x1, (taps1,), start, rows, range(0, RH), lambda o, r, a, d: (0, a * 7 + d)
            )
            for o in rows:
                conv1[pl.ds(o * TW + start, 8), :] = totals[o]
        return 0

    for block in range(TW // 8):
        conv1_block(block, 0)
    norm_rows(conv1, xhat1, rinv1, normed1, table_ref[49, 1:2, :], all1)
    wide[0:count1] = jnp.dot(normed1[...], win_ref[1], preferred_element_type=F32)
    gelu_rows(wide, act1, slope1, all1)
    branch1[...] = jnp.dot(act1[...], wout_ref[1], preferred_element_type=F32)

    sums[...] = jnp.zeros_like(sums)
    g1[...] = jnp.zeros_like(g1)

    def folded(value):
        return jnp.sum(value.reshape(-1, 8, LANES), axis=0)

    def next1(index, at, total):
        rows = 2
        mask = m6[pl.ds(index * rows + RIM, rows), PADC : PADC + TW, :]
        held = x1[pl.ds(index * rows + 3, rows), 3 : 3 + TW, :]
        branch = branch1[at, :].reshape(rows, TW, LANES)
        out_ref[at, :] = (mask * (held + table_ref[50, 1:2, :] * branch)).astype(BF).reshape(rows * TW, LANES)
        masked = mask * (up_ref[at, :].astype(F32) * rescale).reshape(rows, TW, LANES)
        g1[pl.ds(index * rows + 3, rows), 3 : 3 + TW, :] = masked
        thin[at, :] = (masked * table_ref[50, 1:2, :]).reshape(rows * TW, LANES).astype(BF)
        return total + folded(masked * branch)

    total = chunks(all1, next1)(jnp.zeros((8, LANES), F32))
    sums[3:4, :] = jnp.sum(total, axis=0, keepdims=True)

    def grad_wout(layer, count, act):
        packed_ref[WOUT_ROW + 512 * layer : WOUT_ROW + 512 * layer + 512, :] = contract_rows(
            act[...], thin[0:count]
        ).astype(BF)

    def grad_pre(layer, count, slope):
        wide[0:count] = contract_cols(thin[0:count], wout_ref[layer])

        for at in spans_of(count, 16):
            gpre[at, :] = (wide[at, :] * slope(at)).astype(BF)

    def grad_win(layer, count, normed):
        gp = gpre[0:count]
        grad_in = contract_rows(normed[...], gp).astype(BF)
        for part in range(4):
            at = WIN_ROW + 512 * layer + 128 * part
            packed_ref[at : at + 128, :] = grad_in[:, 128 * part : 128 * part + 128]
        wide[0:count, 0:LANES] = contract_cols(gp, win_ref[layer])

    def grad_conv(layer, count, size, xhat, rinv, grad):
        gain = table_ref[49, layer : layer + 1, :]

        def step(index, at, total):
            gn = wide[at, 0:LANES]
            scaled = xhat(at)
            gx = gn * gain
            first = jnp.mean(gx, axis=-1, keepdims=True)
            second = jnp.mean(gx * scaled, axis=-1, keepdims=True)
            grad[at, :] = (rinv(at) * (gx - first - scaled * second)).astype(BF)
            return total + folded(gn * scaled)

        total = chunks(spans_of(count, size), step)(jnp.zeros((8, LANES), F32))
        sums[layer : layer + 1, :] = jnp.sum(total, axis=0, keepdims=True)

    grad_wout(1, count1, act1)
    grad_pre(1, count1, lambda at: slope1[at, :])
    grad_win(1, count1, normed1)
    grad_conv(1, count1, 2 * TW, lambda at: xhat1[at, :], lambda at: rinv1[at, :], grad1)
    padded(grad1, pad1, TW)

    def back1_block(block, _):
        start = block * 8
        for rows in (range(0, 22),):
            totals = conv_block(
                pad1, (taps1,), start + 2, rows, range(6, 6 + TH), lambda o, r, a, d: (0, 48 - (a * 7 + d))
            )
            for o in rows:
                g1[o, pl.ds(start, 8), :] += totals[o]
        return 0

    for block in range(RW // 8):
        back1_block(block, 0)

    def masked0(index, at, total):
        rows = pl.ds(index * 2, 2)
        masked = m6[pl.ds(index * 2 + 3, 2), RING_COL : RING_COL + RW, :] * g1[rows]
        flat = masked.reshape(2 * RW, LANES)
        carry0[at, :] = flat
        thin[at, :] = (flat * table_ref[50, 0:1, :]).astype(BF)
        return total + folded(flat * pick(mid_branch, branch0, at))

    total = chunks(all0, masked0)(jnp.zeros((8, LANES), F32))
    sums[2:3, :] = jnp.sum(total, axis=0, keepdims=True)
    grad_wout(0, count0, act0)
    grad_pre(0, count0, lambda at: pick(mid_slope, slope0, at))
    grad_win(0, count0, normed0)
    grad_conv(
        0,
        count0,
        2 * RW,
        lambda at: pick(mid_xhat, xhat0, at),
        lambda at: pick(mid_rinv, rinv0, at),
        grad0,
    )


def taps1_kernel(flat1, grad1, gk1, x1, pad1):
    for row in range(0, RH, 2):
        x1[row : row + 2] = flat1[row * RW : (row + 2) * RW, :].astype(F32).reshape(2, RW, LANES)
    padded(grad1, pad1, TW)
    gk1[...] = jnp.zeros_like(gk1)

    def kernel1_block(block, _):
        start = block * 8
        grads = [pad1[j, pl.ds(start + PADC, 8), :] for j in range(TH)]
        for d in range(7):
            column = [load_column(x1, r, start + d) for r in range(RH)]
            for a in range(7):
                total = gk1[a * 7 + d]
                for j in range(TH):
                    total = total + grads[j] * column[j + a]
                gk1[a * 7 + d] = total
        return 0

    for block in range(TW // 8):
        kernel1_block(block, 0)


def rest_kernel(
    top_ref,
    dw_ref,
    sums,
    cells,
    flat0,
    grad0,
    carry0,
    gk1,
    small_ref,
    small,
    x0,
    pad0,
    taps0,
    taps0n,
    h0,
    gk0,
    gk0n,
):
    top = top_ref[0] == 1
    north_at = 3 + TH
    levels_count = KERNEL_AT[0] - STEM_AT

    for row in range(0, EH, 4):
        x0[row : row + 4] = flat0[row * EW : (row + 4) * EW, :].astype(F32).reshape(4, EW, LANES)
    padded(grad0, pad0, RW)
    spread_taps(dw_ref, 0, taps0)
    spread_taps(dw_ref, 0, taps0n, top)

    gk0[...] = jnp.zeros_like(gk0)
    gk0n[...] = jnp.zeros_like(gk0n)

    def kernel0_block(block, _):
        start = pl.multiple_of(block * 8, 8)
        grads = [pad0[j, pl.ds(start + PADC, 8), :] for j in range(RH)]
        for d in range(7):
            column = [load_column(x0, r, start + 2 + d) for r in range(EH)]
            for a in range(7):
                total = gk0[a * 7 + d]
                for j in range(north_at):
                    total = total + grads[j] * column[j + a]
                gk0[a * 7 + d] = total
                total = gk0n[a * 7 + d]
                for j in range(north_at, RH):
                    total = total + grads[j] * column[j + a]
                gk0n[a * 7 + d] = total
        return 0

    lax.fori_loop(0, RW // 8, kernel0_block, 0)
    for t in range(49):
        north = jnp.where(top, gk0n[48 - t], gk0n[t])
        small[KERNEL_AT[0] + t : KERNEL_AT[0] + t + 1, :] = jnp.sum(gk0[t] + north, axis=0, keepdims=True)
        small[KERNEL_AT[1] + t : KERNEL_AT[1] + t + 1, :] = jnp.sum(gk1[t], axis=0, keepdims=True)

    def back0_block(block, _):
        start = pl.multiple_of(block * 8, 8)
        for rows in (range(0, 14), range(14, 28)):
            totals = conv_block(
                pad0,
                (taps0, taps0n),
                start,
                rows,
                range(6, 6 + RH),
                lambda o, r, a, d: (1 if r - 6 >= north_at else 0, 48 - (a * 7 + d)),
            )
            for o in rows:
                h0[o, pl.ds(start, 8), :] = totals[o]
        return 0

    lax.fori_loop(0, EW // 8, back0_block, 0)
    for row in range(0, RH, 2):
        h0[row + 3 : row + 5, RING_COL : RING_COL + RW, :] += carry0[
            row * RW : (row + 2) * RW, :
        ].reshape(2, RW, LANES)
    rows = lax.broadcasted_iota(jnp.int32, (LANES, LANES), 0)
    mask = jnp.dot(cells[...], (rows == levels_count).astype(BF), preferred_element_type=F32)
    stem_side = (mask * h0[...].reshape(EH * EW, LANES)).astype(BF)
    stem_grad = contract_rows(cells[...], stem_side)
    small[STEM_AT : KERNEL_AT[0], :] = stem_grad[0:levels_count, :]
    small[GAIN_AT : GAIN_AT + 4, :] = sums[0:4, :]
    small[GAIN_AT + 4 :, :] = jnp.zeros((SMALL - GAIN_AT - 4, LANES), F32)
    small_ref[...] = small[...].astype(BF)


def unpack_kernel(
    order_ref,
    pieces_ref,
    mine_ref,
    other_ref,
    stem_out,
    kernel_out,
    gain_out,
    win_out,
    wout_out,
    scale_out,
    stem_ref,
    kernel_ref,
    gain_ref,
    win_ref,
    wout_ref,
    scale_ref,
    small,
    sent,
):
    count, size = pieces_ref.shape[0], pieces_ref.shape[1]
    stores = [
        pltpu.make_async_copy(source, target, sent.at[index])
        for index, (source, target) in enumerate(
            [(win_ref.at[layer], win_out.at[layer]) for layer in range(2)]
            + [(wout_ref.at[layer], wout_out.at[layer]) for layer in range(2)]
            + [(stem_ref, stem_out), (kernel_ref, kernel_out), (gain_ref, gain_out), (scale_ref, scale_out)]
        )
    ]

    def rows(at, length):
        return [
            pieces_ref[order_ref[index]].astype(F32) if count > 1 else pieces_ref[0, index * 128 : index * 128 + 128].astype(F32)
            for index in range(at // 128, (at + length) // 128)
        ]

    for layer in range(2):
        for part, block in enumerate(rows(WIN_ROW + 512 * layer, 512)):
            win_ref[layer, :, 128 * part : 128 * part + 128] = block
        stores[layer].start()
    for layer in range(2):
        for part, block in enumerate(rows(WOUT_ROW + 512 * layer, 512)):
            wout_ref[layer, 128 * part : 128 * part + 128, :] = block
        stores[2 + layer].start()
    places, size = mine_ref.shape[0], mine_ref.shape[1]
    for index in range(places):
        at = order_ref[count + index]
        small[index * size : (index + 1) * size, :] = mine_ref[at].astype(F32) + other_ref[at].astype(F32)
    for layer in range(2):
        kernel_ref[:, layer, :] = small[KERNEL_AT[layer] : KERNEL_AT[layer] + 49, :]
    stem_ref[...] = small[STEM_AT : STEM_AT + stem_ref.shape[0], :]
    gain_ref[...] = small[GAIN_AT : GAIN_AT + 2, :]
    scale_ref[...] = small[SCALE_AT : SCALE_AT + 2, :]
    for store in stores[4:]:
        store.start()
    for store in stores:
        store.wait()


def permuted(value, pairs):
    return lax.ppermute(value, "gy", pairs)


def crossed(value, bits):
    return permuted(value, [(i, i ^ bits) for i in range(lax.axis_size("gy"))])


def summed_pieces(packed, top, rest):
    size = lax.axis_size("gy")
    if size != 16:
        bulk, small = lax.psum((packed.astype(F32), rest(top).astype(F32)), "gy")
        small = small.astype(BF)[None]
        return bulk.astype(BF)[None], small, jnp.zeros_like(small), jnp.zeros((2,), jnp.int32)
    me = lax.axis_index("gy")
    core, side, deep = me & 1, (me >> 1) & 1, me >> 2

    def halves(value, bit):
        half = value.shape[0] // 2
        low, high = value[:half], value[half:]
        return jnp.where(bit == 0, low, high), jnp.where(bit == 0, high, low)

    keep, send = halves(packed, core)
    came = crossed(send, 1)
    came, top = lax.optimization_barrier((came, top))
    small = rest(top)
    keep, send = halves(keep.astype(F32) + came.astype(F32), side)
    total = keep + crossed(send.astype(BF), 2).astype(F32)
    quarter = total.shape[0] // 4
    part = small.shape[0] // 4

    def shard(step):
        at = deep ^ step
        return jnp.concatenate(
            [
                lax.dynamic_slice_in_dim(total, at * quarter, quarter, 0).astype(BF),
                lax.dynamic_slice_in_dim(small, at * part, part, 0),
            ],
            axis=0,
        )

    arrived = [crossed(shard(step), 4 * step) for step in STEPS]
    bulk = lax.dynamic_slice_in_dim(total, deep * quarter, quarter, 0)
    rest_sum = lax.dynamic_slice_in_dim(small, deep * part, part, 0).astype(F32)
    for other in arrived:
        bulk = bulk + other[:quarter].astype(F32)
        rest_sum = rest_sum + other[quarter:].astype(F32)
    mine = jnp.concatenate([bulk.astype(BF), rest_sum.astype(BF)], axis=0)
    pieces = jnp.stack([mine] + [crossed(mine, 4 * step) for step in STEPS][::-1])
    came = crossed(pieces, 2)
    bulk = jnp.concatenate([pieces[:, :quarter], came[:, :quarter]], axis=0)
    small = (pieces[:, quarter:].astype(F32) + came[:, quarter:].astype(F32)).astype(BF)
    rows = bulk.shape[0] * quarter
    joined = jnp.concatenate([bulk.reshape(rows, LANES), small.reshape(4 * part, LANES)], axis=0)
    came = crossed(joined, 1)
    bulk = jnp.concatenate([bulk, came[:rows].reshape(bulk.shape)], axis=0)
    mixed = ((core << 3) | (side << 2) | deep).astype(jnp.int32)
    order = jnp.arange(20, dtype=jnp.int32) & 15
    order = order ^ jnp.where(jnp.arange(20) < 16, mixed, deep.astype(jnp.int32))
    return bulk, small, came[rows:].reshape(small.shape), order


def shards(levels, ocean, stem, dw_kernel, ln_gain, w_in, w_out, layer_scale, upstream):
    size = lax.axis_size("gy")
    rows = size // TX
    me = lax.axis_index("gy")
    is_top = me // TX == rows - 1
    count = levels.shape[2]
    top = is_top.astype(jnp.int32)[None]
    table = jnp.concatenate([dw_kernel.transpose(1, 0, 2), ln_gain[None], layer_scale[None]])
    tile, to_west, to_east, folded = pl.pallas_call(
        prepare_kernel,
        out_shape=[
            jax.ShapeDtypeStruct((TH, TW, LANES), BF),
            jax.ShapeDtypeStruct((TH + RIM, PADC, LANES), BF),
            jax.ShapeDtypeStruct((TH + RIM, PADC, LANES), BF),
            jax.ShapeDtypeStruct((RIM, TW, LANES), BF),
        ],
        in_specs=vmem(2),
        out_specs=vmem(4),
        scratch_shapes=[pltpu.VMEM((LANES, count), F32)],
        compiler_params=pltpu.CompilerParams(vmem_limit_bytes=4 << 20),
    )(levels[0], ocean.astype(F32))

    def column_pairs(step):
        return [(i, i // TX * TX + (i % TX + step) % TX) for i in range(size)]

    west = permuted(to_east, column_pairs(1))
    east = permuted(to_west, column_pairs(-1))

    lower, upper, folded = pl.pallas_call(
        functools.partial(pack_kernel, stem.shape[0] + 1),
        out_shape=[jax.ShapeDtypeStruct((RIM * TW, LANES), BF)] * 3,
        in_specs=vmem(4),
        out_specs=vmem(3),
        compiler_params=pltpu.CompilerParams(vmem_limit_bytes=4 << 20),
    )(tile, west, east, folded)
    folded = permuted(folded, [(i, i // TX * TX + TX - 1 - i % TX) for i in range(size - TX, size)])
    if rows == 2:
        north = permuted(jnp.where(is_top, lower, upper), [(i, (i + TX) % size) for i in range(size)])
        south = jnp.where(is_top, north, jnp.zeros_like(north))
    else:
        south = permuted(upper, [(i, i + TX) for i in range(size - TX)])
        north = permuted(lower, [(i + TX, i) for i in range(size - TX)])
    north = jnp.where(is_top, folded, north)

    def scratch(*shape, dtype=F32):
        return pltpu.VMEM(shape, dtype)

    count0 = RH * RW
    hidden = w_in.shape[2]
    count_mid = MID_ROWS * RW
    mid_shapes = [
        jax.ShapeDtypeStruct((count_mid, LANES), BF),
        jax.ShapeDtypeStruct((count_mid, LANES), F32),
        jax.ShapeDtypeStruct((count_mid, LANES), F32),
        jax.ShapeDtypeStruct((count_mid, LANES), BF),
        jax.ShapeDtypeStruct((count_mid, hidden), BF),
        jax.ShapeDtypeStruct((count_mid, hidden), F32),
        jax.ShapeDtypeStruct((count_mid, LANES), F32),
    ]
    middle = pl.pallas_call(
        middle_kernel,
        out_shape=mid_shapes,
        in_specs=vmem(7),
        out_specs=vmem(7),
        scratch_shapes=[
            scratch(TH, EW, LANES),
            scratch(TH, EW, LANES),
            scratch(TH, EW, LANES),
            scratch(LANES, 2 * LANES),
            scratch(49, 8, LANES),
            scratch(count_mid, LANES),
            scratch(count_mid, hidden),
        ],
        compiler_params=pltpu.CompilerParams(vmem_limit_bytes=10 << 20),
        cost_estimate=pl.CostEstimate(flops=4_000_000_000, bytes_accessed=3_000_000, transcendentals=0),
    )(tile, west, east, table, stem, w_in, w_out)

    ring_shapes = [
        jax.ShapeDtypeStruct((8, LANES), F32),
        jax.ShapeDtypeStruct((EH * EW, LANES), BF),
        jax.ShapeDtypeStruct((EH * EW, LANES), BF),
        jax.ShapeDtypeStruct((RH * RW, LANES), BF),
        jax.ShapeDtypeStruct((RH * RW, LANES), BF),
        jax.ShapeDtypeStruct((TH * TW, LANES), BF),
        jax.ShapeDtypeStruct((RH * RW, LANES), F32),
    ]
    result, packed, *ring = pl.pallas_call(
        functools.partial(main_kernel, 1.0 / math.sqrt(size * count)),
        out_shape=[
            jax.ShapeDtypeStruct((count, LANES), BF),
            jax.ShapeDtypeStruct((BULK, LANES), BF),
        ]
        + ring_shapes,
        in_specs=[smem()] + vmem(17),
        out_specs=vmem(9),
        scratch_shapes=[
            scratch(EH, EW, LANES),
            scratch(EH, EW, LANES),
            scratch(RH, RW, LANES),
            scratch(49, 8, LANES),
            scratch(49, 8, LANES),
            scratch(TH, EW, LANES),
            scratch(RH, RW, LANES),
            scratch(EH, EW, LANES),
            scratch(LANES, 2 * LANES),
            scratch(49, 8, LANES),
            scratch(count0, LANES),
            scratch(count0, LANES),
            scratch(count0, LANES),
            scratch(count0, LANES),
            scratch(count0, LANES, dtype=BF),
            scratch(count0, hidden, dtype=BF),
            scratch(count0, hidden),
            scratch(count, LANES),
            scratch(count, LANES),
            scratch(count, LANES),
            scratch(count, LANES),
            scratch(count, LANES, dtype=BF),
            scratch(count, hidden, dtype=BF),
            scratch(count, hidden),
            scratch(count0, hidden),
            scratch(count0, LANES, dtype=BF),
            scratch(count0, hidden, dtype=BF),
        ],
        compiler_params=pltpu.CompilerParams(vmem_limit_bytes=20 << 20),
    )(
        top,
        tile,
        west,
        east,
        south,
        north,
        table,
        stem,
        w_in,
        w_out,
        upstream[0],
        *middle,
    )

    sums, cells, flat0, flat1, grad0, grad1, carry0 = ring
    grad_taps1 = pl.pallas_call(
        taps1_kernel,
        out_shape=jax.ShapeDtypeStruct((49, 8, LANES), F32),
        in_specs=vmem(2),
        out_specs=vmem(1)[0],
        scratch_shapes=[scratch(RH, RW, LANES), scratch(TH, EW, LANES)],
        compiler_params=pltpu.CompilerParams(vmem_limit_bytes=6 << 20),
        cost_estimate=pl.CostEstimate(flops=2_000_000_000, bytes_accessed=500_000, transcendentals=0),
    )(flat1, grad1)

    def rest(top):
        return pl.pallas_call(
            rest_kernel,
            out_shape=jax.ShapeDtypeStruct((SMALL, LANES), BF),
            in_specs=[smem()] + vmem(7),
            out_specs=vmem(1)[0],
            scratch_shapes=[
                scratch(SMALL, LANES),
                scratch(EH, EW, LANES),
                scratch(RH, EW + 8, LANES),
                scratch(49, 8, LANES),
                scratch(49, 8, LANES),
                scratch(EH, EW, LANES),
                scratch(49, 8, LANES),
                scratch(49, 8, LANES),
            ],
            compiler_params=pltpu.CompilerParams(vmem_limit_bytes=10 << 20),
            cost_estimate=pl.CostEstimate(flops=10_000_000_000, bytes_accessed=4_000_000, transcendentals=0),
        )(top, table, sums, cells, flat0, grad0, carry0, grad_taps1)

    pieces, mine, other, order = summed_pieces(packed, top, rest)
    shapes = [array.shape for array in (stem, dw_kernel, ln_gain, w_in, w_out, layer_scale)]
    shapes[1] = (shapes[1][1], shapes[1][0], shapes[1][2])
    grads = pl.pallas_call(
        unpack_kernel,
        out_shape=[jax.ShapeDtypeStruct(shape, F32) for shape in shapes],
        in_specs=[smem()] + vmem(3),
        out_specs=[pl.BlockSpec(memory_space=pltpu.HBM)] * 6,
        scratch_shapes=[scratch(*shape) for shape in shapes]
        + [scratch(SMALL, LANES), pltpu.SemaphoreType.DMA((8,))],
        compiler_params=pltpu.CompilerParams(vmem_limit_bytes=8 << 20),
    )(order, pieces, mine, other)
    grads = list(grads)
    grads[1] = grads[1].transpose(1, 0, 2)
    return (result[None], *grads)


def solution(mesh):
    in_specs = (
        P(("groups", "gy"), None, None),
        P(("groups", "gy"), None),
        P(),
        P(),
        P(),
        P(),
        P(),
        P(),
        P(("groups", "gy"), None, None),
    )
    out_specs = (
        P(("groups", "gy"), None, None),
        P("groups", None),
        P("groups", None, None),
        P("groups", None),
        P("groups", None, None),
        P("groups", None, None),
        P("groups", None),
    )
    return jax.shard_map(shards, mesh=mesh, in_specs=in_specs, out_specs=out_specs, check_vma=False)
```

```python
import functools
import math

import jax
import jax.numpy as jnp
from jax import lax
from jax.experimental import pallas as pl
from jax.experimental.pallas import tpu as pltpu
from jax.sharding import PartitionSpec as P

TH = 16
TW = 32
TX = 8
LANES = 128

RIM = 6
PADC = 8
EH, EW = TH + 2 * RIM, TW + 2 * PADC
RH, RW = TH + 6, 40
RING_COL = 5
MID, MID_ROWS = 6, 10

C0 = 0.7978845608028654
C1 = 0.7978845608028654 * 0.044715
NORM_STABILIZER = 1e-06

WIN_ROW, WOUT_ROW, BULK = 0, 1024, 2048
STEM_AT, KERNEL_AT, GAIN_AT, SCALE_AT = 0, (75, 124), 173, 175
SMALL = 192

STEPS = (3, 2, 1)

BF = jnp.bfloat16
F32 = jnp.float32


def vmem(count):
    return [pl.BlockSpec(memory_space=pltpu.VMEM)] * count


def smem():
    return pl.BlockSpec(memory_space=pltpu.SMEM)


def contract_rows(left, right):
    return lax.dot_general(left, right, (((0,), (0,)), ((), ())), preferred_element_type=F32)


def contract_cols(left, right):
    return lax.dot_general(left, right, (((1,), (1,)), ((), ())), preferred_element_type=F32)


def prepare_kernel(levels_ref, ocean_ref, tile_ref, west_ref, east_ref, fold_ref, stage):
    count, cells = levels_ref.shape
    stage[...] = jnp.zeros_like(stage)
    stage[0:count, :] = levels_ref[...].astype(F32)
    stage[count : count + 1, :] = ocean_ref[...]
    rows = lax.broadcasted_iota(jnp.int32, (LANES, LANES), 0)
    cols = lax.broadcasted_iota(jnp.int32, (LANES, LANES), 1)
    eye = (rows == cols).astype(BF)
    turned = contract_rows(stage[...].astype(BF), eye)
    side = RIM * TW
    rows = lax.broadcasted_iota(jnp.int32, (side, side), 0)
    cols = lax.broadcasted_iota(jnp.int32, (side, side), 1)
    swap = (rows + cols == side - 1).astype(BF)
    fold = jnp.dot(swap, turned[cells - side :].astype(BF), preferred_element_type=F32).reshape(RIM, TW, LANES)
    tile = turned.reshape(TH, TW, LANES)
    tile_ref[...] = tile.astype(BF)
    fold_ref[...] = fold.astype(BF)
    west_ref[0:TH] = tile[:, 0:PADC].astype(BF)
    west_ref[TH:] = fold[:, TW - PADC :].astype(BF)
    east_ref[0:TH] = tile[:, TW - PADC :].astype(BF)
    east_ref[TH:] = fold[:, 0:PADC].astype(BF)


def pack_kernel(used, tile_ref, west_ref, east_ref, fold_ref, lower_ref, upper_ref, folded_ref):
    spare, halo = LANES - used, RIM * PADC
    over = used - spare

    def kept(value, low, high):
        lane = lax.broadcasted_iota(jnp.int32, value.shape, 1)
        return jnp.where((lane >= low) & (lane < high), value, 0.0)

    def store(ref, own, first, last):
        own = own.astype(F32).reshape(RIM * TW, LANES)
        first, last = [value.astype(F32).reshape(halo, LANES) for value in (first, last)]
        extra = [
            kept(pltpu.roll(first, used, 1), used, LANES),
            kept(pltpu.roll(last, used, 1), used, LANES),
            kept(pltpu.roll(first, used - spare, 1), used, used + over)
            + kept(pltpu.roll(last, used - spare + over, 1), used + over, used + 2 * over),
        ]
        for index, value in enumerate(extra):
            at = slice(index * halo, (index + 1) * halo)
            ref[at] = (own[at] + value).astype(BF)
        ref[3 * halo :] = own[3 * halo :].astype(BF)

    for ref, at in ((lower_ref, slice(0, RIM)), (upper_ref, slice(TH - RIM, TH))):
        store(ref, tile_ref[at], west_ref[at], east_ref[at])
    store(folded_ref, fold_ref[...], east_ref[TH:], west_ref[TH:])


def unpack_rows(used, packed_ref, ext, at):
    spare, halo = LANES - used, RIM * PADC
    over = used - spare
    rows = packed_ref[...].astype(F32)
    lane = lax.broadcasted_iota(jnp.int32, (halo, LANES), 1)
    own = jnp.where(lax.broadcasted_iota(jnp.int32, rows.shape, 1) < used, rows, 0.0)
    ext[at : at + RIM, PADC : PADC + TW] = own.reshape(RIM, TW, LANES)
    tail = rows[2 * halo : 3 * halo]
    for index, (start, shift) in enumerate(((0, used - spare), (PADC + TW, used - spare + over))):
        front = pltpu.roll(rows[index * halo : (index + 1) * halo], LANES - used, 1)
        back = pltpu.roll(tail, LANES - shift, 1)
        value = jnp.where(lane < spare, front, jnp.where(lane < used, back, 0.0))
        ext[at : at + RIM, start : start + PADC] = value.reshape(RIM, PADC, LANES)


def load_column(ref, row, start):
    return ref[row, pl.ds(start, 8), :]


def conv_block(ref, taps, start, out_rows, in_rows, taps_of):
    totals = {o: None for o in out_rows}
    needed = sorted({o + a for o in out_rows for a in range(7) if o + a in in_rows})
    for d in range(7):
        column = {r: load_column(ref, r - in_rows.start, start + d) for r in needed}
        for a in range(7):
            held = {}
            for o in out_rows:
                r = o + a
                if r not in column:
                    continue
                which, index = taps_of(o, r, a, d)
                if (which, index) not in held:
                    held[(which, index)] = taps[which][index]
                term = held[(which, index)] * column[r]
                totals[o] = term if totals[o] is None else totals[o] + term
    return totals


def chunks(spans, body):
    def run(carry):
        for at in spans:
            carry = body(at.start // (at.stop - at.start), at, carry)
        return carry

    return run


def spans_of(count, size):
    return [slice(at, at + size) for at in range(0, count, size)]


def norm_rows(conv, xhat, rinv, normed, gain, spans):
    for at in spans:
        values = conv[at, :]
        average = jnp.mean(values, axis=-1, keepdims=True)
        centered = values - average
        inverse = lax.rsqrt(jnp.mean(centered * centered, axis=-1, keepdims=True) + NORM_STABILIZER)
        scaled = centered * inverse
        xhat[at, :] = scaled
        rinv[at, :] = jnp.broadcast_to(inverse, values.shape)
        normed[at, :] = (scaled * gain).astype(BF)


def gelu_rows(pre, act, slope, spans):
    for at in spans:
        for start in range(at.start, at.stop, 16):
            here = slice(start, start + 16)
            v = pre[here, :]
            square = v * v
            inner = v * (C0 + C1 * square)
            half = 0.5 * jnp.tanh(inner) + 0.5
            active = v * half
            act[here, :] = active.astype(BF)
            slope[here, :] = half + active * (1.0 - half) * (2.0 * C0 + (6.0 * C1) * square)


def joint_weights(stem_ref, weights):
    count = stem_ref.shape[0]
    weights[...] = jnp.zeros_like(weights)
    weights[0:count, 0:LANES] = stem_ref[...].astype(F32)
    weights[count : count + 1, LANES:] = jnp.ones((1, LANES), F32)
    return weights[...].astype(BF)


def middle_kernel(
    tile_ref,
    west_ref,
    east_ref,
    table_ref,
    stem_ref,
    win_ref,
    wout_ref,
    flat,
    xhat,
    rinv,
    normed,
    act,
    slope,
    branch,
    ext,
    x0,
    m6,
    weights,
    taps,
    conv,
    wide,
):
    joint = joint_weights(stem_ref, weights)
    spread_taps(table_ref, 0, taps)
    ext[:, 0:PADC] = west_ref[0:TH].astype(F32)
    ext[:, PADC : PADC + TW] = tile_ref[...].astype(F32)
    ext[:, PADC + TW :] = east_ref[0:TH].astype(F32)
    for row in range(0, TH, 4):
        at = slice(row, row + 4)
        both = jnp.dot(ext[at].reshape(4 * EW, LANES).astype(BF), joint, preferred_element_type=F32)
        mask = both[:, LANES:]
        m6[at] = mask.reshape(4, EW, LANES)
        x0[at] = (mask * both[:, :LANES]).astype(BF).astype(F32).reshape(4, EW, LANES)

    def conv_columns(block, _):
        start = block * 8
        rows = range(MID, MID + MID_ROWS)
        totals = conv_block(x0, (taps,), start + 2, rows, range(RIM, RIM + TH), lambda o, r, a, d: (0, a * 7 + d))
        for o in rows:
            conv[pl.ds((o - MID) * RW + start, 8), :] = totals[o]
        return 0

    for block in range(RW // 8):
        conv_columns(block, 0)
    count = MID_ROWS * RW
    spans = spans_of(count, 2 * RW)
    norm_rows(conv, xhat, rinv, normed, table_ref[49, 0:1, :], spans)
    wide[...] = jnp.dot(normed[...], win_ref[0], preferred_element_type=F32)
    gelu_rows(wide, act, slope, spans)
    branch[...] = jnp.dot(act[...], wout_ref[0], preferred_element_type=F32)
    for index, at in enumerate(spans):
        rows = slice(index * 2 + MID + 3 - RIM, index * 2 + MID + 5 - RIM)
        mask = m6[rows, RING_COL : RING_COL + RW, :]
        held = x0[rows, RING_COL : RING_COL + RW, :]
        value = mask * (held + table_ref[50, 0:1, :] * branch[at, :].reshape(2, RW, LANES))
        flat[at, :] = value.reshape(2 * RW, LANES).astype(BF)


def spread_taps(dw_ref, layer, taps, top=None):
    for t in range(49):
        row = dw_ref[t, layer : layer + 1, :]
        if top is not None:
            row = jnp.where(top, dw_ref[48 - t, layer : layer + 1, :], row)
        taps[t] = jnp.broadcast_to(row, (8, LANES))


def padded(flat, pad, width):
    rows = flat.shape[0] // width
    pad[:, 0:PADC, :] = jnp.zeros((rows, PADC, LANES), F32)
    pad[:, PADC + width :, :] = jnp.zeros((rows, pad.shape[1] - PADC - width, LANES), F32)
    for row in range(0, rows, 2):
        value = flat[row * width : (row + 2) * width, :].astype(F32)
        pad[row : row + 2, PADC : PADC + width, :] = value.reshape(2, width, LANES)


def main_kernel(
    rescale,
    top_ref,
    tile_ref,
    west_ref,
    east_ref,
    south_ref,
    north_ref,
    table_ref,
    stem_ref,
    win_ref,
    wout_ref,
    up_ref,
    mid_flat,
    mid_xhat,
    mid_rinv,
    mid_normed,
    mid_act,
    mid_slope,
    mid_branch,
    out_ref,
    packed_ref,
    sums,
    cells,
    flat0,
    flat1,
    grad0,
    grad1,
    carry0,
    x0,
    m6,
    x1,
    taps0,
    taps0n,
    pad1,
    g1,
    ext,
    weights,
    taps1,
    conv0,
    xhat0,
    rinv0,
    branch0,
    normed0,
    act0,
    slope0,
    conv1,
    xhat1,
    rinv1,
    branch1,
    normed1,
    act1,
    slope1,
    wide,
    thin,
    gpre,
):
    top = top_ref[0] == 1
    count0, count1 = RH * RW, TH * TW
    all0, all1 = spans_of(count0, 2 * RW), spans_of(count1, 2 * TW)
    middle = slice(MID * RW, (MID + MID_ROWS) * RW)
    rims = [slice(0, middle.start), slice(middle.stop, count0)]
    rim0 = [at for at in all0 if at.stop <= middle.start or at.start >= middle.stop]

    def from_middle(at):
        return middle.start <= at.start < middle.stop

    def pick(mid, ref, at):
        if from_middle(at):
            return mid[at.start - middle.start : at.stop - middle.start, :]
        return ref[at, :]

    unpack_rows(stem_ref.shape[0] + 1, south_ref, ext, 0)
    unpack_rows(stem_ref.shape[0] + 1, north_ref, ext, RIM + TH)
    ext[RIM : RIM + TH, PADC : PADC + TW] = tile_ref[...].astype(F32)
    ext[RIM : RIM + TH, 0:PADC] = west_ref[0:TH].astype(F32)
    ext[RIM : RIM + TH, PADC + TW :] = east_ref[0:TH].astype(F32)

    joint = joint_weights(stem_ref, weights)

    for index in range(EH // 4):
        at = slice(index * 4, index * 4 + 4)
        here = ext[at].reshape(4 * EW, LANES).astype(BF)
        cells[index * 4 * EW : (index + 1) * 4 * EW, :] = here
        both = jnp.dot(here, joint, preferred_element_type=F32)
        mask = both[:, LANES:]
        m6[at] = mask.reshape(4, EW, LANES)
        value = (mask * both[:, :LANES]).astype(BF)
        flat0[index * 4 * EW : (index + 1) * 4 * EW, :] = value
        x0[at] = value.astype(F32).reshape(4, EW, LANES)

    spread_taps(table_ref, 0, taps0)
    spread_taps(table_ref, 0, taps0n, top)
    spread_taps(table_ref, 1, taps1)

    north_at = 3 + TH

    def conv0_block(block, _):
        start = block * 8
        for rows in (range(0, MID), range(MID + MID_ROWS, north_at), range(north_at, RH)):
            totals = conv_block(
                x0,
                (taps0, taps0n),
                start + 2,
                rows,
                range(0, EH),
                lambda o, r, a, d: (1 if o >= north_at else 0, a * 7 + d),
            )
            for o in rows:
                conv0[pl.ds(o * RW + start, 8), :] = totals[o]
        return 0

    for block in range(RW // 8):
        conv0_block(block, 0)

    norm_rows(conv0, xhat0, rinv0, normed0, table_ref[49, 0:1, :], rim0)
    normed0[middle] = mid_normed[...]
    act0[middle] = mid_act[...]
    for at in rims:
        wide[at] = jnp.dot(normed0[at], win_ref[0], preferred_element_type=F32)
    gelu_rows(wide, act0, slope0, rim0)
    for at in rims:
        branch0[at] = jnp.dot(act0[at], wout_ref[0], preferred_element_type=F32)

    flat1[middle] = mid_flat[...]
    for index, at in enumerate(all0):
        if not from_middle(at):
            rows = slice(index * 2 + 3, index * 2 + 5)
            mask = m6[rows, RING_COL : RING_COL + RW, :]
            held = x0[rows, RING_COL : RING_COL + RW, :]
            value = mask * (held + table_ref[50, 0:1, :] * branch0[at, :].reshape(2, RW, LANES))
            flat1[at, :] = value.reshape(2 * RW, LANES).astype(BF)
        x1[index * 2 : index * 2 + 2] = flat1[at, :].astype(F32).reshape(2, RW, LANES)

    def conv1_block(block, _):
        start = block * 8
        for rows in (range(0, 16),):
            totals = conv_block(
                x1, (taps1,), start, rows, range(0, RH), lambda o, r, a, d: (0, a * 7 + d)
            )
            for o in rows:
                conv1[pl.ds(o * TW + start, 8), :] = totals[o]
        return 0

    for block in range(TW // 8):
        conv1_block(block, 0)
    norm_rows(conv1, xhat1, rinv1, normed1, table_ref[49, 1:2, :], all1)
    wide[0:count1] = jnp.dot(normed1[...], win_ref[1], preferred_element_type=F32)
    gelu_rows(wide, act1, slope1, all1)
    branch1[...] = jnp.dot(act1[...], wout_ref[1], preferred_element_type=F32)

    sums[...] = jnp.zeros_like(sums)
    g1[...] = jnp.zeros_like(g1)

    def folded(value):
        return jnp.sum(value.reshape(-1, 8, LANES), axis=0)

    def next1(index, at, total):
        rows = 2
        mask = m6[pl.ds(index * rows + RIM, rows), PADC : PADC + TW, :]
        held = x1[pl.ds(index * rows + 3, rows), 3 : 3 + TW, :]
        branch = branch1[at, :].reshape(rows, TW, LANES)
        out_ref[at, :] = (mask * (held + table_ref[50, 1:2, :] * branch)).astype(BF).reshape(rows * TW, LANES)
        masked = mask * (up_ref[at, :].astype(F32) * rescale).reshape(rows, TW, LANES)
        g1[pl.ds(index * rows + 3, rows), 3 : 3 + TW, :] = masked
        thin[at, :] = (masked * table_ref[50, 1:2, :]).reshape(rows * TW, LANES).astype(BF)
        return total + folded(masked * branch)

    total = chunks(all1, next1)(jnp.zeros((8, LANES), F32))
    sums[3:4, :] = jnp.sum(total, axis=0, keepdims=True)

    def grad_wout(layer, count, act):
        packed_ref[WOUT_ROW + 512 * layer : WOUT_ROW + 512 * layer + 512, :] = contract_rows(
            act[...], thin[0:count]
        ).astype(BF)

    def grad_pre(layer, count, slope):
        wide[0:count] = contract_cols(thin[0:count], wout_ref[layer])

        for at in spans_of(count, 16):
            gpre[at, :] = (wide[at, :] * slope(at)).astype(BF)

    def grad_win(layer, count, normed):
        gp = gpre[0:count]
        grad_in = contract_rows(normed[...], gp).astype(BF)
        for part in range(4):
            at = WIN_ROW + 512 * layer + 128 * part
            packed_ref[at : at + 128, :] = grad_in[:, 128 * part : 128 * part + 128]
        wide[0:count, 0:LANES] = contract_cols(gp, win_ref[layer])

    def grad_conv(layer, count, size, xhat, rinv, grad):
        gain = table_ref[49, layer : layer + 1, :]

        def step(index, at, total):
            gn = wide[at, 0:LANES]
            scaled = xhat(at)
            gx = gn * gain
            first = jnp.mean(gx, axis=-1, keepdims=True)
            second = jnp.mean(gx * scaled, axis=-1, keepdims=True)
            grad[at, :] = (rinv(at) * (gx - first - scaled * second)).astype(BF)
            return total + folded(gn * scaled)

        total = chunks(spans_of(count, size), step)(jnp.zeros((8, LANES), F32))
        sums[layer : layer + 1, :] = jnp.sum(total, axis=0, keepdims=True)

    grad_wout(1, count1, act1)
    grad_pre(1, count1, lambda at: slope1[at, :])
    grad_win(1, count1, normed1)
    grad_conv(1, count1, 2 * TW, lambda at: xhat1[at, :], lambda at: rinv1[at, :], grad1)
    padded(grad1, pad1, TW)

    def back1_block(block, _):
        start = block * 8
        for rows in (range(0, 22),):
            totals = conv_block(
                pad1, (taps1,), start + 2, rows, range(6, 6 + TH), lambda o, r, a, d: (0, 48 - (a * 7 + d))
            )
            for o in rows:
                g1[o, pl.ds(start, 8), :] += totals[o]
        return 0

    for block in range(RW // 8):
        back1_block(block, 0)

    def masked0(index, at, total):
        rows = pl.ds(index * 2, 2)
        masked = m6[pl.ds(index * 2 + 3, 2), RING_COL : RING_COL + RW, :] * g1[rows]
        flat = masked.reshape(2 * RW, LANES)
        carry0[at, :] = flat
        thin[at, :] = (flat * table_ref[50, 0:1, :]).astype(BF)
        return total + folded(flat * pick(mid_branch, branch0, at))

    total = chunks(all0, masked0)(jnp.zeros((8, LANES), F32))
    sums[2:3, :] = jnp.sum(total, axis=0, keepdims=True)
    grad_wout(0, count0, act0)
    grad_pre(0, count0, lambda at: pick(mid_slope, slope0, at))
    grad_win(0, count0, normed0)
    grad_conv(
        0,
        count0,
        2 * RW,
        lambda at: pick(mid_xhat, xhat0, at),
        lambda at: pick(mid_rinv, rinv0, at),
        grad0,
    )


def taps1_kernel(flat1, grad1, gk1, x1, pad1):
    for row in range(0, RH, 2):
        x1[row : row + 2] = flat1[row * RW : (row + 2) * RW, :].astype(F32).reshape(2, RW, LANES)
    padded(grad1, pad1, TW)
    gk1[...] = jnp.zeros_like(gk1)

    def kernel1_block(block, _):
        start = block * 8
        grads = [pad1[j, pl.ds(start + PADC, 8), :] for j in range(TH)]
        for d in range(7):
            column = [load_column(x1, r, start + d) for r in range(RH)]
            for a in range(7):
                total = gk1[a * 7 + d]
                for j in range(TH):
                    total = total + grads[j] * column[j + a]
                gk1[a * 7 + d] = total
        return 0

    for block in range(TW // 8):
        kernel1_block(block, 0)


def rest_kernel(
    top_ref,
    dw_ref,
    sums,
    cells,
    flat0,
    grad0,
    carry0,
    gk1,
    small_ref,
    small,
    x0,
    pad0,
    taps0,
    taps0n,
    h0,
    gk0,
    gk0n,
):
    top = top_ref[0] == 1
    north_at = 3 + TH
    levels_count = KERNEL_AT[0] - STEM_AT

    for row in range(0, EH, 4):
        x0[row : row + 4] = flat0[row * EW : (row + 4) * EW, :].astype(F32).reshape(4, EW, LANES)
    padded(grad0, pad0, RW)
    spread_taps(dw_ref, 0, taps0)
    spread_taps(dw_ref, 0, taps0n, top)

    gk0[...] = jnp.zeros_like(gk0)
    gk0n[...] = jnp.zeros_like(gk0n)

    def kernel0_block(block, _):
        start = block * 8
        grads = [pad0[j, pl.ds(start + PADC, 8), :] for j in range(RH)]
        for d in range(7):
            column = [load_column(x0, r, start + 2 + d) for r in range(EH)]
            for a in range(7):
                total = gk0[a * 7 + d]
                for j in range(north_at):
                    total = total + grads[j] * column[j + a]
                gk0[a * 7 + d] = total
                total = gk0n[a * 7 + d]
                for j in range(north_at, RH):
                    total = total + grads[j] * column[j + a]
                gk0n[a * 7 + d] = total
        return 0

    for block in range(RW // 8):
        kernel0_block(block, 0)
    for t in range(49):
        north = jnp.where(top, gk0n[48 - t], gk0n[t])
        small[KERNEL_AT[0] + t : KERNEL_AT[0] + t + 1, :] = jnp.sum(gk0[t] + north, axis=0, keepdims=True)
        small[KERNEL_AT[1] + t : KERNEL_AT[1] + t + 1, :] = jnp.sum(gk1[t], axis=0, keepdims=True)

    def back0_block(block, _):
        start = pl.multiple_of(block * 8, 8)
        for rows in (range(0, 14), range(14, 28)):
            totals = conv_block(
                pad0,
                (taps0, taps0n),
                start,
                rows,
                range(6, 6 + RH),
                lambda o, r, a, d: (1 if r - 6 >= north_at else 0, 48 - (a * 7 + d)),
            )
            for o in rows:
                h0[o, pl.ds(start, 8), :] = totals[o]
        return 0

    lax.fori_loop(0, EW // 8, back0_block, 0)
    for row in range(0, RH, 2):
        h0[row + 3 : row + 5, RING_COL : RING_COL + RW, :] += carry0[
            row * RW : (row + 2) * RW, :
        ].reshape(2, RW, LANES)
    rows = lax.broadcasted_iota(jnp.int32, (LANES, LANES), 0)
    mask = jnp.dot(cells[...], (rows == levels_count).astype(BF), preferred_element_type=F32)
    stem_side = (mask * h0[...].reshape(EH * EW, LANES)).astype(BF)
    stem_grad = contract_rows(cells[...], stem_side)
    small[STEM_AT : KERNEL_AT[0], :] = stem_grad[0:levels_count, :]
    small[GAIN_AT : GAIN_AT + 4, :] = sums[0:4, :]
    small[GAIN_AT + 4 :, :] = jnp.zeros((SMALL - GAIN_AT - 4, LANES), F32)
    small_ref[...] = small[...].astype(BF)


def unpack_kernel(
    order_ref,
    pieces_ref,
    mine_ref,
    other_ref,
    stem_out,
    kernel_out,
    gain_out,
    win_out,
    wout_out,
    scale_out,
    stem_ref,
    kernel_ref,
    gain_ref,
    win_ref,
    wout_ref,
    scale_ref,
    small,
    sent,
):
    count, size = pieces_ref.shape[0], pieces_ref.shape[1]
    stores = [
        pltpu.make_async_copy(source, target, sent.at[index])
        for index, (source, target) in enumerate(
            [(win_ref.at[layer], win_out.at[layer]) for layer in range(2)]
            + [(wout_ref.at[layer], wout_out.at[layer]) for layer in range(2)]
            + [(stem_ref, stem_out), (kernel_ref, kernel_out), (gain_ref, gain_out), (scale_ref, scale_out)]
        )
    ]

    def rows(at, length):
        return [
            pieces_ref[order_ref[index]].astype(F32) if count > 1 else pieces_ref[0, index * 128 : index * 128 + 128].astype(F32)
            for index in range(at // 128, (at + length) // 128)
        ]

    for layer in range(2):
        for part, block in enumerate(rows(WIN_ROW + 512 * layer, 512)):
            win_ref[layer, :, 128 * part : 128 * part + 128] = block
        stores[layer].start()
    for layer in range(2):
        for part, block in enumerate(rows(WOUT_ROW + 512 * layer, 512)):
            wout_ref[layer, 128 * part : 128 * part + 128, :] = block
        stores[2 + layer].start()
    places, size = mine_ref.shape[0], mine_ref.shape[1]
    for index in range(places):
        at = order_ref[count + index]
        small[index * size : (index + 1) * size, :] = mine_ref[at].astype(F32) + other_ref[at].astype(F32)
    for layer in range(2):
        kernel_ref[:, layer, :] = small[KERNEL_AT[layer] : KERNEL_AT[layer] + 49, :]
    stem_ref[...] = small[STEM_AT : STEM_AT + stem_ref.shape[0], :]
    gain_ref[...] = small[GAIN_AT : GAIN_AT + 2, :]
    scale_ref[...] = small[SCALE_AT : SCALE_AT + 2, :]
    for store in stores[4:]:
        store.start()
    for store in stores:
        store.wait()


def permuted(value, pairs):
    return lax.ppermute(value, "gy", pairs)


def crossed(value, bits):
    return permuted(value, [(i, i ^ bits) for i in range(lax.axis_size("gy"))])


def summed_pieces(packed, top, rest):
    size = lax.axis_size("gy")
    if size != 16:
        bulk, small = lax.psum((packed.astype(F32), rest(top).astype(F32)), "gy")
        small = small.astype(BF)[None]
        return bulk.astype(BF)[None], small, jnp.zeros_like(small), jnp.zeros((2,), jnp.int32)
    me = lax.axis_index("gy")
    core, side, deep = me & 1, (me >> 1) & 1, me >> 2

    def halves(value, bit):
        half = value.shape[0] // 2
        low, high = value[:half], value[half:]
        return jnp.where(bit == 0, low, high), jnp.where(bit == 0, high, low)

    keep, send = halves(packed, core)
    came = crossed(send, 1)
    came, top = lax.optimization_barrier((came, top))
    small = rest(top)
    keep, send = halves(keep.astype(F32) + came.astype(F32), side)
    total = keep + crossed(send.astype(BF), 2).astype(F32)
    quarter = total.shape[0] // 4
    part = small.shape[0] // 4

    def shard(step):
        at = deep ^ step
        return jnp.concatenate(
            [
                lax.dynamic_slice_in_dim(total, at * quarter, quarter, 0).astype(BF),
                lax.dynamic_slice_in_dim(small, at * part, part, 0),
            ],
            axis=0,
        )

    arrived = [crossed(shard(step), 4 * step) for step in STEPS]
    bulk = lax.dynamic_slice_in_dim(total, deep * quarter, quarter, 0)
    rest_sum = lax.dynamic_slice_in_dim(small, deep * part, part, 0).astype(F32)
    for other in arrived:
        bulk = bulk + other[:quarter].astype(F32)
        rest_sum = rest_sum + other[quarter:].astype(F32)
    mine = jnp.concatenate([bulk.astype(BF), rest_sum.astype(BF)], axis=0)
    pieces = jnp.stack([mine] + [crossed(mine, 4 * step) for step in STEPS][::-1])
    came = crossed(pieces, 2)
    bulk = jnp.concatenate([pieces[:, :quarter], came[:, :quarter]], axis=0)
    small = (pieces[:, quarter:].astype(F32) + came[:, quarter:].astype(F32)).astype(BF)
    rows = bulk.shape[0] * quarter
    joined = jnp.concatenate([bulk.reshape(rows, LANES), small.reshape(4 * part, LANES)], axis=0)
    came = crossed(joined, 1)
    bulk = jnp.concatenate([bulk, came[:rows].reshape(bulk.shape)], axis=0)
    mixed = ((core << 3) | (side << 2) | deep).astype(jnp.int32)
    order = jnp.arange(20, dtype=jnp.int32) & 15
    order = order ^ jnp.where(jnp.arange(20) < 16, mixed, deep.astype(jnp.int32))
    return bulk, small, came[rows:].reshape(small.shape), order


def shards(levels, ocean, stem, dw_kernel, ln_gain, w_in, w_out, layer_scale, upstream):
    size = lax.axis_size("gy")
    rows = size // TX
    me = lax.axis_index("gy")
    is_top = me // TX == rows - 1
    count = levels.shape[2]
    top = is_top.astype(jnp.int32)[None]
    table = jnp.concatenate([dw_kernel.transpose(1, 0, 2), ln_gain[None], layer_scale[None]])
    tile, to_west, to_east, folded = pl.pallas_call(
        prepare_kernel,
        out_shape=[
            jax.ShapeDtypeStruct((TH, TW, LANES), BF),
            jax.ShapeDtypeStruct((TH + RIM, PADC, LANES), BF),
            jax.ShapeDtypeStruct((TH + RIM, PADC, LANES), BF),
            jax.ShapeDtypeStruct((RIM, TW, LANES), BF),
        ],
        in_specs=vmem(2),
        out_specs=vmem(4),
        scratch_shapes=[pltpu.VMEM((LANES, count), F32)],
        compiler_params=pltpu.CompilerParams(vmem_limit_bytes=4 << 20),
    )(levels[0], ocean.astype(F32))

    def column_pairs(step):
        return [(i, i // TX * TX + (i % TX + step) % TX) for i in range(size)]

    west = permuted(to_east, column_pairs(1))
    east = permuted(to_west, column_pairs(-1))

    lower, upper, folded = pl.pallas_call(
        functools.partial(pack_kernel, stem.shape[0] + 1),
        out_shape=[jax.ShapeDtypeStruct((RIM * TW, LANES), BF)] * 3,
        in_specs=vmem(4),
        out_specs=vmem(3),
        compiler_params=pltpu.CompilerParams(vmem_limit_bytes=4 << 20),
    )(tile, west, east, folded)
    folded = permuted(folded, [(i, i // TX * TX + TX - 1 - i % TX) for i in range(size - TX, size)])
    if rows == 2:
        north = permuted(jnp.where(is_top, lower, upper), [(i, (i + TX) % size) for i in range(size)])
        south = jnp.where(is_top, north, jnp.zeros_like(north))
    else:
        south = permuted(upper, [(i, i + TX) for i in range(size - TX)])
        north = permuted(lower, [(i + TX, i) for i in range(size - TX)])
    north = jnp.where(is_top, folded, north)

    def scratch(*shape, dtype=F32):
        return pltpu.VMEM(shape, dtype)

    count0 = RH * RW
    hidden = w_in.shape[2]
    count_mid = MID_ROWS * RW
    mid_shapes = [
        jax.ShapeDtypeStruct((count_mid, LANES), BF),
        jax.ShapeDtypeStruct((count_mid, LANES), F32),
        jax.ShapeDtypeStruct((count_mid, LANES), F32),
        jax.ShapeDtypeStruct((count_mid, LANES), BF),
        jax.ShapeDtypeStruct((count_mid, hidden), BF),
        jax.ShapeDtypeStruct((count_mid, hidden), F32),
        jax.ShapeDtypeStruct((count_mid, LANES), F32),
    ]
    middle = pl.pallas_call(
        middle_kernel,
        out_shape=mid_shapes,
        in_specs=vmem(7),
        out_specs=vmem(7),
        scratch_shapes=[
            scratch(TH, EW, LANES),
            scratch(TH, EW, LANES),
            scratch(TH, EW, LANES),
            scratch(LANES, 2 * LANES),
            scratch(49, 8, LANES),
            scratch(count_mid, LANES),
            scratch(count_mid, hidden),
        ],
        compiler_params=pltpu.CompilerParams(vmem_limit_bytes=10 << 20),
        cost_estimate=pl.CostEstimate(flops=4_000_000_000, bytes_accessed=3_000_000, transcendentals=0),
    )(tile, west, east, table, stem, w_in, w_out)

    ring_shapes = [
        jax.ShapeDtypeStruct((8, LANES), F32),
        jax.ShapeDtypeStruct((EH * EW, LANES), BF),
        jax.ShapeDtypeStruct((EH * EW, LANES), BF),
        jax.ShapeDtypeStruct((RH * RW, LANES), BF),
        jax.ShapeDtypeStruct((RH * RW, LANES), BF),
        jax.ShapeDtypeStruct((TH * TW, LANES), BF),
        jax.ShapeDtypeStruct((RH * RW, LANES), F32),
    ]
    result, packed, *ring = pl.pallas_call(
        functools.partial(main_kernel, 1.0 / math.sqrt(size * count)),
        out_shape=[
            jax.ShapeDtypeStruct((count, LANES), BF),
            jax.ShapeDtypeStruct((BULK, LANES), BF),
        ]
        + ring_shapes,
        in_specs=[smem()] + vmem(17),
        out_specs=vmem(9),
        scratch_shapes=[
            scratch(EH, EW, LANES),
            scratch(EH, EW, LANES),
            scratch(RH, RW, LANES),
            scratch(49, 8, LANES),
            scratch(49, 8, LANES),
            scratch(TH, EW, LANES),
            scratch(RH, RW, LANES),
            scratch(EH, EW, LANES),
            scratch(LANES, 2 * LANES),
            scratch(49, 8, LANES),
            scratch(count0, LANES),
            scratch(count0, LANES),
            scratch(count0, LANES),
            scratch(count0, LANES),
            scratch(count0, LANES, dtype=BF),
            scratch(count0, hidden, dtype=BF),
            scratch(count0, hidden),
            scratch(count, LANES),
            scratch(count, LANES),
            scratch(count, LANES),
            scratch(count, LANES),
            scratch(count, LANES, dtype=BF),
            scratch(count, hidden, dtype=BF),
            scratch(count, hidden),
            scratch(count0, hidden),
            scratch(count0, LANES, dtype=BF),
            scratch(count0, hidden, dtype=BF),
        ],
        compiler_params=pltpu.CompilerParams(vmem_limit_bytes=20 << 20),
    )(
        top,
        tile,
        west,
        east,
        south,
        north,
        table,
        stem,
        w_in,
        w_out,
        upstream[0],
        *middle,
    )

    sums, cells, flat0, flat1, grad0, grad1, carry0 = ring
    grad_taps1 = pl.pallas_call(
        taps1_kernel,
        out_shape=jax.ShapeDtypeStruct((49, 8, LANES), F32),
        in_specs=vmem(2),
        out_specs=vmem(1)[0],
        scratch_shapes=[scratch(RH, RW, LANES), scratch(TH, EW, LANES)],
        compiler_params=pltpu.CompilerParams(vmem_limit_bytes=6 << 20),
        cost_estimate=pl.CostEstimate(flops=2_000_000_000, bytes_accessed=500_000, transcendentals=0),
    )(flat1, grad1)

    def rest(top):
        return pl.pallas_call(
            rest_kernel,
            out_shape=jax.ShapeDtypeStruct((SMALL, LANES), BF),
            in_specs=[smem()] + vmem(7),
            out_specs=vmem(1)[0],
            scratch_shapes=[
                scratch(SMALL, LANES),
                scratch(EH, EW, LANES),
                scratch(RH, EW + 8, LANES),
                scratch(49, 8, LANES),
                scratch(49, 8, LANES),
                scratch(EH, EW, LANES),
                scratch(49, 8, LANES),
                scratch(49, 8, LANES),
            ],
            compiler_params=pltpu.CompilerParams(vmem_limit_bytes=10 << 20),
            cost_estimate=pl.CostEstimate(flops=10_000_000_000, bytes_accessed=4_000_000, transcendentals=0),
        )(top, table, sums, cells, flat0, grad0, carry0, grad_taps1)

    pieces, mine, other, order = summed_pieces(packed, top, rest)
    shapes = [array.shape for array in (stem, dw_kernel, ln_gain, w_in, w_out, layer_scale)]
    shapes[1] = (shapes[1][1], shapes[1][0], shapes[1][2])
    grads = pl.pallas_call(
        unpack_kernel,
        out_shape=[jax.ShapeDtypeStruct(shape, F32) for shape in shapes],
        in_specs=[smem()] + vmem(3),
        out_specs=[pl.BlockSpec(memory_space=pltpu.HBM)] * 6,
        scratch_shapes=[scratch(*shape) for shape in shapes]
        + [scratch(SMALL, LANES), pltpu.SemaphoreType.DMA((8,))],
        compiler_params=pltpu.CompilerParams(vmem_limit_bytes=8 << 20),
    )(order, pieces, mine, other)
    grads = list(grads)
    grads[1] = grads[1].transpose(1, 0, 2)
    return (result[None], *grads)


def solution(mesh):
    in_specs = (
        P(("groups", "gy"), None, None),
        P(("groups", "gy"), None),
        P(),
        P(),
        P(),
        P(),
        P(),
        P(),
        P(("groups", "gy"), None, None),
    )
    out_specs = (
        P(("groups", "gy"), None, None),
        P("groups", None),
        P("groups", None, None),
        P("groups", None),
        P("groups", None, None),
        P("groups", None, None),
        P("groups", None),
    )
    return jax.shard_map(shards, mesh=mesh, in_specs=in_specs, out_specs=out_specs, check_vma=False)
```
